32 devices in a mesh: seq: 8 (over z, y), head: 4 (over x, core).
Axes of the slice: x: 2, y: 2, z: 4, core: 2. Of those that a mesh axis runs over, the one named last changes fastest.
Arguments:
- block_in: bfloat16 [1, 2048, 1024], P(None, 'seq'), may hold values from -6 to 6
- upstream: bfloat16 [1, 2048, 1024], P(None, 'seq'), may hold values from -6 to 6
- first_gain: float32 [1024], replicated, may hold values from 0.5 to 1.5
- project_in: bfloat16 [1024, 4, 512], P(None, 'head'), may hold values from -0.1875 to 0.1875
- filter_taps: float32 [4, 4, 512], P(None, 'head'), may hold values from -2 to 2
- squeeze: bfloat16 [1024, 16], replicated, may hold values from -0.1875 to 0.1875
- expand: bfloat16 [16, 512], P(None, 'head'), may hold values from -0.75 to 0.75
- decay_bias: float32 [512], P('head'), may hold values from 0 to 16
- gating: bfloat16 [1024, 1024], P(None, 'head'), may hold values from -0.1875 to 0.1875
- head_scale: float32 [256], replicated, may hold values from 0.5 to 1.5
- project_out: bfloat16 [1024, 1024], P('head'), may hold values from -0.375 to 0.375
- second_gain: float32 [1024], replicated, may hold values from 0.5 to 1.5
- hidden_gate: bfloat16 [1024, 2816], P(None, 'head'), may hold values from -0.1875 to 0.1875
- hidden_lift: bfloat16 [1024, 2816], P(None, 'head'), may hold values from -0.1875 to 0.1875
- hidden_drop: bfloat16 [2816, 1024], P('head'), may hold values from -0.15625 to 0.15625
Outputs:
- block_out: bfloat16 [1, 2048, 1024], P(None, 'seq')
- input_grad: float32 [1, 2048, 1024], P(None, 'seq')
- grad_first: float32 [1024], replicated
- grad_project: float32 [1024, 4, 512], P('seq', 'head')
- grad_taps: float32 [4, 4, 512], P(None, 'head')
- grad_squeeze: float32 [1024, 16], replicated
- grad_expand: float32 [16, 512], P(None, 'head')
- grad_bias: float32 [512], P('head')
- grad_gating: float32 [1024, 1024], P('seq', 'head')
- grad_scale: float32 [256], replicated
- grad_output: float32 [1024, 1024], P('head', 'seq')
- grad_second: float32 [1024], replicated
- grad_gate: float32 [1024, 2816], P('seq', 'head')
- grad_lift: float32 [1024, 2816], P('seq', 'head')
- grad_drop: float32 [2816, 1024], P('head', 'seq')
The draws below stay inside these ranges and needn't reach their ends.
All inputs are finite; a program needn't handle non-finite values.
Results may differ from the reference program's by a relative error of at most 0.02.
Values sent between devices are 32-bit elements; how exact they have to be, the bound alone decides.
A program may use at most 128 MiB of HBM per device.

```python
import math
import jax
import jax.numpy as jnp
from jax import lax

D = 1024
H = 4
DK = 128
DV = 256
FF = 2816
RANK = 16
CONV = 4
GROUP = 64
SEQS = 1
QKV = 512
LENGTH = 2048


def draw_decay_bias(key, part):
    first, second, third = jax.random.split(key, 3)
    pick = jax.random.uniform(first, (H * DK,), jnp.float32)
    share = 0.5
    slow = jnp.exp(jax.random.uniform(second, (H * DK,), jnp.float32, math.log(0.2 / LENGTH), math.log(1.2 / LENGTH)))
    quick = jnp.exp(jax.random.uniform(third, (H * DK,), jnp.float32, math.log(1.0 / 200.0), math.log(1.0 / 25.0)))
    rate = jnp.where(pick < share, slow, quick)
    return -jnp.log(jnp.expm1(16.0 * rate))


def block_scale(rng, extent, pieces, smallest, high):
    def one(axis_at, parts):
        heights = jax.random.uniform(jax.random.fold_in(jax.random.fold_in(rng, 6), axis_at), (parts,), jnp.float32, smallest / len(pieces), high / len(pieces))
        return jnp.repeat(jnp.exp(heights), extent[axis_at] // parts).reshape((-1,) + (1,) * (len(extent) - axis_at - 1))

    level = one(*pieces[0])
    for cut in pieces[1:]:
        level = level * one(*cut)
    return level


def normal_values(rng, dims, width, reach, shards=(), held_as=jnp.bfloat16):
    result = width * jax.random.normal(rng, dims, jnp.float32)
    if shards:
        result = result * block_scale(rng, dims, shards, -0.22, 0.18)
    return jnp.clip(result, -reach, reach).astype(held_as)


def setup_inputs(seed: int = 0) -> dict:
    splits = jax.random.split(jax.random.key(seed), 16)
    return {
        "block_in": normal_values(splits[0], (SEQS, LENGTH, D), 1.0, 6.0, ((1, 8),)),
        "upstream": normal_values(splits[1], (SEQS, LENGTH, D), 1.0, 6.0, ((1, 8),)),
        "first_gain": jnp.clip(1.0 + 0.1 * jax.random.normal(splits[2], (D,), jnp.float32), 0.5, 1.5),
        "project_in": normal_values(splits[3], (D, H, QKV), D ** -0.5, 0.1875, ((1, 4),)),
        "filter_taps": normal_values(splits[4], (CONV, H, QKV), 0.5, 2.0, ((1, 4),), jnp.float32),
        "squeeze": normal_values(splits[5], (D, RANK), D ** -0.5, 0.1875),
        "expand": normal_values(splits[6], (RANK, H * DK), (4 * RANK) ** -0.5, 0.75, ((1, 4),)),
        "decay_bias": draw_decay_bias(jax.random.fold_in(splits[15], 71), 0),
        "gating": normal_values(splits[8], (D, H * DV), D ** -0.5, 0.1875, ((1, 4),)),
        "head_scale": jnp.clip(1.0 + 0.1 * jax.random.normal(splits[9], (DV,), jnp.float32), 0.5, 1.5),
        "project_out": normal_values(splits[10], (H * DV, D), DV ** -0.5, 0.375, ((0, 4),)),
        "second_gain": jnp.clip(1.0 + 0.1 * jax.random.normal(splits[11], (D,), jnp.float32), 0.5, 1.5),
        "hidden_gate": normal_values(splits[12], (D, FF), D ** -0.5, 0.1875, ((1, 4),)),
        "hidden_lift": normal_values(splits[13], (D, FF), D ** -0.5, 0.1875, ((1, 4),)),
        "hidden_drop": normal_values(splits[14], (FF, D), (FF // 2) ** -0.5, 0.15625, ((0, 4),)),
    }


EPS = 1e-05
NORMALIZER = 16.0
HIGH = lax.Precision.HIGHEST

def product(left, right):
    return jnp.dot(left, right, preferred_element_type=jnp.float32)

def rms_scale(values):
    return lax.rsqrt(lax.optimization_barrier(jnp.mean(values * values, axis=-1, keepdims=True)) + EPS)

def rms_back(values, scale, gain, incoming):
    weighted = gain * incoming
    cube = scale * scale * scale
    return scale * weighted - values * cube * lax.optimization_barrier(jnp.mean(values * weighted, axis=-1, keepdims=True))

def silu_grad(values):
    logistic = jax.nn.sigmoid(values)
    return logistic * (1.0 + values * (1.0 - logistic))

def causal_mask():
    rows = lax.broadcasted_iota(jnp.int32, (GROUP, GROUP), 0)
    columns = lax.broadcasted_iota(jnp.int32, (GROUP, GROUP), 1)
    return (columns <= rows).astype(jnp.float32)

def group_view(array):
    return array.reshape((array.shape[0] // GROUP, GROUP) + array.shape[1:])

def run_states(decays, updates, backward):

    def step(carry, item):
        decay, update = item
        return (jnp.exp(decay)[..., None] * carry + update, carry)
    init = jnp.zeros(updates.shape[1:], jnp.float32)
    _, states = lax.scan(step, init, (decays, updates), reverse=backward)
    return states

def attention_parts(query, keys, log_decay):
    running = jnp.cumsum(group_view(log_decay), axis=1)
    last = running[:, -1]
    query_in = group_view(query) * jnp.exp(running)
    key_in = group_view(keys) * jnp.exp(-running)
    key_end = group_view(keys) * jnp.exp(last[:, None] - running)
    return (running, last, query_in, key_in, key_end)

def linear_attention(query, keys, values, log_decay):
    running, last, query_in, key_in, key_end = attention_parts(query, keys, log_decay)
    group_values = group_view(values)
    scores = jnp.einsum('nihc,njhc->nhij', query_in, key_in, precision=HIGH) * causal_mask()
    updates = jnp.einsum('njhc,njhd->nhcd', key_end, group_values, precision=HIGH)
    starts = run_states(last, updates, False)
    mixed = jnp.einsum('nhij,njhd->nihd', scores, group_values, precision=HIGH)
    mixed = mixed + jnp.einsum('nihc,nhcd->nihd', query_in, starts, precision=HIGH)
    return (mixed.reshape(values.shape), starts)

def attention_back(query, keys, values, log_decay, starts, grad_mixed):
    running, last, query_in, key_in, key_end = attention_parts(query, keys, log_decay)
    group_values = group_view(values)
    outgrad = group_view(grad_mixed)
    mask = causal_mask()
    scores = jnp.einsum('nihc,njhc->nhij', query_in, key_in, precision=HIGH) * mask
    query_end = jnp.einsum('nihc,nihd->nhcd', query_in, outgrad, precision=HIGH)
    following = run_states(last, query_end, True)
    inner_group = jnp.einsum('nihd,njhd->nhij', outgrad, group_values, precision=HIGH) * mask
    grad_query = jnp.exp(running) * (jnp.einsum('nhij,njhc->nihc', inner_group, key_in, precision=HIGH) + jnp.einsum('nihd,nhcd->nihc', outgrad, starts, precision=HIGH))
    grad_keys = jnp.exp(-running) * jnp.einsum('nhij,nihc->njhc', inner_group, query_in, precision=HIGH)
    grad_keys = grad_keys + jnp.exp(last[:, None] - running) * jnp.einsum('njhd,nhcd->njhc', group_values, following, precision=HIGH)
    grad_values = jnp.einsum('nhij,nihd->njhd', scores, outgrad, precision=HIGH)
    grad_values = grad_values + jnp.einsum('njhc,nhcd->njhd', key_end, following, precision=HIGH)
    grad_running = group_view(query) * grad_query - group_view(keys) * grad_keys
    flat = grad_running.reshape(log_decay.shape)
    grad_log = jnp.flip(jnp.cumsum(jnp.flip(flat, 0), axis=0), 0)
    return (grad_query.reshape(query.shape), grad_keys.reshape(keys.shape), grad_values.reshape(values.shape), grad_log)

def causal_conv(projected, taps):
    length = projected.shape[0]
    lags = taps.shape[0] - 1
    padded = jnp.concatenate([jnp.zeros((lags,) + projected.shape[1:], jnp.float32), projected], axis=0)
    total = jnp.zeros_like(projected)
    for lag in range(lags + 1):
        total = total + taps[lag] * padded[lags - lag:lags - lag + length]
    return (total, padded)

def conv_back(padded, taps, grad_filtered):
    length = grad_filtered.shape[0]
    lags = taps.shape[0] - 1
    padded_back = jnp.concatenate([grad_filtered, jnp.zeros((lags,) + grad_filtered.shape[1:], jnp.float32)], axis=0)
    grad_projected = jnp.zeros_like(grad_filtered)
    tap_rows = []
    for lag in range(lags + 1):
        grad_projected = grad_projected + taps[lag] * padded_back[lag:lag + length]
        tap_rows.append(lax.optimization_barrier(jnp.sum(grad_filtered * padded[lags - lag:lags - lag + length], axis=0)))
    return (grad_projected, jnp.stack(tap_rows))

def one_sequence(block_in, upstream, first_gain, project_in, filter_taps, squeeze, expand, decay_bias, gating, head_scale, project_out, second_gain, hidden_gate, hidden_lift, hidden_drop):
    length = block_in.shape[0]
    residual_in = block_in.astype(jnp.float32)
    scale_one = rms_scale(residual_in)
    normed_one = (residual_in * scale_one * first_gain).astype(jnp.bfloat16)
    weight_in = project_in.reshape(D, H * QKV)
    projected = product(normed_one, weight_in).reshape(length, H, QKV)
    filtered, padded = causal_conv(projected, filter_taps)
    activated_low = jax.nn.silu(filtered).astype(jnp.bfloat16)
    activated = lax.optimization_barrier(activated_low).astype(jnp.float32)
    root = DK ** (-0.5)
    query = activated[..., :DK] * root
    keys = activated[..., DK:2 * DK]
    values = activated[..., 2 * DK:]
    squeezed = product(normed_one, squeeze).astype(jnp.bfloat16)
    logits = product(squeezed, expand) + decay_bias
    log_decay = (jax.nn.log_sigmoid(logits) / NORMALIZER).reshape(length, H, DK)
    gate_in = product(normed_one, gating).reshape(length, H, DV)
    mixed, starts = linear_attention(query, keys, values, log_decay)
    scale_head = rms_scale(mixed)
    normed_head = mixed * scale_head * head_scale
    gated = (normed_head * jax.nn.silu(gate_in)).astype(jnp.bfloat16).reshape(length, H * DV)
    residual = residual_in + product(gated, project_out)
    scale_two = rms_scale(residual)
    normed_two = (residual * scale_two * second_gain).astype(jnp.bfloat16)
    gate_value = product(normed_two, hidden_gate)
    lift_value = product(normed_two, hidden_lift)
    inner = (jax.nn.silu(gate_value) * lift_value).astype(jnp.bfloat16)
    block_out = (residual + product(inner, hidden_drop)).astype(jnp.bfloat16)
    grad_drop = product(inner.T, upstream)
    grad_inner = product(upstream, hidden_drop.T)
    grad_gv = (grad_inner * lift_value * silu_grad(gate_value)).astype(jnp.bfloat16)
    grad_lv = (grad_inner * jax.nn.silu(gate_value)).astype(jnp.bfloat16)
    grad_gate = product(normed_two.T, grad_gv)
    grad_lift = product(normed_two.T, grad_lv)
    grad_two = product(grad_gv, hidden_gate.T) + product(grad_lv, hidden_lift.T)
    grad_second = lax.optimization_barrier(jnp.sum(grad_two * residual * scale_two, axis=0))
    grad_resid = upstream.astype(jnp.float32) + rms_back(residual, scale_two, second_gain, grad_two)
    resid_low = grad_resid.astype(jnp.bfloat16)
    grad_output = product(gated.T, resid_low)
    grad_gated = product(resid_low, project_out.T).reshape(length, H, DV)
    grad_gatein = (grad_gated * normed_head * silu_grad(gate_in)).astype(jnp.bfloat16)
    grad_normhead = grad_gated * jax.nn.silu(gate_in)
    grad_scale = lax.optimization_barrier(jnp.sum(grad_normhead * mixed * scale_head, axis=(0, 1)))
    grad_mixed_low = rms_back(mixed, scale_head, head_scale, grad_normhead).astype(jnp.bfloat16)
    grad_mixed = lax.optimization_barrier(grad_mixed_low).astype(jnp.float32)
    grad_query, grad_keys, grad_values, grad_log = attention_back(query, keys, values, log_decay, starts, grad_mixed)
    grad_act = jnp.concatenate([grad_query * root, grad_keys, grad_values], axis=-1)
    grad_filtered = grad_act * silu_grad(filtered)
    grad_projected, grad_taps = conv_back(padded, filter_taps, grad_filtered)
    grad_projected = grad_projected.astype(jnp.bfloat16).reshape(length, H * QKV)
    grad_logits = grad_log.reshape(length, H * DK) * jax.nn.sigmoid(-logits) / NORMALIZER
    grad_bias = lax.optimization_barrier(jnp.sum(grad_logits, axis=0))
    logits_low = grad_logits.astype(jnp.bfloat16)
    grad_expand = product(squeezed.T, logits_low)
    squeeze_low = jnp.einsum('lhc,rhc->hlr', logits_low.reshape(length, H, DK).astype(jnp.float32), expand.reshape(RANK, H, DK).astype(jnp.float32), precision=HIGH).astype(jnp.bfloat16)
    squeeze_wide = squeeze_low.astype(jnp.float32)
    grad_squeeze = jnp.einsum('ld,hlr->dr', normed_one.astype(jnp.float32), squeeze_wide, precision=HIGH)
    grad_project = product(normed_one.T, grad_projected).reshape(D, H, QKV)
    gatein_flat = grad_gatein.reshape(length, H * DV)
    grad_gating = product(normed_one.T, gatein_flat)
    grad_one = product(grad_projected, weight_in.T) + product(gatein_flat, gating.T)
    grad_one = grad_one + jnp.einsum('hlr,dr->ld', squeeze_wide, squeeze.astype(jnp.float32), precision=HIGH)
    grad_first = lax.optimization_barrier(jnp.sum(grad_one * residual_in * scale_one, axis=0))
    input_grad = grad_resid + rms_back(residual_in, scale_one, first_gain, grad_one)
    grads = (grad_first, grad_project, grad_taps, grad_squeeze, grad_expand, grad_bias, grad_gating, grad_scale, grad_output, grad_second, grad_gate, grad_lift, grad_drop)
    return (block_out, input_grad, grads)

def reference(block_in, upstream, first_gain, project_in, filter_taps, squeeze, expand, decay_bias, gating, head_scale, project_out, second_gain, hidden_gate, hidden_lift, hidden_drop):
    outputs = []
    in_grads = []
    totals = None
    for index in range(SEQS):
        block_out, input_grad, grads = one_sequence(block_in[index], upstream[index], first_gain, project_in, filter_taps, squeeze, expand, decay_bias, gating, head_scale, project_out, second_gain, hidden_gate, hidden_lift, hidden_drop)
        outputs.append(block_out)
        in_grads.append(input_grad)
        if totals is None:
            totals = grads
        else:
            totals = tuple((left + right for left, right in zip(totals, grads)))
    return (jnp.stack(outputs), jnp.stack(in_grads), totals[0], totals[1], totals[2], totals[3], totals[4], totals[5], totals[6], totals[7], totals[8], totals[9], totals[10], totals[11], totals[12])
```

```python
import functools

import jax
import jax.numpy as jnp
from jax import lax
from jax.experimental import pallas as pl
from jax.experimental.pallas import tpu as pltpu
from jax.sharding import PartitionSpec as P

GROUP = 64


EPS = 1e-05
NORMALIZER = 16.0
HIGH = lax.Precision.HIGHEST


MESH = pl.DeviceIdType.MESH
PIECES = 4


def greet(devices):
    barrier = pltpu.get_barrier_semaphore()
    for device in devices:
        pl.semaphore_signal(barrier, inc=1, device_id=device, device_id_type=MESH)
    pl.semaphore_wait(barrier, len(devices))


def ring_kernel(size, arrays, *refs):
    ins, outs = refs[:arrays], refs[arrays : 2 * arrays]
    slots = refs[2 * arrays : 3 * arrays]
    send_sem, recv_sem = refs[3 * arrays :]
    half = size // 2
    me = lax.axis_index("seq")
    mine_head = lax.axis_index("head")
    low, high = me % 2, me // 2
    place = high + low * (2 * half - 1 - 2 * high)

    def member(position):
        position = (position + 2 * size) % size
        side = position // half
        return 2 * (position + side * (2 * half - 1 - 2 * position)) + side

    partners = (
        (member(place + 1), mine_head),
        (member(place - 1), mine_head),
    )
    greet(partners)
    rows = ins[0].shape[0] // size
    part = rows // 2

    def block(array, direction, position):
        start = pl.multiple_of(member(position) * rows + direction * part, part)
        return ins[array].at[pl.ds(start, part)]

    def copy(array, direction, step, source):
        return pltpu.make_async_remote_copy(
            src_ref=source,
            dst_ref=slots[array].at[direction, step],
            send_sem=send_sem.at[array, direction, step],
            recv_sem=recv_sem.at[array, direction, step],
            device_id=partners[direction],
            device_id_type=MESH,
        )

    for array in range(arrays):
        for direction, sign in ((0, 1), (1, -1)):
            copy(array, direction, 0, block(array, direction, place - sign)).start()

    def lap(step, carry):
        for array in range(arrays):
            for direction, sign in ((0, 1), (1, -1)):
                slot = slots[array].at[direction, step - 1]
                copy(array, direction, step - 1, slot).wait_recv()
                local = block(array, direction, place - sign * (step + 1))
                slot[...] = slot[...] + local[...]
                copy(array, direction, step, slot).start()
        return carry

    lax.fori_loop(1, size - 1, lap, 0)
    for array in range(arrays):
        for direction in range(2):
            slot = slots[array].at[direction, size - 2]
            copy(array, direction, size - 2, slot).wait_recv()
            local = block(array, direction, place)
            outs[array][pl.ds(direction * part, part)] = slot[...] + local[...]

    def finish(step, carry):
        for array in range(arrays):
            for direction in range(2):
                copy(array, direction, step, slots[array].at[direction, step]).wait_send()
        return carry

    lax.fori_loop(0, size - 1, finish, 0)


def ring_scatter(*partials):
    size = lax.axis_size("seq")
    arrays = len(partials)
    rows = partials[0].shape[0] // size
    return pl.pallas_call(
        functools.partial(ring_kernel, size, arrays),
        out_shape=[jax.ShapeDtypeStruct((rows, x.shape[1]), jnp.float32) for x in partials],
        in_specs=[pl.BlockSpec(memory_space=pltpu.VMEM)] * arrays,
        out_specs=[pl.BlockSpec(memory_space=pltpu.VMEM)] * arrays,
        scratch_shapes=[
            pltpu.VMEM((2, size - 1, rows // 2, x.shape[1]), jnp.float32) for x in partials
        ]
        + [pltpu.SemaphoreType.DMA((arrays, 2, size - 1))] * 2,
        compiler_params=pltpu.CompilerParams(
            collective_id=0, has_side_effects=True, vmem_limit_bytes=56 * 1024 * 1024
        ),
    )(*partials)


def head_kernel(in_ref, out_ref, pair, summed, other, back, send_sem, recv_sem):
    me = lax.axis_index("head")
    mine_seq = lax.axis_index("seq")
    core, chip = me % 2, me // 2
    near = (mine_seq, chip * 2 + 1 - core)
    far = (mine_seq, (1 - chip) * 2 + core)
    greet((near, far))
    half = in_ref.shape[0] // 2
    piece = half // PIECES
    mine = pl.multiple_of(core * half, half)
    theirs = pl.multiple_of((1 - core) * half, half)

    def copy(stage, index, source, target, device):
        return pltpu.make_async_remote_copy(
            src_ref=source,
            dst_ref=target.at[pl.ds(index * piece, piece)],
            send_sem=send_sem.at[stage, index],
            recv_sem=recv_sem.at[stage, index],
            device_id=device,
            device_id_type=MESH,
        )

    first, second, third = [], [], []
    for index in range(PIECES):
        source = in_ref.at[pl.ds(theirs + index * piece, piece)]
        first.append(copy(0, index, source, pair, near))
        first[-1].start()
    for index in range(PIECES):
        rows = pl.ds(index * piece, piece)
        first[index].wait_recv()
        summed[rows] = in_ref[pl.ds(mine + index * piece, piece)] + pair[rows]
        second.append(copy(1, index, summed.at[rows], other, far))
        second[-1].start()
    for index in range(PIECES):
        rows = pl.ds(index * piece, piece)
        second[index].wait_recv()
        total = pl.ds(mine + index * piece, piece)
        out_ref[total] = summed[rows] + other[rows]
        third.append(copy(2, index, out_ref.at[total], back, near))
        third[-1].start()
    for index in range(PIECES):
        third[index].wait_recv()
        out_ref[pl.ds(theirs + index * piece, piece)] = back[pl.ds(index * piece, piece)]
    for item in first + second + third:
        item.wait_send()


def head_sum(value):
    rows, columns = value.shape
    landing = pltpu.VMEM((rows // 2, columns), jnp.float32)
    return pl.pallas_call(
        head_kernel,
        out_shape=jax.ShapeDtypeStruct(value.shape, jnp.float32),
        in_specs=[pl.BlockSpec(memory_space=pltpu.VMEM)],
        out_specs=pl.BlockSpec(memory_space=pltpu.VMEM),
        scratch_shapes=[landing] * 4 + [pltpu.SemaphoreType.DMA((3, PIECES))] * 2,
        compiler_params=pltpu.CompilerParams(
            collective_id=1, has_side_effects=True, vmem_limit_bytes=16 * 1024 * 1024
        ),
    )(value)


def shifted(x, axis, by):
    size = lax.axis_size(axis)
    pairs = [(i, i + by) for i in range(size) if 0 <= i + by < size]
    return lax.ppermute(x, axis, pairs)


def entering(value, axis, join, neutral, backward):
    count, mine = (lax.axis_size(axis), lax.axis_index(axis))
    pieces = jax.tree.map(lambda part: lax.all_gather(part, axis), value)
    if backward:
        pieces = jax.tree.map(lambda part: part[::-1], pieces)
        mine = count - 1 - mine
    total = jax.tree.map(
        lambda part, zero: jnp.full_like(part, 0) + jnp.asarray(zero, part.dtype), value, neutral
    )

    def lap(position, total):
        longer = join(total, jax.tree.map(lambda part: part[position], pieces))
        return jax.tree.map(lambda new, old: jnp.where(position < mine, new, old), longer, total)

    return lax.fori_loop(0, count - 1, lap, total)


def product(left, right):
    return jnp.dot(left, right, preferred_element_type=jnp.float32)


def against(left, right):
    return lax.dot_general(
        left, right, (((1,), (1,)), ((), ())), preferred_element_type=jnp.float32
    )


def across(left, right):
    return lax.dot_general(
        left, right, (((0,), (0,)), ((), ())), preferred_element_type=jnp.float32
    )


def rms_scale(values):
    return lax.rsqrt(jnp.mean(values * values, axis=-1, keepdims=True) + EPS)


def rms_back(values, scale, gain, incoming):
    weighted = gain * incoming
    cube = scale * scale * scale
    return scale * weighted - values * cube * jnp.mean(values * weighted, axis=-1, keepdims=True)


def silu_grad(values):
    logistic = jax.nn.sigmoid(values)
    return logistic * (1.0 + values * (1.0 - logistic))


def causal_mask(size):
    rows = lax.broadcasted_iota(jnp.int32, (size, size), 0)
    columns = lax.broadcasted_iota(jnp.int32, (size, size), 1)
    return (columns <= rows).astype(jnp.float32)


def chain(earlier, later):
    return (earlier[0] * later[0], later[0][..., None] * earlier[1] + later[1])


def grouped(array, seqs, count):
    return array.reshape((seqs, count, GROUP) + array.shape[2:])


def running_sums(array):
    rows = [array[:, 0]]
    for index in range(1, array.shape[1]):
        rows.append(rows[-1] + array[:, index])
    return jnp.stack(rows, axis=1)


def local_states(decays, updates, backward):

    def step(carry, item):
        decay, update = item
        return (jnp.exp(decay)[..., None] * carry + update, carry)

    init = jnp.zeros_like(updates[:, 0])
    total, states = lax.scan(
        step, init, (jnp.moveaxis(decays, 1, 0), jnp.moveaxis(updates, 1, 0)), reverse=backward
    )
    return (jnp.moveaxis(states, 0, 1), total)


def body(
    block_in,
    upstream,
    first_gain,
    project_in,
    filter_taps,
    squeeze,
    expand,
    decay_bias,
    gating,
    head_scale,
    project_out,
    second_gain,
    hidden_gate,
    hidden_lift,
    hidden_drop,
):
    seqs, tokens, width = block_in.shape
    total_rows = seqs * tokens
    key_dim = expand.shape[1]
    value_dim = gating.shape[1]
    mixed_dim = project_in.shape[2]
    lags = filter_taps.shape[0] - 1
    count = tokens // GROUP
    taps = filter_taps.reshape(lags + 1, mixed_dim)
    weight_in = project_in.reshape(width, mixed_dim)
    residual_in = block_in.reshape(total_rows, width).astype(jnp.float32)
    scale_one = rms_scale(residual_in)
    normed_one = (residual_in * scale_one * first_gain).astype(jnp.bfloat16)
    projected = product(normed_one, weight_in).reshape(seqs, tokens, mixed_dim)
    before = shifted(projected[:, tokens - lags :], "seq", 1)
    padded = jnp.concatenate([before, projected], axis=1)
    filtered = taps[0] * projected
    for lag in range(1, lags + 1):
        filtered = filtered + taps[lag] * padded[:, lags - lag : lags - lag + tokens]
    activated_low = jax.nn.silu(filtered).astype(jnp.bfloat16)
    activated = lax.optimization_barrier(activated_low).astype(jnp.float32)
    root = key_dim ** (-0.5)
    query = grouped(activated[..., :key_dim] * root, seqs, count)
    keys = grouped(activated[..., key_dim : 2 * key_dim], seqs, count)
    values = grouped(activated[..., 2 * key_dim :], seqs, count)
    squeezed = product(normed_one, squeeze).astype(jnp.bfloat16)
    logits = product(squeezed, expand) + decay_bias
    log_decay = grouped(
        (jax.nn.log_sigmoid(logits) / NORMALIZER).reshape(seqs, tokens, key_dim), seqs, count
    )
    gate_in = product(normed_one, gating)
    mask = causal_mask(GROUP)
    running = jnp.einsum("ij,snjc->snic", mask, log_decay, precision=HIGH)
    last = running[:, :, -1]
    query_in = query * jnp.exp(running)
    key_in = keys * jnp.exp(-running)
    key_end = keys * jnp.exp(last[:, :, None] - running)
    scores = jnp.einsum("snic,snjc->snij", query_in, key_in, precision=HIGH) * mask
    updates = jnp.einsum("snjc,snjd->sncd", key_end, values, precision=HIGH)
    starts_zero, state_total = local_states(last, updates, False)
    decay_sum = jnp.sum(last, axis=1)
    decay_total = jnp.exp(decay_sum)
    identity = (jnp.ones_like(decay_total), jnp.zeros_like(state_total))
    incoming = entering((decay_total, state_total), "seq", chain, identity, False)[1]
    before_group = running_sums(last) - last
    starts = starts_zero + jnp.exp(before_group)[..., None] * incoming[:, None]
    mixed = jnp.einsum("snij,snjd->snid", scores, values, precision=HIGH)
    mixed = mixed + jnp.einsum("snic,sncd->snid", query_in, starts, precision=HIGH)
    mixed = mixed.reshape(total_rows, value_dim)
    scale_head = rms_scale(mixed)
    normed_head = mixed * scale_head * head_scale
    gated = (normed_head * jax.nn.silu(gate_in)).astype(jnp.bfloat16)
    branch = head_sum(product(gated, project_out))
    residual = residual_in + branch
    scale_two = rms_scale(residual)
    normed_two = (residual * scale_two * second_gain).astype(jnp.bfloat16)
    gate_value = product(normed_two, hidden_gate)
    lift_value = product(normed_two, hidden_lift)
    inner = (jax.nn.silu(gate_value) * lift_value).astype(jnp.bfloat16)
    feed = head_sum(product(inner, hidden_drop))
    block_out = (residual + feed).astype(jnp.bfloat16).reshape(seqs, tokens, width)
    seed = upstream.reshape(total_rows, width)
    grad_drop = across(seed, inner)
    grad_inner = against(seed, hidden_drop)
    grad_gv = (grad_inner * lift_value * silu_grad(gate_value)).astype(jnp.bfloat16)
    grad_lv = (grad_inner * jax.nn.silu(gate_value)).astype(jnp.bfloat16)
    feed_both = across(normed_two, jnp.concatenate([grad_gv, grad_lv], axis=1))
    grad_two = head_sum(against(grad_gv, hidden_gate) + against(grad_lv, hidden_lift))
    grad_second = jnp.sum(grad_two * residual * scale_two, axis=0)
    grad_resid = seed.astype(jnp.float32) + rms_back(residual, scale_two, second_gain, grad_two)
    resid_low = grad_resid.astype(jnp.bfloat16)
    grad_output = across(resid_low, gated)
    grad_gated = against(resid_low, project_out)
    grad_gatein = (grad_gated * normed_head * silu_grad(gate_in)).astype(jnp.bfloat16)
    grad_normhead = grad_gated * jax.nn.silu(gate_in)
    grad_scale = jnp.sum(grad_normhead * mixed * scale_head, axis=0)
    grad_mixed_low = rms_back(mixed, scale_head, head_scale, grad_normhead).astype(jnp.bfloat16)
    grad_mixed = lax.optimization_barrier(grad_mixed_low).astype(jnp.float32)
    outgrad = grouped(grad_mixed.reshape(seqs, tokens, value_dim), seqs, count)
    query_end = jnp.einsum("snic,snid->sncd", query_in, outgrad, precision=HIGH)
    following_zero, back_total = local_states(last, query_end, True)
    after = entering((decay_total, back_total), "seq", chain, identity, True)[1]
    after_group = decay_sum[:, None] - running_sums(last)
    following = following_zero + jnp.exp(after_group)[..., None] * after[:, None]
    inner_group = jnp.einsum("snid,snjd->snij", outgrad, values, precision=HIGH) * mask
    grad_query = jnp.exp(running) * (
        jnp.einsum("snij,snjc->snic", inner_group, key_in, precision=HIGH)
        + jnp.einsum("snid,sncd->snic", outgrad, starts, precision=HIGH)
    )
    grad_keys = jnp.exp(-running) * jnp.einsum(
        "snij,snic->snjc", inner_group, query_in, precision=HIGH
    )
    grad_keys = grad_keys + jnp.exp(last[:, :, None] - running) * jnp.einsum(
        "snjd,sncd->snjc", values, following, precision=HIGH
    )
    grad_values = jnp.einsum("snij,snid->snjd", scores, outgrad, precision=HIGH)
    grad_values = grad_values + jnp.einsum("snjc,sncd->snjd", key_end, following, precision=HIGH)
    grad_running = (query * grad_query - keys * grad_keys).reshape(seqs, tokens, key_dim)
    state_end = decay_total[..., None] * incoming + state_total
    beyond = jnp.sum(state_end * after, axis=-1)
    upper = jnp.transpose(causal_mask(tokens))
    suffix = jnp.einsum("ij,sjc->sic", upper, grad_running, precision=HIGH)
    grad_log = suffix + beyond[:, None]
    grad_act = jnp.concatenate(
        [
            grad_query.reshape(seqs, tokens, key_dim) * root,
            grad_keys.reshape(seqs, tokens, key_dim),
            grad_values.reshape(seqs, tokens, value_dim),
        ],
        axis=-1,
    )
    grad_filtered = grad_act * silu_grad(filtered)
    later = shifted(grad_filtered[:, :lags], "seq", -1)
    padded_back = jnp.concatenate([grad_filtered, later], axis=1)
    grad_projected = taps[0] * grad_filtered
    tap_rows = [jnp.sum(grad_filtered * projected, axis=(0, 1))]
    for lag in range(1, lags + 1):
        grad_projected = grad_projected + taps[lag] * padded_back[:, lag : lag + tokens]
        tap_rows.append(
            jnp.sum(grad_filtered * padded[:, lags - lag : lags - lag + tokens], axis=(0, 1))
        )
    grad_taps = jnp.stack(tap_rows).reshape(lags + 1, 1, mixed_dim)
    grad_projected = grad_projected.reshape(total_rows, mixed_dim).astype(jnp.bfloat16)
    grad_logits = grad_log.reshape(total_rows, key_dim) * jax.nn.sigmoid(-logits) / NORMALIZER
    grad_bias = jnp.sum(grad_logits, axis=0)
    logits_low = grad_logits.astype(jnp.bfloat16)
    grad_expand = across(squeezed, logits_low)
    squeeze_low = against(logits_low, expand).astype(jnp.bfloat16)
    grad_squeeze = across(normed_one, squeeze_low)
    mixer_both = across(normed_one, jnp.concatenate([grad_projected, grad_gatein], axis=1))
    partial_value = (
        against(grad_projected, weight_in)
        + against(grad_gatein, gating)
        + against(squeeze_low, squeeze)
    )
    grad_one = head_sum(partial_value)
    grad_first = jnp.sum(grad_one * residual_in * scale_one, axis=0)
    input_grad = (grad_resid + rms_back(residual_in, scale_one, first_gain, grad_one)).reshape(
        seqs, tokens, width
    )
    feed_own, mixer_own, drop_own, output_own = ring_scatter(
        feed_both, mixer_both, grad_drop, grad_output
    )
    hidden = grad_gv.shape[1]
    summed = (
        mixer_own[:, None, :mixed_dim],
        mixer_own[:, mixed_dim:],
        jnp.transpose(output_own),
        feed_own[:, :hidden],
        feed_own[:, hidden:],
        jnp.transpose(drop_own),
    )
    small_head = lax.psum((grad_taps, grad_expand, grad_bias, grad_first, grad_second), "seq")
    shared = lax.psum((grad_scale, grad_squeeze), ("seq", "head"))
    return (
        block_out,
        input_grad,
        small_head[3],
        summed[0],
        small_head[0],
        shared[1],
        small_head[1],
        small_head[2],
        summed[1],
        shared[0],
        summed[2],
        small_head[4],
        summed[3],
        summed[4],
        summed[5],
    )


def solution(mesh):
    in_specs = (
        P(None, "seq", None),
        P(None, "seq", None),
        P(),
        P(None, "head", None),
        P(None, "head", None),
        P(),
        P(None, "head"),
        P("head"),
        P(None, "head"),
        P(),
        P("head", None),
        P(),
        P(None, "head"),
        P(None, "head"),
        P("head", None),
    )
    out_specs = (
        P(None, "seq", None),
        P(None, "seq", None),
        P(),
        P("seq", "head", None),
        P(None, "head", None),
        P(),
        P(None, "head"),
        P("head"),
        P("seq", "head"),
        P(),
        P("head", "seq"),
        P(),
        P("seq", "head"),
        P("seq", "head"),
        P("head", "seq"),
    )
    return jax.shard_map(body, mesh=mesh, in_specs=in_specs, out_specs=out_specs, check_vma=False)
```

```python
import functools

import jax
import jax.numpy as jnp
from jax import lax
from jax.experimental import pallas as pl
from jax.experimental.pallas import tpu as pltpu
from jax.sharding import PartitionSpec as P

GROUP = 64


EPS = 1e-05
NORMALIZER = 16.0
HIGH = lax.Precision.HIGHEST


MESH = pl.DeviceIdType.MESH
PIECES = 4
SHARES = 3


def greet(devices):
    barrier = pltpu.get_barrier_semaphore()
    for device in devices:
        pl.semaphore_signal(barrier, inc=1, device_id=device, device_id_type=MESH)
    pl.semaphore_wait(barrier, len(devices))


def place_of():
    s, h = lax.axis_index("seq"), lax.axis_index("head")
    return s, h, s // 2, s % 2


def head_partners():
    s, h = lax.axis_index("seq"), lax.axis_index("head")
    core, chip = h % 2, h // 2
    return (s, chip * 2 + 1 - core), (s, (1 - chip) * 2 + core)


class HeadSum:
    def __init__(self, value, out, pair, summed, other, back, send_sem, recv_sem):
        self.value, self.out = value, out
        self.pair, self.summed, self.other, self.back = pair, summed, other, back
        self.send_sem, self.recv_sem = send_sem, recv_sem
        self.near, self.far = head_partners()
        core = lax.axis_index("head") % 2
        half = value.shape[0] // 2
        self.piece = half // PIECES
        self.mine = pl.multiple_of(core * half, half)
        self.theirs = pl.multiple_of((1 - core) * half, half)
        self.first, self.second, self.third = [], [], []

    def copy(self, stage, index, source, target, device):
        item = pltpu.make_async_remote_copy(
            src_ref=source,
            dst_ref=target.at[pl.ds(index * self.piece, self.piece)],
            send_sem=self.send_sem.at[stage, index],
            recv_sem=self.recv_sem.at[stage, index],
            device_id=device,
            device_id_type=MESH,
        )
        item.start()
        return item

    def start(self):
        for index in range(PIECES):
            source = self.value.at[pl.ds(self.theirs + index * self.piece, self.piece)]
            self.first.append(self.copy(0, index, source, self.pair, self.near))

    def across_chips(self):
        for index in range(PIECES):
            rows = pl.ds(index * self.piece, self.piece)
            self.first[index].wait_recv()
            self.summed[rows] = (
                self.value[pl.ds(self.mine + index * self.piece, self.piece)] + self.pair[rows]
            )
            self.second.append(self.copy(1, index, self.summed.at[rows], self.other, self.far))

    def hand_back(self):
        for index in range(PIECES):
            rows = pl.ds(index * self.piece, self.piece)
            self.second[index].wait_recv()
            total = pl.ds(self.mine + index * self.piece, self.piece)
            self.out[total] = self.summed[rows] + self.other[rows]
            self.third.append(self.copy(2, index, self.out.at[total], self.back, self.near))

    def finish(self):
        for index in range(PIECES):
            self.third[index].wait_recv()
            rows = pl.ds(self.theirs + index * self.piece, self.piece)
            self.out[rows] = self.back[pl.ds(index * self.piece, self.piece)]
        for item in self.first + self.second + self.third:
            item.wait_send()


def head_scratch(value):
    landing = pltpu.VMEM((value.shape[0] // 2, value.shape[1]), jnp.float32)
    return [landing] * 4 + [pltpu.SemaphoreType.DMA((3, PIECES))] * 2


class ColumnShare:
    def __init__(self, mine, far_out, side_mine, side_far, send_sem, recv_sem):
        self.mine, self.far_out, self.side_mine, self.side_far = mine, far_out, side_mine, side_far
        self.send_sem, self.recv_sem = send_sem, recv_sem
        self.near, self.far = head_partners()
        self.piece = mine.shape[0] // SHARES
        self.items = []

    def copy(self, index, source, target, device):
        item = pltpu.make_async_remote_copy(
            src_ref=source,
            dst_ref=target,
            send_sem=self.send_sem.at[index],
            recv_sem=self.recv_sem.at[index],
            device_id=device,
            device_id_type=MESH,
        )
        item.start()
        self.items.append(item)

    def start(self):
        for k in range(SHARES):
            take = pl.ds(k * self.piece, self.piece)
            self.copy(k, self.mine.at[take], self.far_out.at[take], self.far)
        self.copy(SHARES, self.mine, self.side_mine, self.near)

    def finish(self):
        for k in range(SHARES):
            take = pl.ds(k * self.piece, self.piece)
            self.items[k].wait_recv()
            self.copy(SHARES + 1 + k, self.far_out.at[take], self.side_far.at[take], self.near)
        for item in self.items[SHARES:]:
            item.wait_recv()
        for item in self.items:
            item.wait_send()


def share_scratch():
    return [pltpu.SemaphoreType.DMA((2 * SHARES + 1,))] * 2


def sum_kernel(levels, gathering, sharing, *refs):
    value, *refs = refs
    wide, *refs = refs if gathering else [None] + refs
    shared, *refs = refs if sharing else [None] + refs
    out, *refs = refs
    landed, *refs = refs if gathering else [None] + refs
    far_out, side_mine, side_far, *refs = refs if sharing else [None] * 3 + refs
    stages = HeadSum(value, out, *refs[:6])
    source, send_sem, recv_sem, *refs = refs[6:] if gathering else [None] * 3 + refs[6:]
    share = ColumnShare(shared, far_out, side_mine, side_far, *refs) if sharing else None
    peers, sends = [], []
    if gathering:
        s, h, z, y = place_of()
        peers = [(2 * ((z + k) % levels) + y, h) for k in range(1, levels)]
    greet([stages.near, stages.far] + peers)
    stages.start()
    if gathering:
        rows, width = source.shape
        columns = pl.ds(pl.multiple_of(h * width, width), width)
        source[...] = wide[:, columns].astype(jnp.float32)
        for k in range(1, levels):
            sends.append(
                pltpu.make_async_remote_copy(
                    src_ref=source,
                    dst_ref=landed.at[pl.ds((k - 1) * rows, rows)],
                    send_sem=send_sem.at[k - 1],
                    recv_sem=recv_sem.at[k - 1],
                    device_id=peers[k - 1],
                    device_id_type=MESH,
                )
            )
            sends[-1].start()
    stages.across_chips()
    if sharing:
        share.start()
    stages.hand_back()
    stages.finish()
    if sharing:
        share.finish()
    for item in sends:
        item.wait_recv()
    for item in sends:
        item.wait_send()


def head_sum(value, collective_id, wide=None, shared=None):
    levels = lax.axis_size("seq") // 2
    ins, shapes, scratch = [value], [value.shape], head_scratch(value)
    if wide is not None:
        rows, width = wide.shape[0], wide.shape[1] // lax.axis_size("head")
        ins.append(wide)
        shapes.append(((levels - 1) * rows, width))
        scratch.append(pltpu.VMEM((rows, width), jnp.float32))
        scratch += [pltpu.SemaphoreType.DMA((levels - 1,))] * 2
    if shared is not None:
        ins.append(shared)
        shapes += [shared.shape] * 3
        scratch += share_scratch()
    return pl.pallas_call(
        functools.partial(sum_kernel, levels, wide is not None, shared is not None),
        out_shape=[jax.ShapeDtypeStruct(x, jnp.float32) for x in shapes],
        in_specs=[pl.BlockSpec(memory_space=pltpu.VMEM)] * len(ins),
        out_specs=[pl.BlockSpec(memory_space=pltpu.VMEM)] * len(shapes),
        scratch_shapes=scratch,
        compiler_params=pltpu.CompilerParams(
            collective_id=collective_id, has_side_effects=True, vmem_limit_bytes=24 * 1024 * 1024
        ),
    )(*ins)


def exchange_kernel(size, backward, sharing, *refs):
    pay, *refs = refs
    mine_cols, *refs = refs if sharing else [None] + refs
    out, *refs = refs
    far_out, side_mine, side_far, *refs = refs if sharing else [None] * 3 + refs
    near, pair, landed, part, other, send_sem, recv_sem, *share_sems = refs
    s, h, z, y = place_of()
    levels = size // 2
    beside = (2 * z + 1 - y, h)
    peers = [(2 * ((z + k) % levels) + y, h) for k in range(1, levels)]
    greet([beside] + peers + (list(head_partners()) if sharing else []))
    rows = out.shape[0]
    half = rows // 2

    def copy(index, source, target, device):
        return pltpu.make_async_remote_copy(
            src_ref=source,
            dst_ref=target,
            send_sem=send_sem.at[index],
            recv_sem=recv_sem.at[index],
            device_id=device,
            device_id_type=MESH,
        )

    first = copy(0, pay, near, beside)
    first.start()
    if sharing:
        share = ColumnShare(mine_cols, far_out, side_mine, side_far, *share_sems)
        share.start()
    second = (y == 0) if backward else (y == 1)
    mine = pl.multiple_of(y * half, half)
    theirs = pl.multiple_of((1 - y) * half, half)
    first.wait_recv()
    my_decay, near_decay = pay[rows : rows + 1], near[rows : rows + 1]
    my_half, near_half = pay[pl.ds(mine, half)], near[pl.ds(mine, half)]
    pair[0:half] = jnp.where(
        second, my_decay * near_half + my_half, near_decay * my_half + near_half
    )
    pair[half : half + 8] = pay[rows : rows + 8] * near[rows : rows + 8]
    sends = [copy(k, pair, landed.at[k - 1], peers[k - 1]) for k in range(1, levels)]
    for item in sends:
        item.start()
    for item in sends:
        item.wait_recv()
    total = jnp.zeros((half, out.shape[1]), jnp.float32)
    for back in range(levels - 1, 0, -1):
        k = levels - back if backward else back
        valid = (z + back < levels) if backward else (z - back >= 0)
        longer = landed[k - 1, half : half + 1] * total + landed[k - 1, 0:half]
        total = jnp.where(valid, longer, total)
    part[...] = total
    last = copy(levels, part, other, beside)
    last.start()
    near_decay_again = near[rows : rows + 1]
    out[pl.ds(mine, half)] = jnp.where(second, near_decay_again * total + near_half, total)
    last.wait_recv()
    rest = other[...]
    out[pl.ds(theirs, half)] = jnp.where(
        second, near_decay_again * rest + near[pl.ds(theirs, half)], rest
    )
    if sharing:
        share.finish()
    for item in [first, last] + sends:
        item.wait_send()


def entering(decay, state, backward, columns=None):
    sharing = columns is not None
    ins = [columns] if sharing else []
    size = lax.axis_size("seq")
    levels = size // 2
    rows, lanes = state.shape
    pay = jnp.concatenate([state, jnp.broadcast_to(decay[None], (8, lanes))], axis=0)
    half = rows // 2
    return pl.pallas_call(
        functools.partial(exchange_kernel, size, backward, sharing),
        out_shape=[jax.ShapeDtypeStruct(x.shape, jnp.float32) for x in [state] + ins * 3],
        in_specs=[pl.BlockSpec(memory_space=pltpu.VMEM)] * (1 + len(ins)),
        out_specs=[pl.BlockSpec(memory_space=pltpu.VMEM)] * (1 + 3 * len(ins)),
        scratch_shapes=[
            pltpu.VMEM((rows + 8, lanes), jnp.float32),
            pltpu.VMEM((half + 8, lanes), jnp.float32),
            pltpu.VMEM((levels - 1, half + 8, lanes), jnp.float32),
            pltpu.VMEM((half, lanes), jnp.float32),
            pltpu.VMEM((half, lanes), jnp.float32),
        ]
        + [pltpu.SemaphoreType.DMA((levels + 1,))] * 2
        + (share_scratch() if sharing else []),
        compiler_params=pltpu.CompilerParams(
            collective_id=3 if backward else 2,
            has_side_effects=True,
            vmem_limit_bytes=16 * 1024 * 1024,
        ),
    )(pay, *ins)


def tail_kernel(size, heads, arrays, *refs):
    value, feed, taps, expand, bias, second, squeeze, first, scale, *refs = refs
    ins, (value_out, feed_out, packed, *scratch) = refs[:arrays], refs[arrays:]
    own, shared, own_in, shared_in = scratch[:4]
    slots, scratch = scratch[4 : 4 + arrays], scratch[4 + arrays :]
    own_send, own_recv, shared_send, shared_recv, send_sem, recv_sem, *head_refs = scratch
    stages = HeadSum(value, value_out, *head_refs[:6])
    feeding = HeadSum(feed, feed_out, *head_refs[6:])
    half = size // 2
    me = lax.axis_index("seq")
    mine_head = lax.axis_index("head")
    low, high = me % 2, me // 2
    place = high + low * (2 * half - 1 - 2 * high)

    def member(position):
        position = (position + 2 * size) % size
        side = position // half
        return 2 * (position + side * (2 * half - 1 - 2 * position)) + side

    partners = ((member(place + 1), mine_head), (member(place - 1), mine_head))
    seq_bits, head_bits = size.bit_length() - 1, heads.bit_length() - 1
    small_peers = []
    for bit in range(seq_bits):
        step = 1 << bit
        small_peers.append((me + step - 2 * step * ((me // step) % 2), mine_head))
    small_peers += [stages.near, stages.far]
    greet(list(partners) + small_peers)

    rows = ins[0].shape[0] // size
    part = rows // 2

    def block(array, direction, position):
        start = pl.multiple_of(member(position) * rows + direction * part, part)
        return ins[array].at[pl.ds(start, part)]

    def copy(array, direction, step, source):
        return pltpu.make_async_remote_copy(
            src_ref=source,
            dst_ref=slots[array].at[direction, step],
            send_sem=send_sem.at[array, direction, step],
            recv_sem=recv_sem.at[array, direction, step],
            device_id=partners[direction],
            device_id_type=MESH,
        )

    stages.start()
    for array in range(arrays):
        for direction, sign in ((0, 1), (1, -1)):
            copy(array, direction, 0, block(array, direction, place - sign)).start()

    width, keys = squeeze.shape[1], expand.shape[1]
    mixed, lags, rank = taps.shape[1], taps.shape[0], expand.shape[0]
    own[0, 0:lags] = taps[...]
    for index in range(width // mixed):
        own[0, 8 + index : 9 + index] = second[:, index * mixed : (index + 1) * mixed]
    for index in range(rank // 8):
        own[0, 16:24, index * keys : (index + 1) * keys] = expand[index * 8 : (index + 1) * 8]
    own[0, 24:25, 0:keys] = bias[...]
    shared[0, 0:rank] = squeeze[...]
    shared[0, rank : rank + 1] = first[...]
    shared[0, rank + 1 : rank + 2, 0 : scale.shape[1]] = scale[...]

    def small_copy(buffer, landing, send, recv, index):
        return pltpu.make_async_remote_copy(
            src_ref=buffer.at[index],
            dst_ref=landing.at[index],
            send_sem=send.at[index],
            recv_sem=recv.at[index],
            device_id=small_peers[index],
            device_id_type=MESH,
        )

    own_copies = [small_copy(own, own_in, own_send, own_recv, k) for k in range(seq_bits)]
    shared_copies = [
        small_copy(shared, shared_in, shared_send, shared_recv, k)
        for k in range(seq_bits + head_bits)
    ]

    def small_step(index):
        if index > 0 and index <= seq_bits:
            own_copies[index - 1].wait_recv()
            own[index] = own[index - 1] + own_in[index - 1]
        if index > 0:
            shared_copies[index - 1].wait_recv()
            shared[index] = shared[index - 1] + shared_in[index - 1]
        if index < seq_bits:
            own_copies[index].start()
        if index < seq_bits + head_bits:
            shared_copies[index].start()

    def lap(step, carry):
        for array in range(arrays):
            for direction, sign in ((0, 1), (1, -1)):
                slot = slots[array].at[direction, step - 1]
                copy(array, direction, step - 1, slot).wait_recv()
                local = block(array, direction, place - sign * (step + 1))
                slot[...] = slot[...] + local[...]
                copy(array, direction, step, slot).start()
        return carry

    small_step(0)
    stages.across_chips()
    feeding.start()
    lap(1, 0)
    small_step(1)
    feeding.across_chips()
    lap(2, 0)
    small_step(2)
    stages.hand_back()
    lap(3, 0)
    small_step(3)
    lap(4, 0)
    small_step(4)
    feeding.hand_back()
    lax.fori_loop(5, size - 1, lap, 0)
    for index in range(5, seq_bits + head_bits + 1):
        small_step(index)
    stages.finish()
    feeding.finish()
    base = rows
    packed[base : base + 32, 0:mixed] = own[seq_bits]
    base += 32
    packed[base : base + shared.shape[1], 0:width] = shared[seq_bits + head_bits]
    column = 0
    for array in range(arrays):
        across_columns = slice(column, column + ins[array].shape[1])
        column += -(-ins[array].shape[1] // 128) * 128
        for direction in range(2):
            slot = slots[array].at[direction, size - 2]
            copy(array, direction, size - 2, slot).wait_recv()
            local = block(array, direction, place)
            packed[direction * part : (direction + 1) * part, across_columns] = slot[...] + local[...]

    def finish(step, carry):
        for array in range(arrays):
            for direction in range(2):
                copy(array, direction, step, slots[array].at[direction, step]).wait_send()
        return carry

    lax.fori_loop(0, size - 1, finish, 0)
    for item in own_copies + shared_copies:
        item.wait_send()


def tail(value, feed, own, shared, partials):
    size, heads = lax.axis_size("seq"), lax.axis_size("head")
    arrays = len(partials)
    rows = partials[0].shape[0] // size
    seq_bits, all_bits = size.bit_length() - 1, size.bit_length() + heads.bit_length() - 2
    squeeze = shared[0]
    own_shape = (32, own[0].shape[1])
    shared_shape = (squeeze.shape[0] + 8, squeeze.shape[1])
    wide = sum(-(-x.shape[1] // 128) * 128 for x in partials)
    shapes = [value.shape, feed.shape, (rows + own_shape[0] + shared_shape[0], wide)]
    operands = [value, feed, *own, *shared, *partials]
    return pl.pallas_call(
        functools.partial(tail_kernel, size, heads, arrays),
        out_shape=[jax.ShapeDtypeStruct(x, jnp.float32) for x in shapes],
        in_specs=[pl.BlockSpec(memory_space=pltpu.VMEM)] * len(operands),
        out_specs=[pl.BlockSpec(memory_space=pltpu.VMEM)] * len(shapes),
        scratch_shapes=[
            pltpu.VMEM((seq_bits + 1,) + own_shape, jnp.float32),
            pltpu.VMEM((all_bits + 1,) + shared_shape, jnp.float32),
            pltpu.VMEM((seq_bits,) + own_shape, jnp.float32),
            pltpu.VMEM((all_bits,) + shared_shape, jnp.float32),
        ]
        + [pltpu.VMEM((2, size - 1, rows // 2, x.shape[1]), jnp.float32) for x in partials]
        + [pltpu.SemaphoreType.DMA((seq_bits,))] * 2
        + [pltpu.SemaphoreType.DMA((all_bits,))] * 2
        + [pltpu.SemaphoreType.DMA((arrays, 2, size - 1))] * 2
        + head_scratch(value) * 2,
        compiler_params=pltpu.CompilerParams(
            collective_id=0, has_side_effects=True, vmem_limit_bytes=60 * 1024 * 1024
        ),
    )(*operands)


def feed_kernel(levels, block, *refs):
    n_own, u_own, gate, lift, drop, *refs = refs
    n_mine, n_far, n_side_mine, n_side_far, *refs = refs
    u_mine, u_far, u_side_mine, u_side_far, *refs = refs
    mine, theirs, n_all, u_all, gv_all, lv_all, inner_all, both = refs
    s, h, z, y = place_of()
    tokens, width = n_own.shape
    held = n_mine.shape[1]
    beside = h + 1 - 2 * (h % 2)
    far, beside_far = (h + 2) % 4, (beside + 2) % 4

    def columns(quarter):
        return pl.ds(pl.multiple_of(quarter * held, held), held)

    n_all[0:tokens] = n_own[...]
    u_all[0:tokens] = u_own[...]
    for k in range(levels - 1):
        rows = slice((k + 1) * tokens, (k + 2) * tokens)
        take = slice(k * tokens, (k + 1) * tokens)
        for quarter, n_source, u_source in (
            (h, n_mine, u_mine),
            (far, n_far, u_far),
            (beside, n_side_mine, u_side_mine),
            (beside_far, n_side_far, u_side_far),
        ):
            n_all[rows, columns(quarter)] = n_source[take].astype(jnp.bfloat16)
            u_all[rows, columns(quarter)] = u_source[take].astype(jnp.bfloat16)

    def step(index, carry):
        rows = pl.ds(pl.multiple_of(index * block, block), block)
        n, u = n_all[rows], u_all[rows]
        gate_value = against(n, gate[...])
        lift_value = against(n, lift[...])
        grad_inner = against(u, drop[...])
        logistic = jax.nn.sigmoid(gate_value)
        silu = gate_value * logistic
        slope = logistic * (1.0 + gate_value * (1.0 - logistic))
        gv_all[rows] = (grad_inner * lift_value * slope).astype(jnp.bfloat16)
        lv_all[rows] = (grad_inner * silu).astype(jnp.bfloat16)
        inner_all[rows] = (silu * lift_value).astype(jnp.bfloat16)
        return carry

    lax.fori_loop(0, levels * tokens // block, step, 0)
    per = mine.shape[2]
    pair = pl.ds(pl.multiple_of(2 * z * per, 2 * per), 2 * per)
    for index, (left, right) in enumerate(((n_all, gv_all), (n_all, lv_all), (u_all, inner_all))):
        both[...] = across(right[...], left[:, pair])
        mine[index] = both[:, pl.ds(pl.multiple_of(y * per, per), per)]
        theirs[index] = both[:, pl.ds(pl.multiple_of((1 - y) * per, per), per)]


def feed_gradients(normed_two, seed, gathered, gate, lift, drop):
    size = lax.axis_size("seq")
    levels = size // 2
    tokens, width = normed_two.shape
    hidden = gate.shape[0]
    shape = (3, hidden, width // size)
    everything = (levels * tokens, width)
    inside = (levels * tokens, hidden)
    operands = [normed_two, seed, gate, lift, drop] + gathered
    return pl.pallas_call(
        functools.partial(feed_kernel, levels, min(256, tokens)),
        out_shape=[jax.ShapeDtypeStruct(shape, jnp.float32)] * 2,
        in_specs=[pl.BlockSpec(memory_space=pltpu.VMEM)] * len(operands),
        out_specs=[pl.BlockSpec(memory_space=pltpu.VMEM)] * 2,
        scratch_shapes=[pltpu.VMEM(everything, jnp.bfloat16)] * 2
        + [pltpu.VMEM(inside, jnp.bfloat16)] * 3
        + [pltpu.VMEM((hidden, 2 * width // size), jnp.float32)],
        compiler_params=pltpu.CompilerParams(vmem_limit_bytes=56 * 1024 * 1024),
        cost_estimate=pl.CostEstimate(
            flops=2 * levels * tokens * width * hidden * 4,
            bytes_accessed=16 * 1024 * 1024,
            transcendentals=levels * tokens * hidden,
        ),
    )(*operands)


def finish_kernel(gathering, widths, *refs):
    block_in, gain, grad_one, grad_resid, residual, feed, packed, *refs = refs
    feed_mine, feed_more, *refs = refs if gathering else [None, None] + refs
    block_out, input_grad, first, second, scale, bias, taps, expand, squeeze, *outs = refs

    def step(index, carry):
        rows = pl.ds(pl.multiple_of(index * 64, 64), 64)
        values = block_in[rows].astype(jnp.float32)
        back = rms_back(values, rms_scale(values), gain[...], grad_one[rows])
        input_grad[rows] = grad_resid[rows] + back
        block_out[rows] = (residual[rows] + feed[rows]).astype(jnp.bfloat16)
        return carry

    lax.fori_loop(0, block_in.shape[0] // 64, step, 0)
    rows, width = outs[0].shape[0], block_in.shape[1]
    mixed, lags = taps.shape[2], taps.shape[0]
    rank, keys = expand.shape
    base = rows
    taps[:, 0] = packed[base : base + lags, 0:mixed]
    for index in range(width // mixed):
        second[:, index * mixed : (index + 1) * mixed] = packed[base + 8 + index : base + 9 + index, 0:mixed]
    for index in range(rank // 8):
        expand[index * 8 : (index + 1) * 8] = packed[base + 16 : base + 24, index * keys : (index + 1) * keys]
    bias[...] = packed[base + 24 : base + 25, 0:keys]
    base += 32
    squeeze[...] = packed[base : base + rank, 0:width]
    first[...] = packed[base + rank : base + rank + 1, 0:width]
    scale[...] = packed[base + rank + 1 : base + rank + 2, 0 : scale.shape[1]]
    column = 0
    for index, size in enumerate(widths):
        part = packed[0:rows, column : column + size]
        column += -(-size // 128) * 128
        if index == 0:
            outs[index][:, 0] = part
        else:
            outs[index][...] = jnp.transpose(part) if index == 2 else part
    if gathering:
        for index in range(3):
            outs[len(widths) + index][...] = feed_mine[index] + feed_more[index]


def finishing(block_in, gain, grad_one, grad_resid, residual, feed, packed, feed_pair, lags, expand, scale, widths):
    gathering = len(feed_pair) > 0
    operands = [block_in, gain, grad_one, grad_resid, residual, feed, packed, *feed_pair]
    width = block_in.shape[1]
    rank, keys = expand.shape
    rows = width // lax.axis_size("seq")
    shapes = [grad_one.shape, (1, width), (1, width), (1, scale.shape[0]), (1, keys)]
    shapes += [(lags, 1, widths[0]), expand.shape, (rank, width)]
    shapes += [(rows, 1, widths[0]), (rows, widths[1]), (widths[2], rows)]
    shapes += [(rows, x) for x in widths[3:]]
    if gathering:
        shapes += [feed_pair[0].shape[1:]] * 3
    shapes = [jax.ShapeDtypeStruct(x, jnp.float32) for x in shapes]
    return pl.pallas_call(
        functools.partial(finish_kernel, gathering, widths),
        out_shape=[jax.ShapeDtypeStruct(block_in.shape, jnp.bfloat16)] + shapes,
        in_specs=[pl.BlockSpec(memory_space=pltpu.VMEM)] * len(operands),
        compiler_params=pltpu.CompilerParams(vmem_limit_bytes=40 * 1024 * 1024),
    )(*operands)


def shifted(x, axis, by):
    size = lax.axis_size(axis)
    pairs = [(i, i + by) for i in range(size) if 0 <= i + by < size]
    return lax.ppermute(x, axis, pairs)


def product(left, right):
    return jnp.dot(left, right, preferred_element_type=jnp.float32)


def against(left, right):
    return lax.dot_general(
        left, right, (((1,), (1,)), ((), ())), preferred_element_type=jnp.float32
    )


def across(left, right):
    return lax.dot_general(
        left, right, (((0,), (0,)), ((), ())), preferred_element_type=jnp.float32
    )


def rms_scale(values):
    return lax.rsqrt(jnp.mean(values * values, axis=-1, keepdims=True) + EPS)


def rms_back(values, scale, gain, incoming):
    weighted = gain * incoming
    cube = scale * scale * scale
    return scale * weighted - values * cube * jnp.mean(values * weighted, axis=-1, keepdims=True)


def silu_grad(values):
    logistic = jax.nn.sigmoid(values)
    return logistic * (1.0 + values * (1.0 - logistic))


def causal_mask(size):
    rows = lax.broadcasted_iota(jnp.int32, (size, size), 0)
    columns = lax.broadcasted_iota(jnp.int32, (size, size), 1)
    return (columns <= rows).astype(jnp.float32)


def grouped(array, seqs, count):
    return array.reshape((seqs, count, GROUP) + array.shape[2:])


def running_sums(array):
    rows = [array[:, 0]]
    for index in range(1, array.shape[1]):
        rows.append(rows[-1] + array[:, index])
    return jnp.stack(rows, axis=1)


def local_states(decays, updates, backward):
    count = updates.shape[1]
    carry = jnp.zeros_like(updates[:, 0])
    states = [None] * count
    for index in range(count):
        group = count - 1 - index if backward else index
        states[group] = carry
        carry = jnp.exp(decays[:, group])[:, None] * carry + updates[:, group]
    return (jnp.stack(states, axis=1), carry)


def body(
    block_in,
    upstream,
    first_gain,
    project_in,
    filter_taps,
    squeeze,
    expand,
    decay_bias,
    gating,
    head_scale,
    project_out,
    second_gain,
    hidden_gate,
    hidden_lift,
    hidden_drop,
):
    seqs, tokens, width = block_in.shape
    total_rows = seqs * tokens
    key_dim = expand.shape[1]
    value_dim = gating.shape[1]
    mixed_dim = project_in.shape[2]
    lags = filter_taps.shape[0] - 1
    count = tokens // GROUP
    taps = filter_taps.reshape(lags + 1, mixed_dim)
    weight_in = project_in.reshape(width, mixed_dim)
    size, hidden = lax.axis_size("seq"), hidden_gate.shape[1]
    gathering = (size // 2) * total_rows * width * 18 <= 24 * 1024 * 1024
    seed = upstream.reshape(total_rows, width)
    residual_in = block_in.reshape(total_rows, width).astype(jnp.float32)
    scale_one = rms_scale(residual_in)
    normed_one = (residual_in * scale_one * first_gain).astype(jnp.bfloat16)
    projected = product(normed_one, weight_in).reshape(seqs, tokens, mixed_dim)
    before = shifted(projected[:, tokens - lags :], "seq", 1)
    padded = jnp.concatenate([before, projected], axis=1)
    filtered = taps[0] * projected
    for lag in range(1, lags + 1):
        filtered = filtered + taps[lag] * padded[:, lags - lag : lags - lag + tokens]
    activated_low = jax.nn.silu(filtered).astype(jnp.bfloat16)
    activated = lax.optimization_barrier(activated_low).astype(jnp.float32)
    root = key_dim ** (-0.5)
    query = grouped(activated[..., :key_dim] * root, seqs, count)
    keys = grouped(activated[..., key_dim : 2 * key_dim], seqs, count)
    values = grouped(activated[..., 2 * key_dim :], seqs, count)
    squeezed = product(normed_one, squeeze).astype(jnp.bfloat16)
    logits = product(squeezed, expand) + decay_bias
    log_decay = grouped(
        (jax.nn.log_sigmoid(logits) / NORMALIZER).reshape(seqs, tokens, key_dim), seqs, count
    )
    gate_in = product(normed_one, gating)
    mask = causal_mask(GROUP)
    running = jnp.einsum("ij,snjc->snic", mask, log_decay, precision=HIGH)
    last = running[:, :, -1]
    query_in = query * jnp.exp(running)
    key_in = keys * jnp.exp(-running)
    key_end = keys * jnp.exp(last[:, :, None] - running)
    scores = jnp.einsum("snic,snjc->snij", query_in, key_in, precision=HIGH) * mask
    updates = jnp.einsum("snjc,snjd->sndc", key_end, values, precision=HIGH)
    starts_zero, state_total = local_states(last, updates, False)
    decay_sum = jnp.sum(last, axis=1)
    decay_total = jnp.exp(decay_sum)
    incoming = entering(decay_total[0], state_total[0], False)[0][None]
    before_group = running_sums(last) - last
    starts = starts_zero + jnp.exp(before_group)[:, :, None] * incoming[:, None]
    mixed = jnp.einsum("snij,snjd->snid", scores, values, precision=HIGH)
    mixed = mixed + jnp.einsum("snic,sndc->snid", query_in, starts, precision=HIGH)
    mixed = mixed.reshape(total_rows, value_dim)
    scale_head = rms_scale(mixed)
    normed_head = mixed * scale_head * head_scale
    gated = (normed_head * jax.nn.silu(gate_in)).astype(jnp.bfloat16)
    branch, *seed_cols = head_sum(product(gated, project_out), 1, seed if gathering else None)
    residual = residual_in + branch
    scale_two = rms_scale(residual)
    normed_two = (residual * scale_two * second_gain).astype(jnp.bfloat16)
    gate_value = product(normed_two, hidden_gate)
    lift_value = product(normed_two, hidden_lift)
    inner = (jax.nn.silu(gate_value) * lift_value).astype(jnp.bfloat16)
    partial_feed = product(inner, hidden_drop)
    grad_inner = against(seed, hidden_drop)
    grad_gv = (grad_inner * lift_value * silu_grad(gate_value)).astype(jnp.bfloat16)
    grad_lv = (grad_inner * jax.nn.silu(gate_value)).astype(jnp.bfloat16)
    grad_two, *normed_cols = head_sum(
        against(grad_gv, hidden_gate) + against(grad_lv, hidden_lift),
        4,
        normed_two if gathering else None,
        *seed_cols,
    )
    seed_cols += normed_cols[1:]
    normed_cols = normed_cols[:1]
    grad_second = jnp.sum(grad_two * residual * scale_two, axis=0)
    grad_resid = seed.astype(jnp.float32) + rms_back(residual, scale_two, second_gain, grad_two)
    resid_low = grad_resid.astype(jnp.bfloat16)
    grad_output = across(resid_low, gated)
    grad_gated = against(resid_low, project_out)
    grad_gatein = (grad_gated * normed_head * silu_grad(gate_in)).astype(jnp.bfloat16)
    grad_normhead = grad_gated * jax.nn.silu(gate_in)
    grad_scale = jnp.sum(grad_normhead * mixed * scale_head, axis=0)
    grad_mixed_low = rms_back(mixed, scale_head, head_scale, grad_normhead).astype(jnp.bfloat16)
    grad_mixed = lax.optimization_barrier(grad_mixed_low).astype(jnp.float32)
    outgrad = grouped(grad_mixed.reshape(seqs, tokens, value_dim), seqs, count)
    query_end = jnp.einsum("snic,snid->sndc", query_in, outgrad, precision=HIGH)
    following_zero, back_total = local_states(last, query_end, True)
    after, *others = entering(decay_total[0], back_total[0], True, *normed_cols)
    normed_cols += others
    after = after[None]
    after_group = decay_sum[:, None] - running_sums(last)
    following = following_zero + jnp.exp(after_group)[:, :, None] * after[:, None]
    inner_group = jnp.einsum("snid,snjd->snij", outgrad, values, precision=HIGH) * mask
    grad_query = jnp.exp(running) * (
        jnp.einsum("snij,snjc->snic", inner_group, key_in, precision=HIGH)
        + jnp.einsum("snid,sndc->snic", outgrad, starts, precision=HIGH)
    )
    grad_keys = jnp.exp(-running) * jnp.einsum(
        "snij,snic->snjc", inner_group, query_in, precision=HIGH
    )
    grad_keys = grad_keys + jnp.exp(last[:, :, None] - running) * jnp.einsum(
        "snjd,sndc->snjc", values, following, precision=HIGH
    )
    grad_values = jnp.einsum("snij,snid->snjd", scores, outgrad, precision=HIGH)
    grad_values = grad_values + jnp.einsum("snjc,sndc->snjd", key_end, following, precision=HIGH)
    grad_running = (query * grad_query - keys * grad_keys).reshape(seqs, tokens, key_dim)
    state_end = decay_total[:, None] * incoming + state_total
    beyond = jnp.sum(state_end * after, axis=1)
    upper = jnp.transpose(causal_mask(tokens))
    suffix = jnp.einsum("ij,sjc->sic", upper, grad_running, precision=HIGH)
    grad_log = suffix + beyond[:, None]
    grad_act = jnp.concatenate(
        [
            grad_query.reshape(seqs, tokens, key_dim) * root,
            grad_keys.reshape(seqs, tokens, key_dim),
            grad_values.reshape(seqs, tokens, value_dim),
        ],
        axis=-1,
    )
    grad_filtered = grad_act * silu_grad(filtered)
    later = shifted(grad_filtered[:, :lags], "seq", -1)
    padded_back = jnp.concatenate([grad_filtered, later], axis=1)
    grad_projected = taps[0] * grad_filtered
    tap_rows = [jnp.sum(grad_filtered * projected, axis=(0, 1))]
    for lag in range(1, lags + 1):
        grad_projected = grad_projected + taps[lag] * padded_back[:, lag : lag + tokens]
        tap_rows.append(
            jnp.sum(grad_filtered * padded[:, lags - lag : lags - lag + tokens], axis=(0, 1))
        )
    grad_taps = jnp.stack(tap_rows).reshape(lags + 1, 1, mixed_dim)
    grad_projected = grad_projected.reshape(total_rows, mixed_dim).astype(jnp.bfloat16)
    grad_logits = grad_log.reshape(total_rows, key_dim) * jax.nn.sigmoid(-logits) / NORMALIZER
    grad_bias = jnp.sum(grad_logits, axis=0)
    logits_low = grad_logits.astype(jnp.bfloat16)
    grad_expand = across(squeezed, logits_low)
    squeeze_low = against(logits_low, expand).astype(jnp.bfloat16)
    grad_squeeze = across(squeeze_low, normed_one)
    partials = [across(normed_one, grad_projected), across(normed_one, grad_gatein), grad_output]
    feed_pair = ()
    if gathering:
        feed_mine, feed_theirs = feed_gradients(
            normed_two,
            seed,
            normed_cols + seed_cols,
            jnp.transpose(hidden_gate),
            jnp.transpose(hidden_lift),
            hidden_drop,
        )
        pairs = [(s, s + 1 - 2 * (s % 2)) for s in range(size)]
        feed_pair = (feed_mine, lax.ppermute(feed_theirs, "seq", pairs))
    else:
        partials += [across(normed_two, grad_gv), across(normed_two, grad_lv), across(seed, inner)]
    partial_value = (
        against(grad_projected, weight_in)
        + against(grad_gatein, gating)
        + against(squeeze_low, squeeze)
    )
    partial_first = jnp.sum(partial_value * residual_in * scale_one, axis=0)
    grad_one, feed, packed = tail(
        partial_value,
        partial_feed,
        (grad_taps[:, 0], grad_expand, grad_bias[None], grad_second[None]),
        (grad_squeeze, partial_first[None], grad_scale[None]),
        partials,
    )
    done = finishing(
        block_in[0],
        first_gain[None],
        grad_one,
        grad_resid,
        residual,
        feed,
        packed,
        feed_pair,
        lags + 1,
        expand,
        head_scale,
        tuple(x.shape[1] for x in partials),
    )
    block_out, input_grad, sum_first, sum_second, sum_scale, sum_bias = done[:6]
    sum_taps, sum_expand, sum_squeeze = done[6:9]
    own_project, own_gating, own_output, own_gate, own_lift, own_drop = done[9:]
    if gathering:
        own_gate, own_lift = jnp.transpose(own_gate), jnp.transpose(own_lift)
    else:
        own_drop = jnp.transpose(own_drop)
    return (
        block_out[None],
        input_grad[None],
        sum_first[0],
        own_project,
        sum_taps,
        jnp.transpose(sum_squeeze),
        sum_expand,
        sum_bias[0],
        own_gating,
        sum_scale[0],
        own_output,
        sum_second[0],
        own_gate,
        own_lift,
        own_drop,
    )


def solution(mesh):
    in_specs = (
        P(None, "seq", None),
        P(None, "seq", None),
        P(),
        P(None, "head", None),
        P(None, "head", None),
        P(),
        P(None, "head"),
        P("head"),
        P(None, "head"),
        P(),
        P("head", None),
        P(),
        P(None, "head"),
        P(None, "head"),
        P("head", None),
    )
    out_specs = (
        P(None, "seq", None),
        P(None, "seq", None),
        P(),
        P("seq", "head", None),
        P(None, "head", None),
        P(),
        P(None, "head"),
        P("head"),
        P("seq", "head"),
        P(),
        P("head", "seq"),
        P(),
        P("seq", "head"),
        P("seq", "head"),
        P("head", "seq"),
    )
    return jax.shard_map(body, mesh=mesh, in_specs=in_specs, out_specs=out_specs, check_vma=False)
```

```python
import functools

import jax
import jax.numpy as jnp
from jax import lax
from jax.experimental import pallas as pl
from jax.experimental.pallas import tpu as pltpu
from jax.sharding import PartitionSpec as P

GROUP = 64


EPS = 1e-05
NORMALIZER = 16.0
HIGH = lax.Precision.HIGHEST


MESH = pl.DeviceIdType.MESH
PIECES = 4
SHARES = 3


def greet(devices):
    barrier = pltpu.get_barrier_semaphore()
    for device in devices:
        pl.semaphore_signal(barrier, inc=1, device_id=device, device_id_type=MESH)
    pl.semaphore_wait(barrier, len(devices))


def place_of():
    s, h = lax.axis_index("seq"), lax.axis_index("head")
    return s, h, s // 2, s % 2


def head_partners():
    s, h = lax.axis_index("seq"), lax.axis_index("head")
    core, chip = h % 2, h // 2
    return (s, chip * 2 + 1 - core), (s, (1 - chip) * 2 + core)


class HeadSum:
    def __init__(self, value, out, pair, summed, other, back, send_sem, recv_sem):
        self.value, self.out = value, out
        self.pair, self.summed, self.other, self.back = pair, summed, other, back
        self.send_sem, self.recv_sem = send_sem, recv_sem
        self.near, self.far = head_partners()
        core = lax.axis_index("head") % 2
        half = value.shape[0] // 2
        self.piece = half // PIECES
        self.mine = pl.multiple_of(core * half, half)
        self.theirs = pl.multiple_of((1 - core) * half, half)
        self.first, self.second, self.third = [], [], []

    def copy(self, stage, index, source, target, device):
        item = pltpu.make_async_remote_copy(
            src_ref=source,
            dst_ref=target.at[pl.ds(index * self.piece, self.piece)],
            send_sem=self.send_sem.at[stage, index],
            recv_sem=self.recv_sem.at[stage, index],
            device_id=device,
            device_id_type=MESH,
        )
        item.start()
        return item

    def start(self):
        for index in range(PIECES):
            source = self.value.at[pl.ds(self.theirs + index * self.piece, self.piece)]
            self.first.append(self.copy(0, index, source, self.pair, self.near))

    def across_chips(self):
        for index in range(PIECES):
            rows = pl.ds(index * self.piece, self.piece)
            self.first[index].wait_recv()
            self.summed[rows] = (
                self.value[pl.ds(self.mine + index * self.piece, self.piece)] + self.pair[rows]
            )
            self.second.append(self.copy(1, index, self.summed.at[rows], self.other, self.far))

    def hand_back(self):
        for index in range(PIECES):
            rows = pl.ds(index * self.piece, self.piece)
            self.second[index].wait_recv()
            total = pl.ds(self.mine + index * self.piece, self.piece)
            self.out[total] = self.summed[rows] + self.other[rows]
            self.third.append(self.copy(2, index, self.out.at[total], self.back, self.near))

    def finish(self):
        for index in range(PIECES):
            self.third[index].wait_recv()
            rows = pl.ds(self.theirs + index * self.piece, self.piece)
            self.out[rows] = self.back[pl.ds(index * self.piece, self.piece)]
        for item in self.first + self.second + self.third:
            item.wait_send()


def head_scratch(value):
    landing = pltpu.VMEM((value.shape[0] // 2, value.shape[1]), jnp.float32)
    return [landing] * 4 + [pltpu.SemaphoreType.DMA((3, PIECES))] * 2


class ColumnShare:
    def __init__(self, mine, far_out, side_mine, side_far, send_sem, recv_sem):
        self.mine, self.far_out, self.side_mine, self.side_far = mine, far_out, side_mine, side_far
        self.send_sem, self.recv_sem = send_sem, recv_sem
        self.near, self.far = head_partners()
        self.piece = mine.shape[0] // SHARES
        self.items = {}

    def copy(self, index, source, target, device):
        item = pltpu.make_async_remote_copy(
            src_ref=source,
            dst_ref=target,
            send_sem=self.send_sem.at[index],
            recv_sem=self.recv_sem.at[index],
            device_id=device,
            device_id_type=MESH,
        )
        item.start()
        self.items[index] = item

    def start_piece(self, k):
        take = pl.ds(k * self.piece, self.piece)
        self.copy(k, self.mine.at[take], self.far_out.at[take], self.far)

    def start(self):
        for k in range(SHARES):
            self.start_piece(k)
        self.copy(SHARES, self.mine, self.side_mine, self.near)

    def finish(self):
        for k in range(SHARES):
            take = pl.ds(k * self.piece, self.piece)
            self.items[k].wait_recv()
            self.copy(SHARES + 1 + k, self.far_out.at[take], self.side_far.at[take], self.near)
        for k in range(SHARES, 2 * SHARES + 1):
            self.items[k].wait_recv()
        for k in range(2 * SHARES + 1):
            self.items[k].wait_send()


def share_scratch():
    return [pltpu.SemaphoreType.DMA((2 * SHARES + 1,))] * 2


def sum_kernel(levels, gathering, sharing, *refs):
    value, *refs = refs
    wide, *refs = refs if gathering else [None] + refs
    shared, *refs = refs if sharing else [None] + refs
    out, *refs = refs
    landed, *refs = refs if gathering else [None] + refs
    far_out, side_mine, side_far, *refs = refs if sharing else [None] * 3 + refs
    stages = HeadSum(value, out, *refs[:6])
    source, send_sem, recv_sem, *refs = refs[6:] if gathering else [None] * 3 + refs[6:]
    share = ColumnShare(shared, far_out, side_mine, side_far, *refs) if sharing else None
    peers, sends = [], []
    if gathering:
        s, h, z, y = place_of()
        peers = [(2 * ((z + k) % levels) + y, h) for k in range(1, levels)]
    greet([stages.near, stages.far] + peers)
    stages.start()
    if gathering:
        rows, width = source.shape
        columns = pl.ds(pl.multiple_of(h * width, width), width)
        source[...] = wide[:, columns].astype(jnp.float32)
        for k in range(1, levels):
            sends.append(
                pltpu.make_async_remote_copy(
                    src_ref=source,
                    dst_ref=landed.at[pl.ds((k - 1) * rows, rows)],
                    send_sem=send_sem.at[k - 1],
                    recv_sem=recv_sem.at[k - 1],
                    device_id=peers[k - 1],
                    device_id_type=MESH,
                )
            )
            sends[-1].start()
    stages.across_chips()
    if sharing:
        share.start()
    stages.hand_back()
    stages.finish()
    if sharing:
        share.finish()
    for item in sends:
        item.wait_recv()
    for item in sends:
        item.wait_send()


def head_sum(value, collective_id, wide=None, shared=None):
    levels = lax.axis_size("seq") // 2
    ins, shapes, scratch = [value], [value.shape], head_scratch(value)
    if wide is not None:
        rows, width = wide.shape[0], wide.shape[1] // lax.axis_size("head")
        ins.append(wide)
        shapes.append(((levels - 1) * rows, width))
        scratch.append(pltpu.VMEM((rows, width), jnp.float32))
        scratch += [pltpu.SemaphoreType.DMA((levels - 1,))] * 2
    if shared is not None:
        ins.append(shared)
        shapes += [shared.shape] * 3
        scratch += share_scratch()
    return pl.pallas_call(
        functools.partial(sum_kernel, levels, wide is not None, shared is not None),
        out_shape=[jax.ShapeDtypeStruct(x, jnp.float32) for x in shapes],
        in_specs=[pl.BlockSpec(memory_space=pltpu.VMEM)] * len(ins),
        out_specs=[pl.BlockSpec(memory_space=pltpu.VMEM)] * len(shapes),
        scratch_shapes=scratch,
        compiler_params=pltpu.CompilerParams(
            collective_id=collective_id, has_side_effects=True, vmem_limit_bytes=24 * 1024 * 1024
        ),
    )(*ins)


class Exchange:
    def __init__(self, size, backward, pay, out, near, pair, landed, part, other, send_sem, recv_sem):
        self.backward, self.pay, self.out = backward, pay, out
        self.near, self.pair, self.landed, self.part, self.other = near, pair, landed, part, other
        self.send_sem, self.recv_sem = send_sem, recv_sem
        s, h, self.z, self.y = place_of()
        self.levels = size // 2
        self.beside = (2 * self.z + 1 - self.y, h)
        self.peers = [
            (2 * ((self.z + k) % self.levels) + self.y, h) for k in range(1, self.levels)
        ]
        self.partners = [self.beside] + self.peers
        self.rows = out.shape[0]
        self.half = self.rows // 2
        self.mine = pl.multiple_of(self.y * self.half, self.half)
        self.theirs = pl.multiple_of((1 - self.y) * self.half, self.half)
        self.second = (self.y == 0) if backward else (self.y == 1)

    def copy(self, index, source, target, device):
        item = pltpu.make_async_remote_copy(
            src_ref=source,
            dst_ref=target,
            send_sem=self.send_sem.at[index],
            recv_sem=self.recv_sem.at[index],
            device_id=device,
            device_id_type=MESH,
        )
        item.start()
        return item

    def start(self):
        self.first = self.copy(0, self.pay, self.near, self.beside)

    def along(self):
        pay, near, rows, half = self.pay, self.near, self.rows, self.half
        self.first.wait_recv()
        my_decay, near_decay = pay[rows : rows + 1], near[rows : rows + 1]
        my_half, near_half = pay[pl.ds(self.mine, half)], near[pl.ds(self.mine, half)]
        self.pair[0:half] = jnp.where(
            self.second, my_decay * near_half + my_half, near_decay * my_half + near_half
        )
        self.pair[half : half + 8] = pay[rows : rows + 8] * near[rows : rows + 8]
        self.sends = [
            self.copy(k, self.pair, self.landed.at[k - 1], self.peers[k - 1])
            for k in range(1, self.levels)
        ]

    def join(self):
        half, levels, z = self.half, self.levels, self.z
        for item in self.sends:
            item.wait_recv()
        total = jnp.zeros((half, self.out.shape[1]), jnp.float32)
        for back in range(levels - 1, 0, -1):
            k = levels - back if self.backward else back
            valid = (z + back < levels) if self.backward else (z - back >= 0)
            longer = self.landed[k - 1, half : half + 1] * total + self.landed[k - 1, 0:half]
            total = jnp.where(valid, longer, total)
        self.part[...] = total
        self.last = self.copy(levels, self.part, self.other, self.beside)
        decay, near_half = self.near[self.rows : self.rows + 1], self.near[pl.ds(self.mine, half)]
        self.out[pl.ds(self.mine, half)] = jnp.where(self.second, decay * total + near_half, total)

    def finish(self):
        half = self.half
        self.last.wait_recv()
        rest, near_half = self.other[...], self.near[pl.ds(self.theirs, half)]
        decay = self.near[self.rows : self.rows + 1]
        self.out[pl.ds(self.theirs, half)] = jnp.where(self.second, decay * rest + near_half, rest)
        for item in [self.first, self.last] + self.sends:
            item.wait_send()


def exchange_scratch(size, rows, lanes):
    half, levels = rows // 2, size // 2
    return [
        pltpu.VMEM((rows + 8, lanes), jnp.float32),
        pltpu.VMEM((half + 8, lanes), jnp.float32),
        pltpu.VMEM((levels - 1, half + 8, lanes), jnp.float32),
        pltpu.VMEM((half, lanes), jnp.float32),
        pltpu.VMEM((half, lanes), jnp.float32),
    ] + [pltpu.SemaphoreType.DMA((levels + 1,))] * 2


def exchange_kernel(size, backward, sharing, *refs):
    pay, *refs = refs
    mine_cols, *refs = refs if sharing else [None] + refs
    out, *refs = refs
    far_out, side_mine, side_far, *refs = refs if sharing else [None] * 3 + refs
    exchange = Exchange(size, backward, pay, out, *refs[:7])
    greet(exchange.partners + (list(head_partners()) if sharing else []))
    exchange.start()
    if sharing:
        share = ColumnShare(mine_cols, far_out, side_mine, side_far, *refs[7:])
        share.start()
    exchange.along()
    exchange.join()
    exchange.finish()
    if sharing:
        share.finish()


def entering(decay, state, backward, columns=None):
    sharing = columns is not None
    ins = [columns] if sharing else []
    size = lax.axis_size("seq")
    levels = size // 2
    rows, lanes = state.shape
    pay = jnp.concatenate([state, jnp.broadcast_to(decay[None], (8, lanes))], axis=0)
    return pl.pallas_call(
        functools.partial(exchange_kernel, size, backward, sharing),
        out_shape=[jax.ShapeDtypeStruct(x.shape, jnp.float32) for x in [state] + ins * 3],
        in_specs=[pl.BlockSpec(memory_space=pltpu.VMEM)] * (1 + len(ins)),
        out_specs=[pl.BlockSpec(memory_space=pltpu.VMEM)] * (1 + 3 * len(ins)),
        scratch_shapes=exchange_scratch(size, rows, lanes)
        + (share_scratch() if sharing else []),
        compiler_params=pltpu.CompilerParams(
            collective_id=3 if backward else 2,
            has_side_effects=True,
            vmem_limit_bytes=16 * 1024 * 1024,
        ),
    )(pay, *ins)


def tail_kernel(size, heads, arrays, *refs):
    value, feed, taps, expand, bias, second, squeeze, first, scale, *refs = refs
    ins, (value_out, feed_out, packed, *scratch) = refs[:arrays], refs[arrays:]
    own, shared, own_in, shared_in = scratch[:4]
    slots, scratch = scratch[4 : 4 + arrays], scratch[4 + arrays :]
    own_send, own_recv, shared_send, shared_recv, send_sem, recv_sem, *head_refs = scratch
    stages = HeadSum(value, value_out, *head_refs[:6])
    feeding = HeadSum(feed, feed_out, *head_refs[6:])
    half = size // 2
    me = lax.axis_index("seq")
    mine_head = lax.axis_index("head")
    low, high = me % 2, me // 2
    place = high + low * (2 * half - 1 - 2 * high)

    def member(position):
        position = (position + 2 * size) % size
        side = position // half
        return 2 * (position + side * (2 * half - 1 - 2 * position)) + side

    partners = ((member(place + 1), mine_head), (member(place - 1), mine_head))
    seq_bits, head_bits = size.bit_length() - 1, heads.bit_length() - 1
    small_peers = []
    for bit in range(seq_bits):
        step = 1 << bit
        small_peers.append((me + step - 2 * step * ((me // step) % 2), mine_head))
    small_peers += [stages.near, stages.far]
    greet(list(partners) + small_peers)

    rows = ins[0].shape[0] // size
    part = rows // 2

    def block(array, direction, position):
        start = pl.multiple_of(member(position) * rows + direction * part, part)
        return ins[array].at[pl.ds(start, part)]

    def copy(array, direction, step, source):
        return pltpu.make_async_remote_copy(
            src_ref=source,
            dst_ref=slots[array].at[direction, step],
            send_sem=send_sem.at[array, direction, step],
            recv_sem=recv_sem.at[array, direction, step],
            device_id=partners[direction],
            device_id_type=MESH,
        )

    stages.start()
    for array in range(arrays):
        for direction, sign in ((0, 1), (1, -1)):
            copy(array, direction, 0, block(array, direction, place - sign)).start()

    width, keys = squeeze.shape[1], expand.shape[1]
    mixed, lags, rank = taps.shape[1], taps.shape[0], expand.shape[0]
    own[0, 0:lags] = taps[...]
    for index in range(width // mixed):
        own[0, 8 + index : 9 + index] = second[:, index * mixed : (index + 1) * mixed]
    for index in range(rank // 8):
        own[0, 16:24, index * keys : (index + 1) * keys] = expand[index * 8 : (index + 1) * 8]
    own[0, 24:25, 0:keys] = bias[...]
    shared[0, 0:rank] = squeeze[...]
    shared[0, rank : rank + 1] = first[...]
    shared[0, rank + 1 : rank + 2, 0 : scale.shape[1]] = scale[...]

    def small_copy(buffer, landing, send, recv, index):
        return pltpu.make_async_remote_copy(
            src_ref=buffer.at[index],
            dst_ref=landing.at[index],
            send_sem=send.at[index],
            recv_sem=recv.at[index],
            device_id=small_peers[index],
            device_id_type=MESH,
        )

    own_copies = [small_copy(own, own_in, own_send, own_recv, k) for k in range(seq_bits)]
    shared_copies = [
        small_copy(shared, shared_in, shared_send, shared_recv, k)
        for k in range(seq_bits + head_bits)
    ]

    def small_step(index):
        if index > 0 and index <= seq_bits:
            own_copies[index - 1].wait_recv()
            own[index] = own[index - 1] + own_in[index - 1]
        if index > 0:
            shared_copies[index - 1].wait_recv()
            shared[index] = shared[index - 1] + shared_in[index - 1]
        if index < seq_bits:
            own_copies[index].start()
        if index < seq_bits + head_bits:
            shared_copies[index].start()

    def lap(step, carry):
        for array in range(arrays):
            for direction, sign in ((0, 1), (1, -1)):
                slot = slots[array].at[direction, step - 1]
                copy(array, direction, step - 1, slot).wait_recv()
                local = block(array, direction, place - sign * (step + 1))
                slot[...] = slot[...] + local[...]
                copy(array, direction, step, slot).start()
        return carry

    small_step(0)
    stages.across_chips()
    feeding.start()
    lap(1, 0)
    small_step(1)
    feeding.across_chips()
    lap(2, 0)
    small_step(2)
    stages.hand_back()
    lap(3, 0)
    small_step(3)
    lap(4, 0)
    small_step(4)
    feeding.hand_back()
    lax.fori_loop(5, size - 1, lap, 0)
    for index in range(5, seq_bits + head_bits + 1):
        small_step(index)
    stages.finish()
    feeding.finish()
    base = rows
    packed[base : base + 32, 0:mixed] = own[seq_bits]
    base += 32
    packed[base : base + shared.shape[1], 0:width] = shared[seq_bits + head_bits]
    column = 0
    for array in range(arrays):
        across_columns = slice(column, column + ins[array].shape[1])
        column += -(-ins[array].shape[1] // 128) * 128
        for direction in range(2):
            slot = slots[array].at[direction, size - 2]
            copy(array, direction, size - 2, slot).wait_recv()
            local = block(array, direction, place)
            packed[direction * part : (direction + 1) * part, across_columns] = slot[...] + local[...]

    def finish(step, carry):
        for array in range(arrays):
            for direction in range(2):
                copy(array, direction, step, slots[array].at[direction, step]).wait_send()
        return carry

    lax.fori_loop(0, size - 1, finish, 0)
    for item in own_copies + shared_copies:
        item.wait_send()


def tail(value, feed, own, shared, partials):
    size, heads = lax.axis_size("seq"), lax.axis_size("head")
    arrays = len(partials)
    rows = partials[0].shape[0] // size
    seq_bits, all_bits = size.bit_length() - 1, size.bit_length() + heads.bit_length() - 2
    squeeze = shared[0]
    own_shape = (32, own[0].shape[1])
    shared_shape = (squeeze.shape[0] + 8, squeeze.shape[1])
    wide = sum(-(-x.shape[1] // 128) * 128 for x in partials)
    shapes = [value.shape, feed.shape, (rows + own_shape[0] + shared_shape[0], wide)]
    operands = [value, feed, *own, *shared, *partials]
    return pl.pallas_call(
        functools.partial(tail_kernel, size, heads, arrays),
        out_shape=[jax.ShapeDtypeStruct(x, jnp.float32) for x in shapes],
        in_specs=[pl.BlockSpec(memory_space=pltpu.VMEM)] * len(operands),
        out_specs=[pl.BlockSpec(memory_space=pltpu.VMEM)] * len(shapes),
        scratch_shapes=[
            pltpu.VMEM((seq_bits + 1,) + own_shape, jnp.float32),
            pltpu.VMEM((all_bits + 1,) + shared_shape, jnp.float32),
            pltpu.VMEM((seq_bits,) + own_shape, jnp.float32),
            pltpu.VMEM((all_bits,) + shared_shape, jnp.float32),
        ]
        + [pltpu.VMEM((2, size - 1, rows // 2, x.shape[1]), jnp.float32) for x in partials]
        + [pltpu.SemaphoreType.DMA((seq_bits,))] * 2
        + [pltpu.SemaphoreType.DMA((all_bits,))] * 2
        + [pltpu.SemaphoreType.DMA((arrays, 2, size - 1))] * 2
        + head_scratch(value) * 2,
        compiler_params=pltpu.CompilerParams(
            collective_id=0, has_side_effects=True, vmem_limit_bytes=60 * 1024 * 1024
        ),
    )(*operands)


def feed_kernel(levels, block, *refs):
    n_own, u_own, gate, lift, drop, *refs = refs
    n_mine, n_far, n_side_mine, n_side_far, *refs = refs
    u_mine, u_far, u_side_mine, u_side_far, *refs = refs
    mine, theirs, n_all, u_all, gv_all, lv_all, inner_all, both = refs
    s, h, z, y = place_of()
    tokens, width = n_own.shape
    held = n_mine.shape[1]
    beside = h + 1 - 2 * (h % 2)
    far, beside_far = (h + 2) % 4, (beside + 2) % 4

    def columns(quarter):
        return pl.ds(pl.multiple_of(quarter * held, held), held)

    n_all[0:tokens] = n_own[...]
    u_all[0:tokens] = u_own[...]
    for k in range(levels - 1):
        rows = slice((k + 1) * tokens, (k + 2) * tokens)
        take = slice(k * tokens, (k + 1) * tokens)
        for quarter, n_source, u_source in (
            (h, n_mine, u_mine),
            (far, n_far, u_far),
            (beside, n_side_mine, u_side_mine),
            (beside_far, n_side_far, u_side_far),
        ):
            n_all[rows, columns(quarter)] = n_source[take].astype(jnp.bfloat16)
            u_all[rows, columns(quarter)] = u_source[take].astype(jnp.bfloat16)

    def step(index, carry):
        rows = pl.ds(pl.multiple_of(index * block, block), block)
        n, u = n_all[rows], u_all[rows]
        gate_value = against(n, gate[...])
        lift_value = against(n, lift[...])
        grad_inner = against(u, drop[...])
        logistic = jax.nn.sigmoid(gate_value)
        silu = gate_value * logistic
        slope = logistic * (1.0 + gate_value * (1.0 - logistic))
        gv_all[rows] = (grad_inner * lift_value * slope).astype(jnp.bfloat16)
        lv_all[rows] = (grad_inner * silu).astype(jnp.bfloat16)
        inner_all[rows] = (silu * lift_value).astype(jnp.bfloat16)
        return carry

    lax.fori_loop(0, levels * tokens // block, step, 0)
    per = mine.shape[2]
    pair = pl.ds(pl.multiple_of(2 * z * per, 2 * per), 2 * per)
    for index, (left, right) in enumerate(((n_all, gv_all), (n_all, lv_all), (u_all, inner_all))):
        both[...] = across(right[...], left[:, pair])
        mine[index] = both[:, pl.ds(pl.multiple_of(y * per, per), per)]
        theirs[index] = both[:, pl.ds(pl.multiple_of((1 - y) * per, per), per)]


def feed_gradients(normed_two, seed, gathered, gate, lift, drop):
    size = lax.axis_size("seq")
    levels = size // 2
    tokens, width = normed_two.shape
    hidden = gate.shape[0]
    shape = (3, hidden, width // size)
    everything = (levels * tokens, width)
    inside = (levels * tokens, hidden)
    operands = [normed_two, seed, gate, lift, drop] + gathered
    return pl.pallas_call(
        functools.partial(feed_kernel, levels, min(256, tokens)),
        out_shape=[jax.ShapeDtypeStruct(shape, jnp.float32)] * 2,
        in_specs=[pl.BlockSpec(memory_space=pltpu.VMEM)] * len(operands),
        out_specs=[pl.BlockSpec(memory_space=pltpu.VMEM)] * 2,
        scratch_shapes=[pltpu.VMEM(everything, jnp.bfloat16)] * 2
        + [pltpu.VMEM(inside, jnp.bfloat16)] * 3
        + [pltpu.VMEM((hidden, 2 * width // size), jnp.float32)],
        compiler_params=pltpu.CompilerParams(vmem_limit_bytes=56 * 1024 * 1024),
        cost_estimate=pl.CostEstimate(
            flops=2 * levels * tokens * width * hidden * 4,
            bytes_accessed=16 * 1024 * 1024,
            transcendentals=levels * tokens * hidden,
        ),
    )(*operands)


def finish_kernel(gathering, widths, *refs):
    block_in, gain, grad_one, grad_resid, residual, feed, packed, *refs = refs
    feed_mine, feed_more, *refs = refs if gathering else [None, None] + refs
    block_out, input_grad, first, second, scale, bias, taps, expand, squeeze, *outs = refs

    def step(index, carry):
        rows = pl.ds(pl.multiple_of(index * 64, 64), 64)
        values = block_in[rows].astype(jnp.float32)
        back = rms_back(values, rms_scale(values), gain[...], grad_one[rows])
        input_grad[rows] = grad_resid[rows] + back
        block_out[rows] = (residual[rows] + feed[rows]).astype(jnp.bfloat16)
        return carry

    lax.fori_loop(0, block_in.shape[0] // 64, step, 0)
    rows, width = outs[0].shape[0], block_in.shape[1]
    mixed, lags = taps.shape[2], taps.shape[0]
    rank, keys = expand.shape
    base = rows
    taps[:, 0] = packed[base : base + lags, 0:mixed]
    for index in range(width // mixed):
        second[:, index * mixed : (index + 1) * mixed] = packed[base + 8 + index : base + 9 + index, 0:mixed]
    for index in range(rank // 8):
        expand[index * 8 : (index + 1) * 8] = packed[base + 16 : base + 24, index * keys : (index + 1) * keys]
    bias[...] = packed[base + 24 : base + 25, 0:keys]
    base += 32
    squeeze[...] = packed[base : base + rank, 0:width]
    first[...] = packed[base + rank : base + rank + 1, 0:width]
    scale[...] = packed[base + rank + 1 : base + rank + 2, 0 : scale.shape[1]]
    column = 0
    for index, size in enumerate(widths):
        part = packed[0:rows, column : column + size]
        column += -(-size // 128) * 128
        if index == 0:
            outs[index][:, 0] = part
        else:
            outs[index][...] = jnp.transpose(part) if index == 2 else part
    if gathering:
        for index in range(3):
            outs[len(widths) + index][...] = feed_mine[index] + feed_more[index]


def finishing(block_in, gain, grad_one, grad_resid, residual, feed, packed, feed_pair, lags, expand, scale, widths):
    gathering = len(feed_pair) > 0
    operands = [block_in, gain, grad_one, grad_resid, residual, feed, packed, *feed_pair]
    width = block_in.shape[1]
    rank, keys = expand.shape
    rows = width // lax.axis_size("seq")
    shapes = [grad_one.shape, (1, width), (1, width), (1, scale.shape[0]), (1, keys)]
    shapes += [(lags, 1, widths[0]), expand.shape, (rank, width)]
    shapes += [(rows, 1, widths[0]), (rows, widths[1]), (widths[2], rows)]
    shapes += [(rows, x) for x in widths[3:]]
    if gathering:
        shapes += [feed_pair[0].shape[1:]] * 3
    shapes = [jax.ShapeDtypeStruct(x, jnp.float32) for x in shapes]
    return pl.pallas_call(
        functools.partial(finish_kernel, gathering, widths),
        out_shape=[jax.ShapeDtypeStruct(block_in.shape, jnp.bfloat16)] + shapes,
        in_specs=[pl.BlockSpec(memory_space=pltpu.VMEM)] * len(operands),
        compiler_params=pltpu.CompilerParams(vmem_limit_bytes=40 * 1024 * 1024),
    )(*operands)


def shifted(x, axis, by):
    size = lax.axis_size(axis)
    pairs = [(i, i + by) for i in range(size) if 0 <= i + by < size]
    return lax.ppermute(x, axis, pairs)


def product(left, right):
    return jnp.dot(left, right, preferred_element_type=jnp.float32)


def against(left, right):
    return lax.dot_general(
        left, right, (((1,), (1,)), ((), ())), preferred_element_type=jnp.float32
    )


def across(left, right):
    return lax.dot_general(
        left, right, (((0,), (0,)), ((), ())), preferred_element_type=jnp.float32
    )


def rms_scale(values):
    return lax.rsqrt(jnp.mean(values * values, axis=-1, keepdims=True) + EPS)


def rms_back(values, scale, gain, incoming):
    weighted = gain * incoming
    cube = scale * scale * scale
    return scale * weighted - values * cube * jnp.mean(values * weighted, axis=-1, keepdims=True)


def silu_grad(values):
    logistic = jax.nn.sigmoid(values)
    return logistic * (1.0 + values * (1.0 - logistic))


def causal_mask(size):
    rows = lax.broadcasted_iota(jnp.int32, (size, size), 0)
    columns = lax.broadcasted_iota(jnp.int32, (size, size), 1)
    return (columns <= rows).astype(jnp.float32)


def exact(left, right, contract):
    return lax.dot_general(
        left, right, (contract, ((), ())), precision=HIGH, preferred_element_type=jnp.float32
    )


class LineGather:
    def __init__(self, levels, landed, source, send_sem, recv_sem):
        self.levels, self.landed, self.source = levels, landed, source
        self.send_sem, self.recv_sem = send_sem, recv_sem
        s, h, z, y = place_of()
        self.head = h
        self.peers = [(2 * ((z + k) % levels) + y, h) for k in range(1, levels)]

    def start(self, wide):
        rows, width = self.source.shape
        columns = pl.ds(pl.multiple_of(self.head * width, width), width)
        self.source[...] = wide[:, columns].astype(jnp.float32)
        self.sends = [
            pltpu.make_async_remote_copy(
                src_ref=self.source,
                dst_ref=self.landed.at[pl.ds(k * rows, rows)],
                send_sem=self.send_sem.at[k],
                recv_sem=self.recv_sem.at[k],
                device_id=self.peers[k],
                device_id_type=MESH,
            )
            for k in range(self.levels - 1)
        ]
        self.sends[0].start()
        self.sends[-1].start()

    def start_rest(self):
        for item in self.sends[1:-1]:
            item.start()

    def arrive(self, k):
        self.sends[k].wait_recv()

    def finish(self):
        for item in self.sends:
            item.wait_send()


def gather_scratch(levels, rows, width):
    return [pltpu.VMEM((rows, width), jnp.float32)] + [pltpu.SemaphoreType.DMA((levels - 1,))] * 2


FRONT_OUTS = 13


def front_kernel(size, gathering, *refs):
    block_in, gain, weight, taps, squeeze, expand, bias, gating, head_scale, project_out, *refs = refs
    wide, *refs = refs if gathering else [None] + refs
    outs, refs = refs[:FRONT_OUTS], refs[FRONT_OUTS:]
    normed, padded, filtered, activated, squeezed, logits, gate_in, running, scores = outs[:9]
    starts, state_end, mixed, branch = outs[9:]
    gated, *refs = refs
    landed, far_out, side_mine, side_far, *refs = refs if gathering else [None] * 4 + refs
    edge, edge_in, edge_send, edge_recv, pay, incoming, value, *refs = refs
    exchange = Exchange(size, False, pay, incoming, *refs[:7])
    stages = HeadSum(value, branch, *refs[7:13])
    refs = refs[13:]
    if gathering:
        line = LineGather(size // 2, landed, *refs[:3])
        share = ColumnShare(landed, far_out, side_mine, side_far, *refs[3:])
    s, h, z, y = place_of()
    following, preceding = ((s + 1) % size, h), ((s + size - 1) % size, h)
    greet([following, preceding, stages.near, stages.far] + exchange.partners)
    tokens = block_in.shape[0]
    keys = expand.shape[1]
    lags = taps.shape[0] - 1
    edge[...] = block_in[tokens - 16 : tokens].astype(jnp.float32)
    edge_copy = pltpu.make_async_remote_copy(
        src_ref=edge,
        dst_ref=edge_in,
        send_sem=edge_send,
        recv_sem=edge_recv,
        device_id=following,
        device_id_type=MESH,
    )
    edge_copy.start()
    if gathering:
        line.start(wide)

    def norm(values):
        return (values * rms_scale(values) * gain[...]).astype(jnp.bfloat16)

    def norm_rows(index, carry):
        rows = pl.ds(pl.multiple_of(index * GROUP, GROUP), GROUP)
        normed[rows] = norm(block_in[rows].astype(jnp.float32))
        return carry

    lax.fori_loop(0, tokens // GROUP, norm_rows, 0)
    padded[16 : 16 + tokens] = product(normed[...], weight[...])
    if gathering:
        line.start_rest()
    squeezed[...] = against(normed[...], squeeze[...]).astype(jnp.bfloat16)
    logits[...] = product(squeezed[...], expand[...]) + bias[...]
    edge_copy.wait_recv()
    before = product(norm(edge_in[...]), weight[...])
    padded[0:16] = jnp.where(s > 0, before, 0.0)
    mask = causal_mask(GROUP)
    root = keys ** (-0.5)
    count = tokens // GROUP
    carry = jnp.zeros(incoming.shape, jnp.float32)
    decay_sum = jnp.zeros((1, keys), jnp.float32)
    decays = []
    for group in range(count):
        base = group * GROUP
        rows = slice(base, base + GROUP)
        conv = taps[0:1] * padded[16 + base : 16 + base + GROUP]
        for lag in range(1, lags + 1):
            conv = conv + taps[lag : lag + 1] * padded[16 + base - lag : 16 + base - lag + GROUP]
        filtered[rows] = conv
        act = (conv * jax.nn.sigmoid(conv)).astype(jnp.bfloat16)
        activated[rows] = act
        act = act.astype(jnp.float32)
        query, key, val = act[:, :keys] * root, act[:, keys : 2 * keys], act[:, 2 * keys :]
        logit = logits[rows]
        log_decay = (jnp.minimum(logit, 0.0) - jnp.log1p(jnp.exp(-jnp.abs(logit)))) / NORMALIZER
        run = exact(mask, log_decay, ((1,), (0,)))
        running[rows] = run
        last = run[GROUP - 1 : GROUP]
        query_in, key_in, key_end = query * jnp.exp(run), key * jnp.exp(-run), key * jnp.exp(last - run)
        score = exact(query_in, key_in, ((1,), (1,))) * mask
        scores[rows] = score
        mixed[rows] = exact(score, val, ((1,), (0,)))
        starts[group] = carry
        carry = jnp.exp(last) * carry + exact(val, key_end, ((0,), (0,)))
        decays.append(decay_sum)
        decay_sum = decay_sum + last
    dim = carry.shape[0]
    pay[0:dim] = carry
    pay[dim : dim + 8] = jnp.broadcast_to(jnp.exp(decay_sum), (8, keys))
    exchange.start()
    if gathering:
        line.arrive(0)
        share.start_piece(0)
        line.arrive(SHARES - 1)
        share.start_piece(SHARES - 1)
    gate_in[...] = product(normed[...], gating[...])
    exchange.along()
    if gathering:
        for k in range(1, SHARES - 1):
            line.arrive(k)
            share.start_piece(k)
        share.copy(SHARES, share.mine, share.side_mine, share.near)
    exchange.join()
    exchange.finish()
    entered = incoming[...]
    state_end[...] = jnp.exp(decay_sum) * entered + pay[0:dim]
    for group in range(count):
        rows = slice(group * GROUP, (group + 1) * GROUP)
        start = starts[group] + jnp.exp(decays[group]) * entered
        starts[group] = start
        query_in = activated[rows, 0:keys].astype(jnp.float32) * root * jnp.exp(running[rows])
        total = mixed[rows] + exact(query_in, start, ((1,), (1,)))
        mixed[rows] = total
        gate = gate_in[rows]
        head = total * rms_scale(total) * head_scale[...]
        gated[rows] = (head * (gate * jax.nn.sigmoid(gate))).astype(jnp.bfloat16)
    value[...] = product(gated[...], project_out[...])
    stages.start()
    stages.across_chips()
    stages.hand_back()
    stages.finish()
    if gathering:
        share.finish()
        line.finish()
    edge_copy.wait_send()


def front(block_in, gain, weight, taps, squeeze, expand, bias, gating, head_scale, project_out, wide):
    size, heads = lax.axis_size("seq"), lax.axis_size("head")
    tokens, width = block_in.shape
    mixed_dim, keys, dim, rank = weight.shape[1], expand.shape[1], gating.shape[1], expand.shape[0]
    gathering = wide is not None
    operands = [block_in, gain, weight, taps, squeeze, expand, bias, gating, head_scale, project_out]
    operands += [wide] if gathering else []
    f32, b16 = jnp.float32, jnp.bfloat16
    shapes = [((tokens, width), b16), ((16 + tokens, mixed_dim), f32), ((tokens, mixed_dim), f32)]
    shapes += [((tokens, mixed_dim), b16), ((tokens, rank), b16), ((tokens, keys), f32)]
    shapes += [((tokens, dim), f32), ((tokens, keys), f32), ((tokens, GROUP), f32)]
    shapes += [((tokens // GROUP, dim, keys), f32), ((dim, keys), f32), ((tokens, dim), f32)]
    shapes += [((tokens, width), f32), ((tokens, dim), b16)]
    levels, share = size // 2, width // heads
    if gathering:
        shapes += [(((levels - 1) * tokens, share), f32)] * 4
    edge = pltpu.VMEM((16, width), f32)
    value = jax.ShapeDtypeStruct((tokens, width), f32)
    scratch = [edge, edge, pltpu.SemaphoreType.DMA, pltpu.SemaphoreType.DMA]
    scratch += [pltpu.VMEM((dim + 8, keys), f32), pltpu.VMEM((dim, keys), f32)]
    scratch += [pltpu.VMEM(value.shape, f32)]
    scratch += exchange_scratch(size, dim, keys) + head_scratch(value)
    if gathering:
        scratch += gather_scratch(levels, tokens, share) + share_scratch()
    return pl.pallas_call(
        functools.partial(front_kernel, size, gathering),
        out_shape=[jax.ShapeDtypeStruct(*x) for x in shapes],
        in_specs=[pl.BlockSpec(memory_space=pltpu.VMEM)] * len(operands),
        out_specs=[pl.BlockSpec(memory_space=pltpu.VMEM)] * len(shapes),
        scratch_shapes=scratch,
        compiler_params=pltpu.CompilerParams(
            collective_id=2, has_side_effects=True, vmem_limit_bytes=48 * 1024 * 1024
        ),
    )(*operands)


def grouped(array, seqs, count):
    return array.reshape((seqs, count, GROUP) + array.shape[2:])


def running_sums(array):
    rows = [array[:, 0]]
    for index in range(1, array.shape[1]):
        rows.append(rows[-1] + array[:, index])
    return jnp.stack(rows, axis=1)


def local_states(decays, updates, backward):
    count = updates.shape[1]
    carry = jnp.zeros_like(updates[:, 0])
    states = [None] * count
    for index in range(count):
        group = count - 1 - index if backward else index
        states[group] = carry
        carry = jnp.exp(decays[:, group])[:, None] * carry + updates[:, group]
    return (jnp.stack(states, axis=1), carry)


def body(
    block_in,
    upstream,
    first_gain,
    project_in,
    filter_taps,
    squeeze,
    expand,
    decay_bias,
    gating,
    head_scale,
    project_out,
    second_gain,
    hidden_gate,
    hidden_lift,
    hidden_drop,
):
    seqs, tokens, width = block_in.shape
    total_rows = seqs * tokens
    key_dim = expand.shape[1]
    value_dim = gating.shape[1]
    mixed_dim = project_in.shape[2]
    lags = filter_taps.shape[0] - 1
    count = tokens // GROUP
    taps = filter_taps.reshape(lags + 1, mixed_dim)
    weight_in = project_in.reshape(width, mixed_dim)
    size, hidden = lax.axis_size("seq"), hidden_gate.shape[1]
    gathering = size // 2 == SHARES + 1 and total_rows * width <= 512 * 1024
    seed = upstream.reshape(total_rows, width)
    residual_in = block_in.reshape(total_rows, width).astype(jnp.float32)
    scale_one = rms_scale(residual_in)
    (
        normed_one,
        padded,
        filtered,
        activated,
        squeezed,
        logits,
        gate_in,
        running,
        scores,
        starts,
        state_end,
        mixed,
        branch,
        gated,
        *seed_cols,
    ) = front(
        block_in.reshape(total_rows, width),
        first_gain[None],
        weight_in,
        taps,
        jnp.transpose(squeeze),
        expand,
        decay_bias[None],
        gating,
        head_scale[None],
        project_out,
        seed if gathering else None,
    )
    padded = padded[16 - lags :][None]
    projected = padded[:, lags:]
    filtered, state_end = filtered[None], state_end[None]
    activated = activated.astype(jnp.float32)[None]
    root = key_dim ** (-0.5)
    query = grouped(activated[..., :key_dim] * root, seqs, count)
    keys = grouped(activated[..., key_dim : 2 * key_dim], seqs, count)
    values = grouped(activated[..., 2 * key_dim :], seqs, count)
    mask = causal_mask(GROUP)
    running, starts = grouped(running[None], seqs, count), starts[None]
    last = running[:, :, -1]
    query_in = query * jnp.exp(running)
    key_in = keys * jnp.exp(-running)
    key_end = keys * jnp.exp(last[:, :, None] - running)
    scores = grouped(scores[None], seqs, count)
    decay_sum = jnp.sum(last, axis=1)
    decay_total = jnp.exp(decay_sum)
    scale_head = rms_scale(mixed)
    normed_head = mixed * scale_head * head_scale
    residual = residual_in + branch
    scale_two = rms_scale(residual)
    normed_two = (residual * scale_two * second_gain).astype(jnp.bfloat16)
    gate_value = product(normed_two, hidden_gate)
    lift_value = product(normed_two, hidden_lift)
    inner = (jax.nn.silu(gate_value) * lift_value).astype(jnp.bfloat16)
    partial_feed = product(inner, hidden_drop)
    grad_inner = against(seed, hidden_drop)
    grad_gv = (grad_inner * lift_value * silu_grad(gate_value)).astype(jnp.bfloat16)
    grad_lv = (grad_inner * jax.nn.silu(gate_value)).astype(jnp.bfloat16)
    grad_two, *normed_cols = head_sum(
        against(grad_gv, hidden_gate) + against(grad_lv, hidden_lift),
        4,
        normed_two if gathering else None,
    )
    grad_second = jnp.sum(grad_two * residual * scale_two, axis=0)
    grad_resid = seed.astype(jnp.float32) + rms_back(residual, scale_two, second_gain, grad_two)
    resid_low = grad_resid.astype(jnp.bfloat16)
    grad_output = across(resid_low, gated)
    grad_gated = against(resid_low, project_out)
    grad_gatein = (grad_gated * normed_head * silu_grad(gate_in)).astype(jnp.bfloat16)
    grad_normhead = grad_gated * jax.nn.silu(gate_in)
    grad_scale = jnp.sum(grad_normhead * mixed * scale_head, axis=0)
    grad_mixed_low = rms_back(mixed, scale_head, head_scale, grad_normhead).astype(jnp.bfloat16)
    grad_mixed = lax.optimization_barrier(grad_mixed_low).astype(jnp.float32)
    outgrad = grouped(grad_mixed.reshape(seqs, tokens, value_dim), seqs, count)
    query_end = jnp.einsum("snic,snid->sndc", query_in, outgrad, precision=HIGH)
    following_zero, back_total = local_states(last, query_end, True)
    after, *others = entering(decay_total[0], back_total[0], True, *normed_cols)
    normed_cols += others
    after = after[None]
    after_group = decay_sum[:, None] - running_sums(last)
    following = following_zero + jnp.exp(after_group)[:, :, None] * after[:, None]
    inner_group = jnp.einsum("snid,snjd->snij", outgrad, values, precision=HIGH) * mask
    grad_query = jnp.exp(running) * (
        jnp.einsum("snij,snjc->snic", inner_group, key_in, precision=HIGH)
        + jnp.einsum("snid,sndc->snic", outgrad, starts, precision=HIGH)
    )
    grad_keys = jnp.exp(-running) * jnp.einsum(
        "snij,snic->snjc", inner_group, query_in, precision=HIGH
    )
    grad_keys = grad_keys + jnp.exp(last[:, :, None] - running) * jnp.einsum(
        "snjd,sndc->snjc", values, following, precision=HIGH
    )
    grad_values = jnp.einsum("snij,snid->snjd", scores, outgrad, precision=HIGH)
    grad_values = grad_values + jnp.einsum("snjc,sndc->snjd", key_end, following, precision=HIGH)
    grad_running = (query * grad_query - keys * grad_keys).reshape(seqs, tokens, key_dim)
    beyond = jnp.sum(state_end * after, axis=1)
    upper = jnp.transpose(causal_mask(tokens))
    suffix = jnp.einsum("ij,sjc->sic", upper, grad_running, precision=HIGH)
    grad_log = suffix + beyond[:, None]
    grad_act = jnp.concatenate(
        [
            grad_query.reshape(seqs, tokens, key_dim) * root,
            grad_keys.reshape(seqs, tokens, key_dim),
            grad_values.reshape(seqs, tokens, value_dim),
        ],
        axis=-1,
    )
    grad_filtered = grad_act * silu_grad(filtered)
    later = shifted(grad_filtered[:, :lags], "seq", -1)
    padded_back = jnp.concatenate([grad_filtered, later], axis=1)
    grad_projected = taps[0] * grad_filtered
    tap_rows = [jnp.sum(grad_filtered * projected, axis=(0, 1))]
    for lag in range(1, lags + 1):
        grad_projected = grad_projected + taps[lag] * padded_back[:, lag : lag + tokens]
        tap_rows.append(
            jnp.sum(grad_filtered * padded[:, lags - lag : lags - lag + tokens], axis=(0, 1))
        )
    grad_taps = jnp.stack(tap_rows).reshape(lags + 1, 1, mixed_dim)
    grad_projected = grad_projected.reshape(total_rows, mixed_dim).astype(jnp.bfloat16)
    grad_logits = grad_log.reshape(total_rows, key_dim) * jax.nn.sigmoid(-logits) / NORMALIZER
    grad_bias = jnp.sum(grad_logits, axis=0)
    logits_low = grad_logits.astype(jnp.bfloat16)
    grad_expand = across(squeezed, logits_low)
    squeeze_low = against(logits_low, expand).astype(jnp.bfloat16)
    grad_squeeze = across(squeeze_low, normed_one)
    partials = [across(normed_one, grad_projected), across(normed_one, grad_gatein), grad_output]
    feed_pair = ()
    if gathering:
        feed_mine, feed_theirs = feed_gradients(
            normed_two,
            seed,
            normed_cols + seed_cols,
            jnp.transpose(hidden_gate),
            jnp.transpose(hidden_lift),
            hidden_drop,
        )
        pairs = [(s, s + 1 - 2 * (s % 2)) for s in range(size)]
        feed_pair = (feed_mine, lax.ppermute(feed_theirs, "seq", pairs))
    else:
        partials += [across(normed_two, grad_gv), across(normed_two, grad_lv), across(seed, inner)]
    partial_value = (
        against(grad_projected, weight_in)
        + against(grad_gatein, gating)
        + against(squeeze_low, squeeze)
    )
    partial_first = jnp.sum(partial_value * residual_in * scale_one, axis=0)
    grad_one, feed, packed = tail(
        partial_value,
        partial_feed,
        (grad_taps[:, 0], grad_expand, grad_bias[None], grad_second[None]),
        (grad_squeeze, partial_first[None], grad_scale[None]),
        partials,
    )
    done = finishing(
        block_in[0],
        first_gain[None],
        grad_one,
        grad_resid,
        residual,
        feed,
        packed,
        feed_pair,
        lags + 1,
        expand,
        head_scale,
        tuple(x.shape[1] for x in partials),
    )
    block_out, input_grad, sum_first, sum_second, sum_scale, sum_bias = done[:6]
    sum_taps, sum_expand, sum_squeeze = done[6:9]
    own_project, own_gating, own_output, own_gate, own_lift, own_drop = done[9:]
    if gathering:
        own_gate, own_lift = jnp.transpose(own_gate), jnp.transpose(own_lift)
    else:
        own_drop = jnp.transpose(own_drop)
    return (
        block_out[None],
        input_grad[None],
        sum_first[0],
        own_project,
        sum_taps,
        jnp.transpose(sum_squeeze),
        sum_expand,
        sum_bias[0],
        own_gating,
        sum_scale[0],
        own_output,
        sum_second[0],
        own_gate,
        own_lift,
        own_drop,
    )


def solution(mesh):
    in_specs = (
        P(None, "seq", None),
        P(None, "seq", None),
        P(),
        P(None, "head", None),
        P(None, "head", None),
        P(),
        P(None, "head"),
        P("head"),
        P(None, "head"),
        P(),
        P("head", None),
        P(),
        P(None, "head"),
        P(None, "head"),
        P("head", None),
    )
    out_specs = (
        P(None, "seq", None),
        P(None, "seq", None),
        P(),
        P("seq", "head", None),
        P(None, "head", None),
        P(),
        P(None, "head"),
        P("head"),
        P("seq", "head"),
        P(),
        P("head", "seq"),
        P(),
        P("seq", "head"),
        P("seq", "head"),
        P("head", "seq"),
    )
    return jax.shard_map(body, mesh=mesh, in_specs=in_specs, out_specs=out_specs, check_vma=False)
```

```python
import functools

import jax
import jax.numpy as jnp
from jax import lax
from jax.experimental import pallas as pl
from jax.experimental.pallas import tpu as pltpu
from jax.sharding import PartitionSpec as P

GROUP = 64


EPS = 1e-05
NORMALIZER = 16.0
HIGH = lax.Precision.HIGHEST


MESH = pl.DeviceIdType.MESH
PIECES = 4
SHARES = 3


def greet(devices):
    barrier = pltpu.get_barrier_semaphore()
    for device in devices:
        pl.semaphore_signal(barrier, inc=1, device_id=device, device_id_type=MESH)
    pl.semaphore_wait(barrier, len(devices))


def place_of():
    s, h = lax.axis_index("seq"), lax.axis_index("head")
    return s, h, s // 2, s % 2


def head_partners():
    s, h = lax.axis_index("seq"), lax.axis_index("head")
    core, chip = h % 2, h // 2
    return (s, chip * 2 + 1 - core), (s, (1 - chip) * 2 + core)


class HeadSum:
    def __init__(self, value, out, pair, summed, other, back, send_sem, recv_sem):
        self.value, self.out = value, out
        self.pair, self.summed, self.other, self.back = pair, summed, other, back
        self.send_sem, self.recv_sem = send_sem, recv_sem
        self.near, self.far = head_partners()
        core = lax.axis_index("head") % 2
        half = value.shape[0] // 2
        self.piece = half // PIECES
        self.mine = pl.multiple_of(core * half, half)
        self.theirs = pl.multiple_of((1 - core) * half, half)
        self.first, self.second, self.third = [], [], []

    def copy(self, stage, index, source, target, device):
        item = pltpu.make_async_remote_copy(
            src_ref=source,
            dst_ref=target.at[pl.ds(index * self.piece, self.piece)],
            send_sem=self.send_sem.at[stage, index],
            recv_sem=self.recv_sem.at[stage, index],
            device_id=device,
            device_id_type=MESH,
        )
        item.start()
        return item

    def start(self):
        for index in range(PIECES):
            source = self.value.at[pl.ds(self.theirs + index * self.piece, self.piece)]
            self.first.append(self.copy(0, index, source, self.pair, self.near))

    def across_chips(self):
        for index in range(PIECES):
            rows = pl.ds(index * self.piece, self.piece)
            self.first[index].wait_recv()
            self.summed[rows] = (
                self.value[pl.ds(self.mine + index * self.piece, self.piece)] + self.pair[rows]
            )
            self.second.append(self.copy(1, index, self.summed.at[rows], self.other, self.far))

    def hand_back(self):
        for index in range(PIECES):
            rows = pl.ds(index * self.piece, self.piece)
            self.second[index].wait_recv()
            total = pl.ds(self.mine + index * self.piece, self.piece)
            self.out[total] = self.summed[rows] + self.other[rows]
            self.third.append(self.copy(2, index, self.out.at[total], self.back, self.near))

    def finish(self):
        for index in range(PIECES):
            self.third[index].wait_recv()
            rows = pl.ds(self.theirs + index * self.piece, self.piece)
            self.out[rows] = self.back[pl.ds(index * self.piece, self.piece)]
        for item in self.first + self.second + self.third:
            item.wait_send()


def head_scratch(value):
    landing = pltpu.VMEM((value.shape[0] // 2, value.shape[1]), jnp.float32)
    return [landing] * 4 + [pltpu.SemaphoreType.DMA((3, PIECES))] * 2


class ColumnShare:
    def __init__(self, mine, far_out, side_mine, side_far, send_sem, recv_sem):
        self.mine, self.far_out, self.side_mine, self.side_far = mine, far_out, side_mine, side_far
        self.send_sem, self.recv_sem = send_sem, recv_sem
        self.near, self.far = head_partners()
        self.piece = mine.shape[0] // SHARES
        self.items = {}

    def copy(self, index, source, target, device):
        item = pltpu.make_async_remote_copy(
            src_ref=source,
            dst_ref=target,
            send_sem=self.send_sem.at[index],
            recv_sem=self.recv_sem.at[index],
            device_id=device,
            device_id_type=MESH,
        )
        item.start()
        self.items[index] = item

    def start_piece(self, k):
        take = pl.ds(k * self.piece, self.piece)
        self.copy(k, self.mine.at[take], self.far_out.at[take], self.far)

    def start(self):
        for k in range(SHARES):
            self.start_piece(k)
        self.copy(SHARES, self.mine, self.side_mine, self.near)

    def finish(self):
        for k in range(SHARES):
            take = pl.ds(k * self.piece, self.piece)
            self.items[k].wait_recv()
            self.copy(SHARES + 1 + k, self.far_out.at[take], self.side_far.at[take], self.near)
        for k in range(SHARES, 2 * SHARES + 1):
            self.items[k].wait_recv()
        for k in range(2 * SHARES + 1):
            self.items[k].wait_send()


def share_scratch():
    return [pltpu.SemaphoreType.DMA((2 * SHARES + 1,))] * 2


def sum_kernel(value, out, *scratch):
    stages = HeadSum(value, out, *scratch)
    greet((stages.near, stages.far))
    stages.start()
    stages.across_chips()
    stages.hand_back()
    stages.finish()


def head_sum(value):
    return pl.pallas_call(
        sum_kernel,
        out_shape=jax.ShapeDtypeStruct(value.shape, jnp.float32),
        in_specs=[pl.BlockSpec(memory_space=pltpu.VMEM)],
        out_specs=pl.BlockSpec(memory_space=pltpu.VMEM),
        scratch_shapes=head_scratch(value),
        compiler_params=pltpu.CompilerParams(
            collective_id=4, has_side_effects=True, vmem_limit_bytes=24 * 1024 * 1024
        ),
    )(value)


class Exchange:
    def __init__(self, size, backward, pay, out, near, pair, landed, part, other, send_sem, recv_sem):
        self.backward, self.pay, self.out = backward, pay, out
        self.near, self.pair, self.landed, self.part, self.other = near, pair, landed, part, other
        self.send_sem, self.recv_sem = send_sem, recv_sem
        s, h, self.z, self.y = place_of()
        self.levels = size // 2
        self.beside = (2 * self.z + 1 - self.y, h)
        self.peers = [
            (2 * ((self.z + k) % self.levels) + self.y, h) for k in range(1, self.levels)
        ]
        self.partners = [self.beside] + self.peers
        self.rows = out.shape[0]
        self.half = self.rows // 2
        self.mine = pl.multiple_of(self.y * self.half, self.half)
        self.theirs = pl.multiple_of((1 - self.y) * self.half, self.half)
        self.second = (self.y == 0) if backward else (self.y == 1)

    def copy(self, index, source, target, device):
        item = pltpu.make_async_remote_copy(
            src_ref=source,
            dst_ref=target,
            send_sem=self.send_sem.at[index],
            recv_sem=self.recv_sem.at[index],
            device_id=device,
            device_id_type=MESH,
        )
        item.start()
        return item

    def start(self):
        self.first = self.copy(0, self.pay, self.near, self.beside)

    def along(self):
        pay, near, rows, half = self.pay, self.near, self.rows, self.half
        self.first.wait_recv()
        my_decay, near_decay = pay[rows : rows + 1], near[rows : rows + 1]
        my_half, near_half = pay[pl.ds(self.mine, half)], near[pl.ds(self.mine, half)]
        self.pair[0:half] = jnp.where(
            self.second, my_decay * near_half + my_half, near_decay * my_half + near_half
        )
        self.pair[half : half + 8] = pay[rows : rows + 8] * near[rows : rows + 8]
        self.sends = [
            self.copy(k, self.pair, self.landed.at[k - 1], self.peers[k - 1])
            for k in range(1, self.levels)
        ]

    def join(self):
        half, levels, z = self.half, self.levels, self.z
        for item in self.sends:
            item.wait_recv()
        total = jnp.zeros((half, self.out.shape[1]), jnp.float32)
        for back in range(levels - 1, 0, -1):
            k = levels - back if self.backward else back
            valid = (z + back < levels) if self.backward else (z - back >= 0)
            longer = self.landed[k - 1, half : half + 1] * total + self.landed[k - 1, 0:half]
            total = jnp.where(valid, longer, total)
        self.part[...] = total
        self.last = self.copy(levels, self.part, self.other, self.beside)
        decay, near_half = self.near[self.rows : self.rows + 1], self.near[pl.ds(self.mine, half)]
        self.out[pl.ds(self.mine, half)] = jnp.where(self.second, decay * total + near_half, total)

    def finish(self):
        half = self.half
        self.last.wait_recv()
        rest, near_half = self.other[...], self.near[pl.ds(self.theirs, half)]
        decay = self.near[self.rows : self.rows + 1]
        self.out[pl.ds(self.theirs, half)] = jnp.where(self.second, decay * rest + near_half, rest)
        for item in [self.first, self.last] + self.sends:
            item.wait_send()


def exchange_scratch(size, rows, lanes):
    half, levels = rows // 2, size // 2
    return [
        pltpu.VMEM((rows + 8, lanes), jnp.float32),
        pltpu.VMEM((half + 8, lanes), jnp.float32),
        pltpu.VMEM((levels - 1, half + 8, lanes), jnp.float32),
        pltpu.VMEM((half, lanes), jnp.float32),
        pltpu.VMEM((half, lanes), jnp.float32),
    ] + [pltpu.SemaphoreType.DMA((levels + 1,))] * 2


def exchange_kernel(size, pay, out, *scratch):
    exchange = Exchange(size, True, pay, out, *scratch)
    greet(exchange.partners)
    exchange.start()
    exchange.along()
    exchange.join()
    exchange.finish()


def entering(decay, state):
    size = lax.axis_size("seq")
    rows, lanes = state.shape
    pay = jnp.concatenate([state, jnp.broadcast_to(decay[None], (8, lanes))], axis=0)
    return pl.pallas_call(
        functools.partial(exchange_kernel, size),
        out_shape=jax.ShapeDtypeStruct(state.shape, jnp.float32),
        in_specs=[pl.BlockSpec(memory_space=pltpu.VMEM)],
        out_specs=pl.BlockSpec(memory_space=pltpu.VMEM),
        scratch_shapes=exchange_scratch(size, rows, lanes),
        compiler_params=pltpu.CompilerParams(
            collective_id=3, has_side_effects=True, vmem_limit_bytes=16 * 1024 * 1024
        ),
    )(pay)


def tail_kernel(size, heads, arrays, *refs):
    value, feed, taps, expand, bias, second, squeeze, first, scale, *refs = refs
    ins, (value_out, feed_out, packed, *scratch) = refs[:arrays], refs[arrays:]
    own, shared, own_in, shared_in = scratch[:4]
    slots, scratch = scratch[4 : 4 + arrays], scratch[4 + arrays :]
    own_send, own_recv, shared_send, shared_recv, send_sem, recv_sem, *head_refs = scratch
    stages = HeadSum(value, value_out, *head_refs[:6])
    feeding = HeadSum(feed, feed_out, *head_refs[6:])
    half = size // 2
    me = lax.axis_index("seq")
    mine_head = lax.axis_index("head")
    low, high = me % 2, me // 2
    place = high + low * (2 * half - 1 - 2 * high)

    def member(position):
        position = (position + 2 * size) % size
        side = position // half
        return 2 * (position + side * (2 * half - 1 - 2 * position)) + side

    partners = ((member(place + 1), mine_head), (member(place - 1), mine_head))
    seq_bits, head_bits = size.bit_length() - 1, heads.bit_length() - 1
    small_peers = []
    for bit in range(seq_bits):
        step = 1 << bit
        small_peers.append((me + step - 2 * step * ((me // step) % 2), mine_head))
    small_peers += [stages.near, stages.far]
    greet(list(partners) + small_peers)

    rows = ins[0].shape[0] // size
    part = rows // 2

    def block(array, direction, position):
        start = pl.multiple_of(member(position) * rows + direction * part, part)
        return ins[array].at[pl.ds(start, part)]

    def copy(array, direction, step, source):
        return pltpu.make_async_remote_copy(
            src_ref=source,
            dst_ref=slots[array].at[direction, step],
            send_sem=send_sem.at[array, direction, step],
            recv_sem=recv_sem.at[array, direction, step],
            device_id=partners[direction],
            device_id_type=MESH,
        )

    stages.start()
    for array in range(arrays):
        for direction, sign in ((0, 1), (1, -1)):
            copy(array, direction, 0, block(array, direction, place - sign)).start()

    width, keys = squeeze.shape[1], expand.shape[1]
    mixed, lags, rank = taps.shape[1], taps.shape[0], expand.shape[0]
    own[0, 0:lags] = taps[...]
    for index in range(width // mixed):
        own[0, 8 + index : 9 + index] = second[:, index * mixed : (index + 1) * mixed]
    for index in range(rank // 8):
        own[0, 16:24, index * keys : (index + 1) * keys] = expand[index * 8 : (index + 1) * 8]
    own[0, 24:25, 0:keys] = bias[...]
    shared[0, 0:rank] = squeeze[...]
    shared[0, rank : rank + 1] = first[...]
    shared[0, rank + 1 : rank + 2, 0 : scale.shape[1]] = scale[...]

    def small_copy(buffer, landing, send, recv, index):
        return pltpu.make_async_remote_copy(
            src_ref=buffer.at[index],
            dst_ref=landing.at[index],
            send_sem=send.at[index],
            recv_sem=recv.at[index],
            device_id=small_peers[index],
            device_id_type=MESH,
        )

    own_copies = [small_copy(own, own_in, own_send, own_recv, k) for k in range(seq_bits)]
    shared_copies = [
        small_copy(shared, shared_in, shared_send, shared_recv, k)
        for k in range(seq_bits + head_bits)
    ]

    def small_step(index):
        if index > 0 and index <= seq_bits:
            own_copies[index - 1].wait_recv()
            own[index] = own[index - 1] + own_in[index - 1]
        if index > 0:
            shared_copies[index - 1].wait_recv()
            shared[index] = shared[index - 1] + shared_in[index - 1]
        if index < seq_bits:
            own_copies[index].start()
        if index < seq_bits + head_bits:
            shared_copies[index].start()

    def lap(step, carry):
        for array in range(arrays):
            for direction, sign in ((0, 1), (1, -1)):
                slot = slots[array].at[direction, step - 1]
                copy(array, direction, step - 1, slot).wait_recv()
                local = block(array, direction, place - sign * (step + 1))
                slot[...] = slot[...] + local[...]
                copy(array, direction, step, slot).start()
        return carry

    small_step(0)
    stages.across_chips()
    feeding.start()
    lap(1, 0)
    small_step(1)
    feeding.across_chips()
    lap(2, 0)
    small_step(2)
    stages.hand_back()
    lap(3, 0)
    small_step(3)
    lap(4, 0)
    small_step(4)
    feeding.hand_back()
    lax.fori_loop(5, size - 1, lap, 0)
    for index in range(5, seq_bits + head_bits + 1):
        small_step(index)
    stages.finish()
    feeding.finish()
    base = rows
    packed[base : base + 32, 0:mixed] = own[seq_bits]
    base += 32
    packed[base : base + shared.shape[1], 0:width] = shared[seq_bits + head_bits]
    column = 0
    for array in range(arrays):
        across_columns = slice(column, column + ins[array].shape[1])
        column += -(-ins[array].shape[1] // 128) * 128
        for direction in range(2):
            slot = slots[array].at[direction, size - 2]
            copy(array, direction, size - 2, slot).wait_recv()
            local = block(array, direction, place)
            packed[direction * part : (direction + 1) * part, across_columns] = slot[...] + local[...]

    def finish(step, carry):
        for array in range(arrays):
            for direction in range(2):
                copy(array, direction, step, slots[array].at[direction, step]).wait_send()
        return carry

    lax.fori_loop(0, size - 1, finish, 0)
    for item in own_copies + shared_copies:
        item.wait_send()


def tail(value, feed, own, shared, partials):
    size, heads = lax.axis_size("seq"), lax.axis_size("head")
    arrays = len(partials)
    rows = partials[0].shape[0] // size
    seq_bits, all_bits = size.bit_length() - 1, size.bit_length() + heads.bit_length() - 2
    squeeze = shared[0]
    own_shape = (32, own[0].shape[1])
    shared_shape = (squeeze.shape[0] + 8, squeeze.shape[1])
    wide = sum(-(-x.shape[1] // 128) * 128 for x in partials)
    shapes = [value.shape, feed.shape, (rows + own_shape[0] + shared_shape[0], wide)]
    operands = [value, feed, *own, *shared, *partials]
    return pl.pallas_call(
        functools.partial(tail_kernel, size, heads, arrays),
        out_shape=[jax.ShapeDtypeStruct(x, jnp.float32) for x in shapes],
        in_specs=[pl.BlockSpec(memory_space=pltpu.VMEM)] * len(operands),
        out_specs=[pl.BlockSpec(memory_space=pltpu.VMEM)] * len(shapes),
        scratch_shapes=[
            pltpu.VMEM((seq_bits + 1,) + own_shape, jnp.float32),
            pltpu.VMEM((all_bits + 1,) + shared_shape, jnp.float32),
            pltpu.VMEM((seq_bits,) + own_shape, jnp.float32),
            pltpu.VMEM((all_bits,) + shared_shape, jnp.float32),
        ]
        + [pltpu.VMEM((2, size - 1, rows // 2, x.shape[1]), jnp.float32) for x in partials]
        + [pltpu.SemaphoreType.DMA((seq_bits,))] * 2
        + [pltpu.SemaphoreType.DMA((all_bits,))] * 2
        + [pltpu.SemaphoreType.DMA((arrays, 2, size - 1))] * 2
        + head_scratch(value) * 2,
        compiler_params=pltpu.CompilerParams(
            collective_id=0, has_side_effects=True, vmem_limit_bytes=60 * 1024 * 1024
        ),
    )(*operands)


def finish_kernel(gathering, widths, *refs):
    block_in, gain, grad_one, grad_resid, residual, feed, packed, *refs = refs
    feed_mine, feed_more, *refs = refs if gathering else [None, None] + refs
    block_out, input_grad, first, second, scale, bias, taps, expand, squeeze, *outs = refs

    def step(index, carry):
        rows = pl.ds(pl.multiple_of(index * 64, 64), 64)
        values = block_in[rows].astype(jnp.float32)
        back = rms_back(values, rms_scale(values), gain[...], grad_one[rows])
        input_grad[rows] = grad_resid[rows] + back
        block_out[rows] = (residual[rows] + feed[rows]).astype(jnp.bfloat16)
        return carry

    lax.fori_loop(0, block_in.shape[0] // 64, step, 0)
    rows, width = outs[0].shape[0], block_in.shape[1]
    mixed, lags = taps.shape[2], taps.shape[0]
    rank, keys = expand.shape
    base = rows
    taps[:, 0] = packed[base : base + lags, 0:mixed]
    for index in range(width // mixed):
        second[:, index * mixed : (index + 1) * mixed] = packed[base + 8 + index : base + 9 + index, 0:mixed]
    for index in range(rank // 8):
        expand[index * 8 : (index + 1) * 8] = packed[base + 16 : base + 24, index * keys : (index + 1) * keys]
    bias[...] = packed[base + 24 : base + 25, 0:keys]
    base += 32
    squeeze[...] = packed[base : base + rank, 0:width]
    first[...] = packed[base + rank : base + rank + 1, 0:width]
    scale[...] = packed[base + rank + 1 : base + rank + 2, 0 : scale.shape[1]]
    column = 0
    for index, size in enumerate(widths):
        part = packed[0:rows, column : column + size]
        column += -(-size // 128) * 128
        if index == 0:
            outs[index][:, 0] = part
        else:
            outs[index][...] = jnp.transpose(part) if index == 2 else part
    if gathering:
        for index in range(3):
            outs[len(widths) + index][...] = feed_mine[index] + feed_more[index]


def finishing(block_in, gain, grad_one, grad_resid, residual, feed, packed, feed_pair, lags, expand, scale, widths):
    gathering = len(feed_pair) > 0
    operands = [block_in, gain, grad_one, grad_resid, residual, feed, packed, *feed_pair]
    width = block_in.shape[1]
    rank, keys = expand.shape
    rows = width // lax.axis_size("seq")
    shapes = [grad_one.shape, (1, width), (1, width), (1, scale.shape[0]), (1, keys)]
    shapes += [(lags, 1, widths[0]), expand.shape, (rank, width)]
    shapes += [(rows, 1, widths[0]), (rows, widths[1]), (widths[2], rows)]
    shapes += [(rows, x) for x in widths[3:]]
    if gathering:
        shapes += [feed_pair[0].shape[1:]] * 3
    shapes = [jax.ShapeDtypeStruct(x, jnp.float32) for x in shapes]
    return pl.pallas_call(
        functools.partial(finish_kernel, gathering, widths),
        out_shape=[jax.ShapeDtypeStruct(block_in.shape, jnp.bfloat16)] + shapes,
        in_specs=[pl.BlockSpec(memory_space=pltpu.VMEM)] * len(operands),
        compiler_params=pltpu.CompilerParams(vmem_limit_bytes=40 * 1024 * 1024),
    )(*operands)


def shifted(x, axis, by):
    size = lax.axis_size(axis)
    pairs = [(i, i + by) for i in range(size) if 0 <= i + by < size]
    return lax.ppermute(x, axis, pairs)


def product(left, right):
    return jnp.dot(left, right, preferred_element_type=jnp.float32)


def against(left, right):
    return lax.dot_general(
        left, right, (((1,), (1,)), ((), ())), preferred_element_type=jnp.float32
    )


def across(left, right):
    return lax.dot_general(
        left, right, (((0,), (0,)), ((), ())), preferred_element_type=jnp.float32
    )


def rms_scale(values):
    return lax.rsqrt(jnp.mean(values * values, axis=-1, keepdims=True) + EPS)


def rms_back(values, scale, gain, incoming):
    weighted = gain * incoming
    cube = scale * scale * scale
    return scale * weighted - values * cube * jnp.mean(values * weighted, axis=-1, keepdims=True)


def silu_grad(values):
    logistic = jax.nn.sigmoid(values)
    return logistic * (1.0 + values * (1.0 - logistic))


def causal_mask(size):
    rows = lax.broadcasted_iota(jnp.int32, (size, size), 0)
    columns = lax.broadcasted_iota(jnp.int32, (size, size), 1)
    return (columns <= rows).astype(jnp.float32)


def exact(left, right, contract):
    return lax.dot_general(
        left, right, (contract, ((), ())), precision=HIGH, preferred_element_type=jnp.float32
    )


class LineGather:
    def __init__(self, levels, landed, source, send_sem, recv_sem):
        self.levels, self.landed, self.source = levels, landed, source
        self.send_sem, self.recv_sem = send_sem, recv_sem
        s, h, z, y = place_of()
        self.peers = [(2 * ((z + k) % levels) + y, h) for k in range(1, levels)]

    def start(self, wide, part):
        rows, width = self.source.shape
        columns = pl.ds(pl.multiple_of(part * width, width), width)
        self.source[...] = wide[:, columns].astype(jnp.float32)
        self.sends = [
            pltpu.make_async_remote_copy(
                src_ref=self.source,
                dst_ref=self.landed.at[pl.ds(k * rows, rows)],
                send_sem=self.send_sem.at[k],
                recv_sem=self.recv_sem.at[k],
                device_id=self.peers[k],
                device_id_type=MESH,
            )
            for k in range(self.levels - 1)
        ]
        self.sends[0].start()
        self.sends[-1].start()

    def start_rest(self):
        for item in self.sends[1:-1]:
            item.start()

    def arrive(self, k):
        self.sends[k].wait_recv()

    def finish(self):
        for item in self.sends:
            item.wait_send()


def gather_scratch(levels, rows, width):
    return [pltpu.VMEM((rows, width), jnp.float32)] + [pltpu.SemaphoreType.DMA((levels - 1,))] * 2


FRONT_OUTS = 13


def front_kernel(size, gathering, *refs):
    loads, held, between = load_all(refs, 11 if gathering else 10)
    for item in loads[:1] + loads[10:] + loads[1:10]:
        item.start()
    refs = held + between
    block_in, gain, weight, taps, squeeze, expand, bias, gating, head_scale, project_out, *refs = refs
    wide, *refs = refs if gathering else [None] + refs
    outs, refs = refs[:FRONT_OUTS], refs[FRONT_OUTS:]
    normed, padded, filtered, activated, squeezed, logits, gate_in, running, scores = outs[:9]
    starts, state_end, mixed, branch = outs[9:]
    gated, *refs = refs
    seed_all, *refs = refs if gathering else [None] + refs
    edge, edge_in, edge_send, edge_recv, pay, incoming, value, *refs = refs
    exchange = Exchange(size, False, pay, incoming, *refs[:7])
    stages = HeadSum(value, branch, *refs[7:13])
    refs = refs[13:]
    if gathering:
        landed, far_out, side_mine, side_far, *refs = refs
        line = LineGather(size // 2, landed, *refs[:3])
        share = ColumnShare(landed, far_out, side_mine, side_far, *refs[3:])
    s, h, z, y = place_of()
    following, preceding = ((s + 1) % size, h), ((s + size - 1) % size, h)
    greet([following, preceding, stages.near, stages.far] + exchange.partners)
    tokens = block_in.shape[0]
    keys = expand.shape[1]
    lags = taps.shape[0] - 1
    for item in loads[:2] + loads[10:]:
        item.wait()
    edge[...] = block_in[tokens - 16 : tokens].astype(jnp.float32)
    edge_copy = pltpu.make_async_remote_copy(
        src_ref=edge,
        dst_ref=edge_in,
        send_sem=edge_send,
        recv_sem=edge_recv,
        device_id=following,
        device_id_type=MESH,
    )
    edge_copy.start()
    if gathering:
        line.start(wide, h)

    def norm(values):
        return (values * rms_scale(values) * gain[...]).astype(jnp.bfloat16)

    def norm_rows(index, carry):
        rows = pl.ds(pl.multiple_of(index * GROUP, GROUP), GROUP)
        normed[rows] = norm(block_in[rows].astype(jnp.float32))
        return carry

    lax.fori_loop(0, tokens // GROUP, norm_rows, 0)
    for item in loads[2:10]:
        item.wait()
    padded[16 : 16 + tokens] = product(normed[...], weight[...])
    squeezed[...] = against(normed[...], squeeze[...]).astype(jnp.bfloat16)
    logits[...] = product(squeezed[...], expand[...]) + bias[...]
    edge_copy.wait_recv()
    before = product(norm(edge_in[...]), weight[...])
    padded[0:16] = jnp.where(s > 0, before, 0.0)
    mask = causal_mask(GROUP)
    root = keys ** (-0.5)
    count = tokens // GROUP
    carry = jnp.zeros(incoming.shape, jnp.float32)
    decay_sum = jnp.zeros((1, keys), jnp.float32)
    decays = []
    for group in range(count):
        base = group * GROUP
        rows = slice(base, base + GROUP)
        conv = taps[0:1] * padded[16 + base : 16 + base + GROUP]
        for lag in range(1, lags + 1):
            conv = conv + taps[lag : lag + 1] * padded[16 + base - lag : 16 + base - lag + GROUP]
        filtered[rows] = conv
        act = (conv * jax.nn.sigmoid(conv)).astype(jnp.bfloat16)
        activated[rows] = act
        act = act.astype(jnp.float32)
        query, key, val = act[:, :keys] * root, act[:, keys : 2 * keys], act[:, 2 * keys :]
        logit = logits[rows]
        log_decay = (jnp.minimum(logit, 0.0) - jnp.log1p(jnp.exp(-jnp.abs(logit)))) / NORMALIZER
        run = exact(mask, log_decay, ((1,), (0,)))
        running[rows] = run
        last = run[GROUP - 1 : GROUP]
        query_in, key_in, key_end = query * jnp.exp(run), key * jnp.exp(-run), key * jnp.exp(last - run)
        score = exact(query_in, key_in, ((1,), (1,))) * mask
        scores[rows] = score
        mixed[rows] = exact(score, val, ((1,), (0,)))
        starts[group] = carry
        carry = jnp.exp(last) * carry + exact(val, key_end, ((0,), (0,)))
        decays.append(decay_sum)
        decay_sum = decay_sum + last
    dim = carry.shape[0]
    pay[0:dim] = carry
    pay[dim : dim + 8] = jnp.broadcast_to(jnp.exp(decay_sum), (8, keys))
    exchange.start()
    if gathering:
        for k in (0, SHARES - 1):
            line.arrive(k)
            share.start_piece(k)
    gate_in[...] = product(normed[...], gating[...])
    exchange.along()
    exchange.join()
    if gathering:
        line.start_rest()
    exchange.finish()
    entered = incoming[...]
    state_end[...] = jnp.exp(decay_sum) * entered + pay[0:dim]
    for group in range(count):
        rows = slice(group * GROUP, (group + 1) * GROUP)
        start = starts[group] + jnp.exp(decays[group]) * entered
        starts[group] = start
        query_in = activated[rows, 0:keys].astype(jnp.float32) * root * jnp.exp(running[rows])
        total = mixed[rows] + exact(query_in, start, ((1,), (1,)))
        mixed[rows] = total
        gate = gate_in[rows]
        head = total * rms_scale(total) * head_scale[...]
        gated[rows] = (head * (gate * jax.nn.sigmoid(gate))).astype(jnp.bfloat16)
    value[...] = product(gated[...], project_out[...])
    stages.start()
    stages.across_chips()
    if gathering:
        for k in range(1, SHARES - 1):
            line.arrive(k)
            share.start_piece(k)
        share.copy(SHARES, share.mine, share.side_mine, share.near)
    stages.hand_back()
    stages.finish()
    if gathering:
        share.finish()
        line.finish()
        seed_all[0:tokens] = wide[...]
        collect(seed_all, tokens, h, landed, far_out, side_mine, side_far)
    edge_copy.wait_send()


def collect(target, first, h, mine, far, side_mine, side_far):
    beside = h + 1 - 2 * (h % 2)
    rows, held = mine.shape
    for quarter, source in (
        (h, mine),
        ((h + 2) % 4, far),
        (beside, side_mine),
        ((beside + 2) % 4, side_far),
    ):
        columns = pl.ds(pl.multiple_of(quarter * held, held), held)
        target[first : first + rows, columns] = source[...].astype(jnp.bfloat16)


def load_all(refs, count):
    operands, between = refs[:count], refs[count : -count - 1]
    held, sem = refs[-count - 1 : -1], refs[-1]
    loads = [pltpu.make_async_copy(operands[i], held[i], sem.at[i]) for i in range(count)]
    return loads, list(held), list(between)


def load_scratch(operands):
    return [pltpu.VMEM(x.shape, x.dtype) for x in operands] + [
        pltpu.SemaphoreType.DMA((len(operands),))
    ]


def front(block_in, gain, weight, taps, squeeze, expand, bias, gating, head_scale, project_out, wide):
    size, heads = lax.axis_size("seq"), lax.axis_size("head")
    tokens, width = block_in.shape
    mixed_dim, keys, dim, rank = weight.shape[1], expand.shape[1], gating.shape[1], expand.shape[0]
    gathering = wide is not None
    operands = [block_in, gain, weight, taps, squeeze, expand, bias, gating, head_scale, project_out]
    operands += [wide] if gathering else []
    f32, b16 = jnp.float32, jnp.bfloat16
    shapes = [((tokens, width), b16), ((16 + tokens, mixed_dim), f32), ((tokens, mixed_dim), f32)]
    shapes += [((tokens, mixed_dim), b16), ((tokens, rank), b16), ((tokens, keys), f32)]
    shapes += [((tokens, dim), f32), ((tokens, keys), f32), ((tokens, GROUP), f32)]
    shapes += [((tokens // GROUP, dim, keys), f32), ((dim, keys), f32), ((tokens, dim), f32)]
    shapes += [((tokens, width), f32), ((tokens, dim), b16)]
    levels, share = size // 2, width // heads
    if gathering:
        shapes += [((levels * tokens, width), b16)]
    edge = pltpu.VMEM((16, width), f32)
    value = jax.ShapeDtypeStruct((tokens, width), f32)
    scratch = [edge, edge, pltpu.SemaphoreType.DMA, pltpu.SemaphoreType.DMA]
    scratch += [pltpu.VMEM((dim + 8, keys), f32), pltpu.VMEM((dim, keys), f32)]
    scratch += [pltpu.VMEM(value.shape, f32)]
    scratch += exchange_scratch(size, dim, keys) + head_scratch(value)
    if gathering:
        scratch += [pltpu.VMEM(((levels - 1) * tokens, share), f32)] * 4
        scratch += gather_scratch(levels, tokens, share) + share_scratch()
    scratch += load_scratch(operands)
    return pl.pallas_call(
        functools.partial(front_kernel, size, gathering),
        out_shape=[jax.ShapeDtypeStruct(*x) for x in shapes],
        in_specs=[pl.BlockSpec(memory_space=pl.ANY)] * len(operands),
        out_specs=[pl.BlockSpec(memory_space=pltpu.VMEM)] * len(shapes),
        scratch_shapes=scratch,
        compiler_params=pltpu.CompilerParams(
            collective_id=2, has_side_effects=True, vmem_limit_bytes=60 * 1024 * 1024
        ),
    )(*operands)


def grouped(array, seqs, count):
    return array.reshape((seqs, count, GROUP) + array.shape[2:])


def running_sums(array):
    rows = [array[:, 0]]
    for index in range(1, array.shape[1]):
        rows.append(rows[-1] + array[:, index])
    return jnp.stack(rows, axis=1)


class Ring:
    def __init__(self, size, ins, slots, send_sem, recv_sem):
        self.size, self.ins, self.slots = size, ins, slots
        self.send_sem, self.recv_sem = send_sem, recv_sem
        self.half = size // 2
        me, h = lax.axis_index("seq"), lax.axis_index("head")
        low, high = me % 2, me // 2
        self.place = high + low * (2 * self.half - 1 - 2 * high)
        self.partners = ((self.member(self.place + 1), h), (self.member(self.place - 1), h))
        self.rows = ins[0].shape[0] // size
        self.part = self.rows // 2

    def member(self, position):
        position = (position + 2 * self.size) % self.size
        side = position // self.half
        return 2 * (position + side * (2 * self.half - 1 - 2 * position)) + side

    def block(self, array, direction, position):
        start = self.member(position) * self.rows + direction * self.part
        return self.ins[array].at[pl.ds(pl.multiple_of(start, self.part), self.part)]

    def copy(self, array, direction, step, source):
        return pltpu.make_async_remote_copy(
            src_ref=source,
            dst_ref=self.slots[array].at[direction, step],
            send_sem=self.send_sem.at[array, direction, step],
            recv_sem=self.recv_sem.at[array, direction, step],
            device_id=self.partners[direction],
            device_id_type=MESH,
        )

    def start(self, array):
        for direction, sign in ((0, 1), (1, -1)):
            self.copy(array, direction, 0, self.block(array, direction, self.place - sign)).start()

    def lap(self, array, step):
        for direction, sign in ((0, 1), (1, -1)):
            slot = self.slots[array].at[direction, step - 1]
            self.copy(array, direction, step - 1, slot).wait_recv()
            local = self.block(array, direction, self.place - sign * (step + 1))
            slot[...] = slot[...] + local[...]
            self.copy(array, direction, step, slot).start()

    def last(self, array, packed, columns):
        for direction in range(2):
            slot = self.slots[array].at[direction, self.size - 2]
            self.copy(array, direction, self.size - 2, slot).wait_recv()
            local = self.block(array, direction, self.place)
            rows = slice(direction * self.part, (direction + 1) * self.part)
            packed[rows, columns] = slot[...] + local[...]

    def finish(self):
        for array in range(len(self.ins)):
            for direction in range(2):
                for step in range(self.size - 1):
                    slot = self.slots[array].at[direction, step]
                    self.copy(array, direction, step, slot).wait_send()


OPERANDS = 29


def back_kernel(size, heads, *refs):
    loads, held, between = load_all(refs, OPERANDS)
    early, next_loads = [12, 15, 18], [16, 26, 27, 28]
    others = [i for i in range(OPERANDS) if i not in early + next_loads]
    for i in early + next_loads + others:
        loads[i].start()
    refs = held + between
    normed, padded, filtered, activated, squeezed, logits, gate_in, running, scores, *refs = refs
    starts, state_end, mixed, branch, gated, u_all, *refs = refs
    block_in, seed, first_gain, second_gain, weight, taps, squeeze, expand, gating, *refs = refs
    head_scale, project_out, gate, lift, drop, *refs = refs
    block_out, input_grad, packed, feed_sum, *refs = refs
    residual, normed_two, grad_resid, resid_low, value, feed, grad_two, grad_one, *refs = refs
    feed_out, gatein, mixed_low, act_grad, filtered_grad, edge_in, following, projected_low, *refs = refs
    logits_low, pay, after, n_all, gv_all, lv_all, inner_all, both, *refs = refs
    theirs, theirs_in, landed, far_out, side_mine, side_far, *refs = refs
    own, shared, own_in, shared_in, part_project, part_gating, part_output, *refs = refs
    slots, refs = refs[:3], refs[3:]
    ring_send, ring_recv, own_send, own_recv, shared_send, shared_recv, *refs = refs
    edge_send, edge_recv, pair_send, pair_recv, *refs = refs
    exchange = Exchange(size, True, pay, after, *refs[:7])
    stages = HeadSum(value, grad_two, *refs[7:13])
    feeding = HeadSum(feed, feed_out, *refs[13:19])
    ending = HeadSum(value, grad_one, *refs[19:25])
    line = LineGather(size // 2, landed, *refs[25:28])
    share = ColumnShare(landed, far_out, side_mine, side_far, *refs[28:30])
    ring = Ring(size, (part_project, part_gating, part_output), slots, ring_send, ring_recv)
    levels = size // 2
    s, h, z, y = place_of()
    near, far = stages.near, stages.far
    preceding, later = ((s + size - 1) % size, h), ((s + 1) % size, h)
    seq_bits, head_bits = size.bit_length() - 1, heads.bit_length() - 1
    small_peers = []
    for bit in range(seq_bits):
        step = 1 << bit
        small_peers.append((s + step - 2 * step * ((s // step) % 2), h))
    small_peers += [near, far]
    greet([preceding, later] + exchange.partners + list(ring.partners) + small_peers)

    tokens, width = block_in.shape
    hidden, keys, dim = drop.shape[0], expand.shape[1], gating.shape[1]
    rank, qkv, lags = expand.shape[0], taps.shape[1], taps.shape[0] - 1
    count = tokens // GROUP
    root = keys ** (-0.5)

    def rows_loop(step, carry, block=GROUP):
        def at(index, carry):
            return step(pl.ds(pl.multiple_of(index * block, block), block), carry)

        return lax.fori_loop(0, tokens // block, at, carry)

    def norm_two(rows, carry):
        values = block_in[rows].astype(jnp.float32) + branch[rows]
        residual[rows] = values
        normed_two[rows] = (values * rms_scale(values) * second_gain[...]).astype(jnp.bfloat16)
        return carry

    for i in early:
        loads[i].wait()
    rows_loop(norm_two, 0)
    line.start(normed_two, h)
    line.start_rest()

    def hidden_units(n, u_grad, rows):
        gate_value = against(n, gate[...])
        lift_value = against(n, lift[...])
        logistic = jax.nn.sigmoid(gate_value)
        silu = gate_value * logistic
        slope = logistic * (1.0 + gate_value * (1.0 - logistic))
        gv_all[rows] = (u_grad * lift_value * slope).astype(jnp.bfloat16)
        lv_all[rows] = (u_grad * silu).astype(jnp.bfloat16)
        inner_all[rows] = (silu * lift_value).astype(jnp.bfloat16)

    def feed_rows(rows, carry):
        hidden_units(normed_two[rows], against(seed[rows], drop[...]), rows)
        value[rows] = product(gv_all[rows], gate[...]) + product(lv_all[rows], lift[...])
        return carry

    for i in next_loads:
        loads[i].wait()
    rows_loop(feed_rows, 0, 128)
    stages.start()
    for i in others:
        loads[i].wait()
    stages.across_chips()
    feed[...] = product(inner_all[0:tokens], drop[...])
    n_all[0:tokens] = normed_two[...]
    stages.hand_back()
    stages.finish()

    def resid_rows(rows, total):
        incoming, values = grad_two[rows], residual[rows]
        scale = rms_scale(values)
        grad = seed[rows].astype(jnp.float32) + rms_back(values, scale, second_gain[...], incoming)
        grad_resid[rows] = grad
        resid_low[rows] = grad.astype(jnp.bfloat16)
        return total + jnp.sum(incoming * values * scale, axis=0, keepdims=True)

    grad_second = rows_loop(resid_rows, jnp.zeros((1, width), jnp.float32))

    def head_rows(rows, total):
        grad_gated = against(resid_low[rows], project_out[...])
        values, gates = mixed[rows], gate_in[rows]
        scale = rms_scale(values)
        logistic = jax.nn.sigmoid(gates)
        slope = logistic * (1.0 + gates * (1.0 - logistic))
        gatein[rows] = (grad_gated * (values * scale * head_scale[...]) * slope).astype(jnp.bfloat16)
        grad_norm = grad_gated * (gates * logistic)
        grad = rms_back(values, scale, head_scale[...], grad_norm)
        mixed_low[rows] = grad.astype(jnp.bfloat16).astype(jnp.float32)
        return total + jnp.sum(grad_norm * values * scale, axis=0, keepdims=True)

    grad_scale = rows_loop(head_rows, jnp.zeros((1, dim), jnp.float32))
    mask = causal_mask(GROUP)

    def group_rows(group):
        return slice(group * GROUP, (group + 1) * GROUP)

    def parts(group):
        rows = group_rows(group)
        run = running[rows]
        act = activated[rows].astype(jnp.float32)
        query, key, val = act[:, :keys] * root, act[:, keys : 2 * keys], act[:, 2 * keys :]
        return rows, run, run[GROUP - 1 : GROUP], query, key, val

    carry = jnp.zeros((dim, keys), jnp.float32)
    decay_sum = jnp.zeros((1, keys), jnp.float32)
    decays = [None] * count
    for group in range(count - 1, -1, -1):
        rows, run, last, query, key, val = parts(group)
        following[group] = carry
        decays[group] = decay_sum
        carry = jnp.exp(last) * carry + exact(mixed_low[rows], query * jnp.exp(run), ((0,), (0,)))
        decay_sum = decay_sum + last
    pay[0:dim] = carry
    pay[dim : dim + 8] = jnp.broadcast_to(jnp.exp(decay_sum), (8, keys))
    exchange.start()
    for k in range(levels - 1):
        line.arrive(k)
        share.start_piece(k)
    share.copy(SHARES, share.mine, share.side_mine, share.near)

    def local(group):
        rows, run, last, query, key, val = parts(group)
        outgrad = mixed_low[rows]
        query_in, key_in = query * jnp.exp(run), key * jnp.exp(-run)
        inside = exact(outgrad, val, ((1,), (1,))) * mask
        grad_query = exact(inside, key_in, ((1,), (0,))) + exact(outgrad, starts[group], ((1,), (0,)))
        act_grad[rows, 0:keys] = jnp.exp(run) * grad_query
        act_grad[rows, keys : 2 * keys] = jnp.exp(-run) * exact(inside, query_in, ((0,), (0,)))
        act_grad[rows, 2 * keys : qkv] = exact(scores[rows], outgrad, ((0,), (0,)))

    local(0)
    exchange.along()
    part_gating[...] = across(normed[...], gatein[...])
    part_output[...] = across(resid_low[...], gated[...])
    for group in range(1, count):
        local(group)
    exchange.join()
    ring.start(1)
    ring.start(2)
    exchange.finish()
    entered = after[...]
    tail_sum = jnp.sum(state_end[...] * entered, axis=0, keepdims=True)
    grad_bias = jnp.zeros((1, keys), jnp.float32)
    for group in range(count - 1, -1, -1):
        rows, run, last, query, key, val = parts(group)
        state = following[group] + jnp.exp(decays[group]) * entered
        to_end = jnp.exp(last - run)
        grad_key = act_grad[rows, keys : 2 * keys] + to_end * exact(val, state, ((1,), (0,)))
        grad_val = act_grad[rows, 2 * keys : qkv] + exact(key * to_end, state, ((1,), (1,)))
        grad_query = act_grad[rows, 0:keys]
        grad_run = query * grad_query - key * grad_key
        grad_log = exact(mask, grad_run, ((0,), (0,))) + tail_sum
        tail_sum = tail_sum + jnp.sum(grad_run, axis=0, keepdims=True)
        grad_logits = grad_log * jax.nn.sigmoid(-logits[rows]) / NORMALIZER
        grad_bias = grad_bias + jnp.sum(grad_logits, axis=0, keepdims=True)
        logits_low[rows] = grad_logits.astype(jnp.bfloat16)
        for first, grad in ((0, grad_query * root), (keys, grad_key), (2 * keys, grad_val)):
            columns = slice(first, first + grad.shape[1])
            filtered_grad[rows, columns] = grad * silu_grad(filtered[rows, columns])
    edge_copy = pltpu.make_async_remote_copy(
        src_ref=filtered_grad.at[pl.ds(0, 16)],
        dst_ref=edge_in,
        send_sem=edge_send,
        recv_sem=edge_recv,
        device_id=preceding,
        device_id_type=MESH,
    )
    edge_copy.start()
    ring.lap(1, 1)
    ring.lap(2, 1)
    for lag in range(lags + 1):
        total = jnp.zeros((1, qkv), jnp.float32)
        for group in range(count):
            base = group * GROUP
            before = padded[16 + base - lag : 16 + base - lag + GROUP]
            total = total + jnp.sum(filtered_grad[group_rows(group)] * before, axis=0, keepdims=True)
        own[0, lag : lag + 1] = total
    grad_expand = across(squeezed[...], logits_low[...])
    squeeze_low = against(logits_low[...], expand[...]).astype(jnp.bfloat16)
    shared[0, 0:rank] = across(squeeze_low, normed[...])
    edge_copy.wait_recv()
    filtered_grad[tokens : tokens + 16] = jnp.where(s < size - 1, edge_in[...], 0.0)
    for group in range(count):
        base = group * GROUP
        total = taps[0:1] * filtered_grad[base : base + GROUP]
        for lag in range(1, lags + 1):
            total = total + taps[lag : lag + 1] * filtered_grad[base + lag : base + lag + GROUP]
        projected_low[base : base + GROUP] = total.astype(jnp.bfloat16)
    value[...] = (
        against(projected_low[...], weight[...])
        + against(gatein[...], gating[...])
        + product(squeeze_low, squeeze[...])
    )
    ending.start()
    part_project[...] = across(normed[...], projected_low[...])
    ring.start(0)
    ring.lap(1, 2)
    ring.lap(2, 2)
    ending.across_chips()
    feeding.start()

    def first_rows(rows, total):
        values = block_in[rows].astype(jnp.float32)
        return total + jnp.sum(value[rows] * values * rms_scale(values), axis=0, keepdims=True)

    shared[0, rank : rank + 1] = rows_loop(first_rows, jnp.zeros((1, width), jnp.float32))
    shared[0, rank + 1 : rank + 2, 0:dim] = grad_scale
    for index in range(width // qkv):
        own[0, 8 + index : 9 + index] = grad_second[:, index * qkv : (index + 1) * qkv]
    for index in range(rank // 8):
        own[0, 16:24, index * keys : (index + 1) * keys] = grad_expand[index * 8 : (index + 1) * 8]
    own[0, 24:25, 0:keys] = grad_bias

    def small_copy(buffer, landing, send, recv, index):
        return pltpu.make_async_remote_copy(
            src_ref=buffer.at[index],
            dst_ref=landing.at[index],
            send_sem=send.at[index],
            recv_sem=recv.at[index],
            device_id=small_peers[index],
            device_id_type=MESH,
        )

    own_copies = [small_copy(own, own_in, own_send, own_recv, k) for k in range(seq_bits)]
    shared_copies = [
        small_copy(shared, shared_in, shared_send, shared_recv, k)
        for k in range(seq_bits + head_bits)
    ]

    def small_step(index):
        if index > 0 and index <= seq_bits:
            own_copies[index - 1].wait_recv()
            own[index] = own[index - 1] + own_in[index - 1]
        if index > 0:
            shared_copies[index - 1].wait_recv()
            shared[index] = shared[index - 1] + shared_in[index - 1]
        if index < seq_bits:
            own_copies[index].start()
        if index < seq_bits + head_bits:
            shared_copies[index].start()

    share.finish()
    collect(n_all, tokens, h, landed, far_out, side_mine, side_far)

    def gathered_rows(index, carry):
        rows = pl.ds(pl.multiple_of(tokens + index * 128, 128), 128)
        hidden_units(n_all[rows], against(u_all[rows], drop[...]), rows)
        return carry

    steps = (levels - 1) * tokens // 128
    cuts = [0, steps // 3, 2 * steps // 3, steps]
    small_step(0)
    lax.fori_loop(cuts[0], cuts[1], gathered_rows, 0)
    ring.lap(0, 1)
    ring.lap(1, 3)
    ring.lap(2, 3)
    lax.fori_loop(cuts[1], cuts[2], gathered_rows, 0)
    small_step(1)
    feeding.across_chips()
    ring.lap(0, 2)
    ring.lap(1, 4)
    ring.lap(2, 4)
    lax.fori_loop(cuts[2], cuts[3], gathered_rows, 0)
    per = theirs.shape[2]
    pair = pl.ds(pl.multiple_of(2 * z * per, 2 * per), 2 * per)
    pair_copies = []
    for index, (left, right) in enumerate(((n_all, gv_all), (n_all, lv_all), (u_all, inner_all))):
        both[...] = across(right[...], left[:, pair])
        theirs[index] = both[:, pl.ds(pl.multiple_of((1 - y) * per, per), per)]
        item = pltpu.make_async_remote_copy(
            src_ref=theirs.at[index],
            dst_ref=theirs_in.at[index],
            send_sem=pair_send.at[index],
            recv_sem=pair_recv.at[index],
            device_id=exchange.beside,
            device_id_type=MESH,
        )
        item.start()
        pair_copies.append(item)
        feed_sum[index] = both[:, pl.ds(pl.multiple_of(y * per, per), per)]
        if index == 0:
            small_step(2)
        ring.lap(0, 3 + index)
        if index < 2:
            ring.lap(1, 5 + index)
            ring.lap(2, 5 + index)
    ending.hand_back()
    small_step(3)
    ring.lap(0, 6)
    small_step(4)
    ending.finish()

    def input_rows(rows, carry):
        values = block_in[rows].astype(jnp.float32)
        back = rms_back(values, rms_scale(values), first_gain[...], grad_one[rows])
        input_grad[rows] = grad_resid[rows] + back
        return carry

    rows_loop(input_rows, 0)
    feeding.hand_back()
    small_step(5)
    ring.last(1, packed, slice(qkv, qkv + dim))
    ring.last(2, packed, slice(qkv + dim, qkv + 2 * dim))
    feeding.finish()

    def out_rows(rows, carry):
        block_out[rows] = (residual[rows] + feed_out[rows]).astype(jnp.bfloat16)
        return carry

    rows_loop(out_rows, 0)
    base = ring.rows
    packed[base : base + 32, 0:qkv] = own[seq_bits]
    base += 32
    packed[base : base + shared.shape[1], 0:width] = shared[seq_bits + head_bits]
    ring.last(0, packed, slice(0, qkv))
    for index in range(3):
        pair_copies[index].wait_recv()
        feed_sum[index] = feed_sum[index] + theirs_in[index]
    for item in pair_copies + own_copies + shared_copies + [edge_copy]:
        item.wait_send()
    line.finish()
    ring.finish()


def back(forward, params):
    size, heads = lax.axis_size("seq"), lax.axis_size("head")
    levels = size // 2
    f32, b16 = jnp.float32, jnp.bfloat16
    block_in, weight, taps, squeeze, expand, gating, drop = (params[k] for k in (0, 4, 5, 6, 7, 8, 13))
    tokens, width = block_in.shape
    qkv, keys, dim, rank, hidden = weight.shape[1], expand.shape[1], gating.shape[1], expand.shape[0], drop.shape[0]
    rows, inside, share = width // size, levels * tokens, width // heads
    seq_bits, all_bits = size.bit_length() - 1, size.bit_length() + heads.bit_length() - 2
    own_shape, shared_shape = (32, qkv), (rank + 8, width)
    outs = [((tokens, width), b16), ((tokens, width), f32)]
    outs += [((rows + 32 + shared_shape[0], qkv + 2 * dim), f32), ((3, hidden, rows), f32)]
    held = [((tokens, width), f32), ((tokens, width), b16), ((tokens, width), f32), ((tokens, width), b16)]
    held += [((tokens, width), f32)] * 5
    held += [((tokens, dim), b16), ((tokens, dim), f32), ((tokens, qkv), f32)]
    held += [((tokens + 16, qkv), f32), ((16, qkv), f32), ((tokens // GROUP, dim, keys), f32)]
    held += [((tokens, qkv), b16), ((tokens, keys), b16), ((dim + 8, keys), f32), ((dim, keys), f32)]
    held += [((inside, width), b16)] + [((inside, hidden), b16)] * 3
    held += [((hidden, 2 * rows), f32)]
    held += [((3, hidden, rows), f32)] * 2 + [((inside - tokens, share), f32)] * 4
    held += [((seq_bits + 1,) + own_shape, f32), ((all_bits + 1,) + shared_shape, f32)]
    held += [((seq_bits,) + own_shape, f32), ((all_bits,) + shared_shape, f32)]
    held += [((width, qkv), f32), ((width, dim), f32), ((width, dim), f32)]
    held += [((2, size - 1, rows // 2, x), f32) for x in (qkv, dim, dim)]
    value = jax.ShapeDtypeStruct((tokens, width), f32)
    dma = pltpu.SemaphoreType.DMA
    scratch = [pltpu.VMEM(*x) for x in held]
    scratch += [dma((3, 2, size - 1))] * 2 + [dma((seq_bits,))] * 2 + [dma((all_bits,))] * 2
    scratch += [dma, dma] + [dma((3,))] * 2
    scratch += exchange_scratch(size, dim, keys) + head_scratch(value) * 3
    scratch += gather_scratch(levels, tokens, share) + share_scratch()
    operands = list(forward) + list(params)
    scratch += load_scratch(operands)
    return pl.pallas_call(
        functools.partial(back_kernel, size, heads),
        out_shape=[jax.ShapeDtypeStruct(*x) for x in outs],
        in_specs=[pl.BlockSpec(memory_space=pl.ANY)] * len(operands),
        out_specs=[pl.BlockSpec(memory_space=pltpu.VMEM)] * len(outs),
        scratch_shapes=scratch,
        compiler_params=pltpu.CompilerParams(
            collective_id=5, has_side_effects=True, vmem_limit_bytes=60 * 1024 * 1024
        ),
    )(*operands)


def unpack(packed, taps, rank, keys, dim, width, rows, results):
    lags, qkv = taps.shape[0], taps.shape[1]
    first, second, scale, bias, taps_out, expand, squeeze, *outs = results
    base = rows
    taps_out[:, 0] = packed[base : base + lags, 0:qkv]
    for index in range(width // qkv):
        second[:, index * qkv : (index + 1) * qkv] = packed[base + 8 + index : base + 9 + index, 0:qkv]
    for index in range(rank // 8):
        expand[index * 8 : (index + 1) * 8] = packed[base + 16 : base + 24, index * keys : (index + 1) * keys]
    bias[...] = packed[base + 24 : base + 25, 0:keys]
    base += 32
    squeeze[...] = packed[base : base + rank, 0:width]
    first[...] = packed[base + rank : base + rank + 1, 0:width]
    scale[...] = packed[base + rank + 1 : base + rank + 2, 0:dim]


def spread_kernel(taps_shape, dim, *refs):
    packed, feed, *results = refs
    taps = jax.ShapeDtypeStruct(taps_shape, jnp.float32)
    qkv = taps.shape[1]
    rank, keys = results[5].shape
    rows, width = results[7].shape[0], results[0].shape[1]
    unpack(packed, taps, rank, keys, dim, width, rows, results)
    results[7][:, 0] = packed[0:rows, 0:qkv]
    results[8][...] = packed[0:rows, qkv : qkv + dim]
    results[9][...] = jnp.transpose(packed[0:rows, qkv + dim : qkv + 2 * dim])
    for index in range(3):
        results[10 + index][...] = feed[index]


def spread(packed, feed, taps, expand, dim, width):
    rank, keys = expand.shape
    rows, lags, qkv = width // lax.axis_size("seq"), taps.shape[0], taps.shape[1]
    shapes = [(1, width), (1, width), (1, dim), (1, keys), (lags, 1, qkv), expand.shape, (rank, width)]
    shapes += [(rows, 1, qkv), (rows, dim), (dim, rows)] + [feed.shape[1:]] * 3
    return pl.pallas_call(
        functools.partial(spread_kernel, taps.shape, dim),
        out_shape=[jax.ShapeDtypeStruct(x, jnp.float32) for x in shapes],
        in_specs=[pl.BlockSpec(memory_space=pltpu.VMEM)] * 2,
        compiler_params=pltpu.CompilerParams(vmem_limit_bytes=60 * 1024 * 1024),
    )(packed, feed)


def local_states(decays, updates, backward):
    count = updates.shape[1]
    carry = jnp.zeros_like(updates[:, 0])
    states = [None] * count
    for index in range(count):
        group = count - 1 - index if backward else index
        states[group] = carry
        carry = jnp.exp(decays[:, group])[:, None] * carry + updates[:, group]
    return (jnp.stack(states, axis=1), carry)


def body(
    block_in,
    upstream,
    first_gain,
    project_in,
    filter_taps,
    squeeze,
    expand,
    decay_bias,
    gating,
    head_scale,
    project_out,
    second_gain,
    hidden_gate,
    hidden_lift,
    hidden_drop,
):
    seqs, tokens, width = block_in.shape
    total_rows = seqs * tokens
    key_dim = expand.shape[1]
    value_dim = gating.shape[1]
    mixed_dim = project_in.shape[2]
    lags = filter_taps.shape[0] - 1
    count = tokens // GROUP
    taps = filter_taps.reshape(lags + 1, mixed_dim)
    weight_in = project_in.reshape(width, mixed_dim)
    size, hidden = lax.axis_size("seq"), hidden_gate.shape[1]
    gathering = size // 2 == SHARES + 1 and total_rows * width <= 512 * 1024
    seed = upstream.reshape(total_rows, width)
    residual_in = block_in.reshape(total_rows, width).astype(jnp.float32)
    scale_one = rms_scale(residual_in)
    (
        normed_one,
        padded,
        filtered,
        activated,
        squeezed,
        logits,
        gate_in,
        running,
        scores,
        starts,
        state_end,
        mixed,
        branch,
        gated,
        *seed_cols,
    ) = front(
        block_in.reshape(total_rows, width),
        first_gain[None],
        weight_in,
        taps,
        jnp.transpose(squeeze),
        expand,
        decay_bias[None],
        gating,
        head_scale[None],
        project_out,
        seed if gathering else None,
    )
    if gathering:
        block_out, input_grad, packed, feed_sum = back(
            (
                normed_one,
                padded,
                filtered,
                activated,
                squeezed,
                logits,
                gate_in,
                running,
                scores,
                starts,
                state_end,
                mixed,
                branch,
                gated,
                *seed_cols,
            ),
            (
                block_in.reshape(total_rows, width),
                seed,
                first_gain[None],
                second_gain[None],
                weight_in,
                taps,
                jnp.transpose(squeeze),
                expand,
                gating,
                head_scale[None],
                project_out,
                jnp.transpose(hidden_gate),
                jnp.transpose(hidden_lift),
                hidden_drop,
            ),
        )
        done = spread(packed, feed_sum, taps, expand, value_dim, width)
        return (
            block_out[None],
            input_grad[None],
            done[0][0],
            done[7],
            done[4],
            jnp.transpose(done[6]),
            done[5],
            done[3][0],
            done[8],
            done[2][0],
            done[9],
            done[1][0],
            jnp.transpose(done[10]),
            jnp.transpose(done[11]),
            done[12],
        )
    padded = padded[16 - lags :][None]
    projected = padded[:, lags:]
    filtered, state_end = filtered[None], state_end[None]
    activated = activated.astype(jnp.float32)[None]
    root = key_dim ** (-0.5)
    query = grouped(activated[..., :key_dim] * root, seqs, count)
    keys = grouped(activated[..., key_dim : 2 * key_dim], seqs, count)
    values = grouped(activated[..., 2 * key_dim :], seqs, count)
    mask = causal_mask(GROUP)
    running, starts = grouped(running[None], seqs, count), starts[None]
    last = running[:, :, -1]
    query_in = query * jnp.exp(running)
    key_in = keys * jnp.exp(-running)
    key_end = keys * jnp.exp(last[:, :, None] - running)
    scores = grouped(scores[None], seqs, count)
    decay_sum = jnp.sum(last, axis=1)
    decay_total = jnp.exp(decay_sum)
    scale_head = rms_scale(mixed)
    normed_head = mixed * scale_head * head_scale
    residual = residual_in + branch
    scale_two = rms_scale(residual)
    normed_two = (residual * scale_two * second_gain).astype(jnp.bfloat16)
    gate_value = product(normed_two, hidden_gate)
    lift_value = product(normed_two, hidden_lift)
    inner = (jax.nn.silu(gate_value) * lift_value).astype(jnp.bfloat16)
    partial_feed = product(inner, hidden_drop)
    grad_inner = against(seed, hidden_drop)
    grad_gv = (grad_inner * lift_value * silu_grad(gate_value)).astype(jnp.bfloat16)
    grad_lv = (grad_inner * jax.nn.silu(gate_value)).astype(jnp.bfloat16)
    grad_two = head_sum(against(grad_gv, hidden_gate) + against(grad_lv, hidden_lift))
    grad_second = jnp.sum(grad_two * residual * scale_two, axis=0)
    grad_resid = seed.astype(jnp.float32) + rms_back(residual, scale_two, second_gain, grad_two)
    resid_low = grad_resid.astype(jnp.bfloat16)
    grad_output = across(resid_low, gated)
    grad_gated = against(resid_low, project_out)
    grad_gatein = (grad_gated * normed_head * silu_grad(gate_in)).astype(jnp.bfloat16)
    grad_normhead = grad_gated * jax.nn.silu(gate_in)
    grad_scale = jnp.sum(grad_normhead * mixed * scale_head, axis=0)
    grad_mixed_low = rms_back(mixed, scale_head, head_scale, grad_normhead).astype(jnp.bfloat16)
    grad_mixed = lax.optimization_barrier(grad_mixed_low).astype(jnp.float32)
    outgrad = grouped(grad_mixed.reshape(seqs, tokens, value_dim), seqs, count)
    query_end = jnp.einsum("snic,snid->sndc", query_in, outgrad, precision=HIGH)
    following_zero, back_total = local_states(last, query_end, True)
    after = entering(decay_total[0], back_total[0])[None]
    after_group = decay_sum[:, None] - running_sums(last)
    following = following_zero + jnp.exp(after_group)[:, :, None] * after[:, None]
    inner_group = jnp.einsum("snid,snjd->snij", outgrad, values, precision=HIGH) * mask
    grad_query = jnp.exp(running) * (
        jnp.einsum("snij,snjc->snic", inner_group, key_in, precision=HIGH)
        + jnp.einsum("snid,sndc->snic", outgrad, starts, precision=HIGH)
    )
    grad_keys = jnp.exp(-running) * jnp.einsum(
        "snij,snic->snjc", inner_group, query_in, precision=HIGH
    )
    grad_keys = grad_keys + jnp.exp(last[:, :, None] - running) * jnp.einsum(
        "snjd,sndc->snjc", values, following, precision=HIGH
    )
    grad_values = jnp.einsum("snij,snid->snjd", scores, outgrad, precision=HIGH)
    grad_values = grad_values + jnp.einsum("snjc,sndc->snjd", key_end, following, precision=HIGH)
    grad_running = (query * grad_query - keys * grad_keys).reshape(seqs, tokens, key_dim)
    beyond = jnp.sum(state_end * after, axis=1)
    upper = jnp.transpose(causal_mask(tokens))
    suffix = jnp.einsum("ij,sjc->sic", upper, grad_running, precision=HIGH)
    grad_log = suffix + beyond[:, None]
    grad_act = jnp.concatenate(
        [
            grad_query.reshape(seqs, tokens, key_dim) * root,
            grad_keys.reshape(seqs, tokens, key_dim),
            grad_values.reshape(seqs, tokens, value_dim),
        ],
        axis=-1,
    )
    grad_filtered = grad_act * silu_grad(filtered)
    later = shifted(grad_filtered[:, :lags], "seq", -1)
    padded_back = jnp.concatenate([grad_filtered, later], axis=1)
    grad_projected = taps[0] * grad_filtered
    tap_rows = [jnp.sum(grad_filtered * projected, axis=(0, 1))]
    for lag in range(1, lags + 1):
        grad_projected = grad_projected + taps[lag] * padded_back[:, lag : lag + tokens]
        tap_rows.append(
            jnp.sum(grad_filtered * padded[:, lags - lag : lags - lag + tokens], axis=(0, 1))
        )
    grad_taps = jnp.stack(tap_rows).reshape(lags + 1, 1, mixed_dim)
    grad_projected = grad_projected.reshape(total_rows, mixed_dim).astype(jnp.bfloat16)
    grad_logits = grad_log.reshape(total_rows, key_dim) * jax.nn.sigmoid(-logits) / NORMALIZER
    grad_bias = jnp.sum(grad_logits, axis=0)
    logits_low = grad_logits.astype(jnp.bfloat16)
    grad_expand = across(squeezed, logits_low)
    squeeze_low = against(logits_low, expand).astype(jnp.bfloat16)
    grad_squeeze = across(squeeze_low, normed_one)
    partials = [across(normed_one, grad_projected), across(normed_one, grad_gatein), grad_output]
    partials += [across(normed_two, grad_gv), across(normed_two, grad_lv), across(seed, inner)]
    partial_value = (
        against(grad_projected, weight_in)
        + against(grad_gatein, gating)
        + against(squeeze_low, squeeze)
    )
    partial_first = jnp.sum(partial_value * residual_in * scale_one, axis=0)
    grad_one, feed, packed = tail(
        partial_value,
        partial_feed,
        (grad_taps[:, 0], grad_expand, grad_bias[None], grad_second[None]),
        (grad_squeeze, partial_first[None], grad_scale[None]),
        partials,
    )
    done = finishing(
        block_in[0],
        first_gain[None],
        grad_one,
        grad_resid,
        residual,
        feed,
        packed,
        (),
        lags + 1,
        expand,
        head_scale,
        tuple(x.shape[1] for x in partials),
    )
    block_out, input_grad, sum_first, sum_second, sum_scale, sum_bias = done[:6]
    sum_taps, sum_expand, sum_squeeze = done[6:9]
    own_project, own_gating, own_output, own_gate, own_lift, own_drop = done[9:]
    own_drop = jnp.transpose(own_drop)
    return (
        block_out[None],
        input_grad[None],
        sum_first[0],
        own_project,
        sum_taps,
        jnp.transpose(sum_squeeze),
        sum_expand,
        sum_bias[0],
        own_gating,
        sum_scale[0],
        own_output,
        sum_second[0],
        own_gate,
        own_lift,
        own_drop,
    )


def solution(mesh):
    in_specs = (
        P(None, "seq", None),
        P(None, "seq", None),
        P(),
        P(None, "head", None),
        P(None, "head", None),
        P(),
        P(None, "head"),
        P("head"),
        P(None, "head"),
        P(),
        P("head", None),
        P(),
        P(None, "head"),
        P(None, "head"),
        P("head", None),
    )
    out_specs = (
        P(None, "seq", None),
        P(None, "seq", None),
        P(),
        P("seq", "head", None),
        P(None, "head", None),
        P(),
        P(None, "head"),
        P("head"),
        P("seq", "head"),
        P(),
        P("head", "seq"),
        P(),
        P("seq", "head"),
        P("seq", "head"),
        P("head", "seq"),
    )
    return jax.shard_map(body, mesh=mesh, in_specs=in_specs, out_specs=out_specs, check_vma=False)
```

```python
import functools

import jax
import jax.numpy as jnp
from jax import lax
from jax.experimental import pallas as pl
from jax.experimental.pallas import tpu as pltpu
from jax.sharding import PartitionSpec as P

GROUP = 64


EPS = 1e-05
NORMALIZER = 16.0
HIGH = lax.Precision.HIGHEST


MESH = pl.DeviceIdType.MESH
PIECES = 4
SHARES = 3


def greet(devices):
    barrier = pltpu.get_barrier_semaphore()
    for device in devices:
        pl.semaphore_signal(barrier, inc=1, device_id=device, device_id_type=MESH)
    pl.semaphore_wait(barrier, len(devices))


def place_of():
    s, h = lax.axis_index("seq"), lax.axis_index("head")
    return s, h, s // 2, s % 2


def head_partners():
    s, h = lax.axis_index("seq"), lax.axis_index("head")
    core, chip = h % 2, h // 2
    return (s, chip * 2 + 1 - core), (s, (1 - chip) * 2 + core)


class HeadSum:
    def __init__(self, value, out, pair, summed, other, back, send_sem, recv_sem):
        self.value, self.out = value, out
        self.pair, self.summed, self.other, self.back = pair, summed, other, back
        self.send_sem, self.recv_sem = send_sem, recv_sem
        self.near, self.far = head_partners()
        core = lax.axis_index("head") % 2
        half = value.shape[0] // 2
        self.piece = half // PIECES
        self.mine = pl.multiple_of(core * half, half)
        self.theirs = pl.multiple_of((1 - core) * half, half)
        self.first, self.second, self.third = [], [], []

    def copy(self, stage, index, source, target, device):
        item = pltpu.make_async_remote_copy(
            src_ref=source,
            dst_ref=target.at[pl.ds(index * self.piece, self.piece)],
            send_sem=self.send_sem.at[stage, index],
            recv_sem=self.recv_sem.at[stage, index],
            device_id=device,
            device_id_type=MESH,
        )
        item.start()
        return item

    def start(self):
        for index in range(PIECES):
            source = self.value.at[pl.ds(self.theirs + index * self.piece, self.piece)]
            self.first.append(self.copy(0, index, source, self.pair, self.near))

    def across_chips(self):
        for index in range(PIECES):
            rows = pl.ds(index * self.piece, self.piece)
            self.first[index].wait_recv()
            self.summed[rows] = (
                self.value[pl.ds(self.mine + index * self.piece, self.piece)] + self.pair[rows]
            )
            self.second.append(self.copy(1, index, self.summed.at[rows], self.other, self.far))

    def hand_back(self):
        for index in range(PIECES):
            rows = pl.ds(index * self.piece, self.piece)
            self.second[index].wait_recv()
            total = pl.ds(self.mine + index * self.piece, self.piece)
            self.out[total] = self.summed[rows] + self.other[rows]
            self.third.append(self.copy(2, index, self.out.at[total], self.back, self.near))

    def finish(self):
        for index in range(PIECES):
            self.third[index].wait_recv()
            rows = pl.ds(self.theirs + index * self.piece, self.piece)
            self.out[rows] = self.back[pl.ds(index * self.piece, self.piece)]
        for item in self.first + self.second + self.third:
            item.wait_send()


def head_scratch(value):
    landing = pltpu.VMEM((value.shape[0] // 2, value.shape[1]), jnp.float32)
    return [landing] * 4 + [pltpu.SemaphoreType.DMA((3, PIECES))] * 2


class ColumnShare:
    def __init__(self, mine, far_out, side_mine, side_far, send_sem, recv_sem):
        self.mine, self.far_out, self.side_mine, self.side_far = mine, far_out, side_mine, side_far
        self.send_sem, self.recv_sem = send_sem, recv_sem
        self.near, self.far = head_partners()
        self.piece = mine.shape[0] // SHARES
        self.items = {}

    def copy(self, index, source, target, device):
        item = pltpu.make_async_remote_copy(
            src_ref=source,
            dst_ref=target,
            send_sem=self.send_sem.at[index],
            recv_sem=self.recv_sem.at[index],
            device_id=device,
            device_id_type=MESH,
        )
        item.start()
        self.items[index] = item

    def start_piece(self, k):
        take = pl.ds(k * self.piece, self.piece)
        self.copy(k, self.mine.at[take], self.far_out.at[take], self.far)

    def start(self):
        for k in range(SHARES):
            self.start_piece(k)
        self.copy(SHARES, self.mine, self.side_mine, self.near)

    def finish(self):
        for k in range(SHARES):
            take = pl.ds(k * self.piece, self.piece)
            self.items[k].wait_recv()
            self.copy(SHARES + 1 + k, self.far_out.at[take], self.side_far.at[take], self.near)
        for k in range(SHARES, 2 * SHARES + 1):
            self.items[k].wait_recv()
        for k in range(2 * SHARES + 1):
            self.items[k].wait_send()


def share_scratch():
    return [pltpu.SemaphoreType.DMA((2 * SHARES + 1,))] * 2


def sum_kernel(value, out, *scratch):
    stages = HeadSum(value, out, *scratch)
    greet((stages.near, stages.far))
    stages.start()
    stages.across_chips()
    stages.hand_back()
    stages.finish()


def head_sum(value):
    return pl.pallas_call(
        sum_kernel,
        out_shape=jax.ShapeDtypeStruct(value.shape, jnp.float32),
        in_specs=[pl.BlockSpec(memory_space=pltpu.VMEM)],
        out_specs=pl.BlockSpec(memory_space=pltpu.VMEM),
        scratch_shapes=head_scratch(value),
        compiler_params=pltpu.CompilerParams(
            collective_id=4, has_side_effects=True, vmem_limit_bytes=24 * 1024 * 1024
        ),
    )(value)


class Exchange:
    def __init__(self, size, backward, pay, out, near, pair, landed, part, other, send_sem, recv_sem):
        self.backward, self.pay, self.out = backward, pay, out
        self.near, self.pair, self.landed, self.part, self.other = near, pair, landed, part, other
        self.send_sem, self.recv_sem = send_sem, recv_sem
        s, h, self.z, self.y = place_of()
        self.levels = size // 2
        self.beside = (2 * self.z + 1 - self.y, h)
        self.peers = [
            (2 * ((self.z + k) % self.levels) + self.y, h) for k in range(1, self.levels)
        ]
        self.partners = [self.beside] + self.peers
        self.rows = out.shape[0]
        self.half = self.rows // 2
        self.mine = pl.multiple_of(self.y * self.half, self.half)
        self.theirs = pl.multiple_of((1 - self.y) * self.half, self.half)
        self.second = (self.y == 0) if backward else (self.y == 1)

    def copy(self, index, source, target, device):
        item = pltpu.make_async_remote_copy(
            src_ref=source,
            dst_ref=target,
            send_sem=self.send_sem.at[index],
            recv_sem=self.recv_sem.at[index],
            device_id=device,
            device_id_type=MESH,
        )
        item.start()
        return item

    def start(self):
        self.first = self.copy(0, self.pay, self.near, self.beside)

    def along(self):
        pay, near, rows, half = self.pay, self.near, self.rows, self.half
        self.first.wait_recv()
        my_decay, near_decay = pay[rows : rows + 1], near[rows : rows + 1]
        my_half, near_half = pay[pl.ds(self.mine, half)], near[pl.ds(self.mine, half)]
        self.pair[0:half] = jnp.where(
            self.second, my_decay * near_half + my_half, near_decay * my_half + near_half
        )
        self.pair[half : half + 8] = pay[rows : rows + 8] * near[rows : rows + 8]
        self.sends = [
            self.copy(k, self.pair, self.landed.at[k - 1], self.peers[k - 1])
            for k in range(1, self.levels)
        ]

    def join(self):
        half, levels, z = self.half, self.levels, self.z
        for item in self.sends:
            item.wait_recv()
        total = jnp.zeros((half, self.out.shape[1]), jnp.float32)
        for back in range(levels - 1, 0, -1):
            k = levels - back if self.backward else back
            valid = (z + back < levels) if self.backward else (z - back >= 0)
            longer = self.landed[k - 1, half : half + 1] * total + self.landed[k - 1, 0:half]
            total = jnp.where(valid, longer, total)
        self.part[...] = total
        self.last = self.copy(levels, self.part, self.other, self.beside)
        decay, near_half = self.near[self.rows : self.rows + 1], self.near[pl.ds(self.mine, half)]
        self.out[pl.ds(self.mine, half)] = jnp.where(self.second, decay * total + near_half, total)

    def finish(self):
        half = self.half
        self.last.wait_recv()
        rest, near_half = self.other[...], self.near[pl.ds(self.theirs, half)]
        decay = self.near[self.rows : self.rows + 1]
        self.out[pl.ds(self.theirs, half)] = jnp.where(self.second, decay * rest + near_half, rest)
        for item in [self.first, self.last] + self.sends:
            item.wait_send()


def exchange_scratch(size, rows, lanes):
    half, levels = rows // 2, size // 2
    return [
        pltpu.VMEM((rows + 8, lanes), jnp.float32),
        pltpu.VMEM((half + 8, lanes), jnp.float32),
        pltpu.VMEM((levels - 1, half + 8, lanes), jnp.float32),
        pltpu.VMEM((half, lanes), jnp.float32),
        pltpu.VMEM((half, lanes), jnp.float32),
    ] + [pltpu.SemaphoreType.DMA((levels + 1,))] * 2


def exchange_kernel(size, pay, out, *scratch):
    exchange = Exchange(size, True, pay, out, *scratch)
    greet(exchange.partners)
    exchange.start()
    exchange.along()
    exchange.join()
    exchange.finish()


def entering(decay, state):
    size = lax.axis_size("seq")
    rows, lanes = state.shape
    pay = jnp.concatenate([state, jnp.broadcast_to(decay[None], (8, lanes))], axis=0)
    return pl.pallas_call(
        functools.partial(exchange_kernel, size),
        out_shape=jax.ShapeDtypeStruct(state.shape, jnp.float32),
        in_specs=[pl.BlockSpec(memory_space=pltpu.VMEM)],
        out_specs=pl.BlockSpec(memory_space=pltpu.VMEM),
        scratch_shapes=exchange_scratch(size, rows, lanes),
        compiler_params=pltpu.CompilerParams(
            collective_id=3, has_side_effects=True, vmem_limit_bytes=16 * 1024 * 1024
        ),
    )(pay)


def tail_kernel(size, heads, arrays, *refs):
    value, feed, taps, expand, bias, second, squeeze, first, scale, *refs = refs
    ins, (value_out, feed_out, packed, *scratch) = refs[:arrays], refs[arrays:]
    own, shared, own_in, shared_in = scratch[:4]
    slots, scratch = scratch[4 : 4 + arrays], scratch[4 + arrays :]
    own_send, own_recv, shared_send, shared_recv, send_sem, recv_sem, *head_refs = scratch
    stages = HeadSum(value, value_out, *head_refs[:6])
    feeding = HeadSum(feed, feed_out, *head_refs[6:])
    half = size // 2
    me = lax.axis_index("seq")
    mine_head = lax.axis_index("head")
    low, high = me % 2, me // 2
    place = high + low * (2 * half - 1 - 2 * high)

    def member(position):
        position = (position + 2 * size) % size
        side = position // half
        return 2 * (position + side * (2 * half - 1 - 2 * position)) + side

    partners = ((member(place + 1), mine_head), (member(place - 1), mine_head))
    seq_bits, head_bits = size.bit_length() - 1, heads.bit_length() - 1
    small_peers = []
    for bit in range(seq_bits):
        step = 1 << bit
        small_peers.append((me + step - 2 * step * ((me // step) % 2), mine_head))
    small_peers += [stages.near, stages.far]
    greet(list(partners) + small_peers)

    rows = ins[0].shape[0] // size
    part = rows // 2

    def block(array, direction, position):
        start = pl.multiple_of(member(position) * rows + direction * part, part)
        return ins[array].at[pl.ds(start, part)]

    def copy(array, direction, step, source):
        return pltpu.make_async_remote_copy(
            src_ref=source,
            dst_ref=slots[array].at[direction, step],
            send_sem=send_sem.at[array, direction, step],
            recv_sem=recv_sem.at[array, direction, step],
            device_id=partners[direction],
            device_id_type=MESH,
        )

    stages.start()
    for array in range(arrays):
        for direction, sign in ((0, 1), (1, -1)):
            copy(array, direction, 0, block(array, direction, place - sign)).start()

    width, keys = squeeze.shape[1], expand.shape[1]
    mixed, lags, rank = taps.shape[1], taps.shape[0], expand.shape[0]
    own[0, 0:lags] = taps[...]
    for index in range(width // mixed):
        own[0, 8 + index : 9 + index] = second[:, index * mixed : (index + 1) * mixed]
    for index in range(rank // 8):
        own[0, 16:24, index * keys : (index + 1) * keys] = expand[index * 8 : (index + 1) * 8]
    own[0, 24:25, 0:keys] = bias[...]
    shared[0, 0:rank] = squeeze[...]
    shared[0, rank : rank + 1] = first[...]
    shared[0, rank + 1 : rank + 2, 0 : scale.shape[1]] = scale[...]

    def small_copy(buffer, landing, send, recv, index):
        return pltpu.make_async_remote_copy(
            src_ref=buffer.at[index],
            dst_ref=landing.at[index],
            send_sem=send.at[index],
            recv_sem=recv.at[index],
            device_id=small_peers[index],
            device_id_type=MESH,
        )

    own_copies = [small_copy(own, own_in, own_send, own_recv, k) for k in range(seq_bits)]
    shared_copies = [
        small_copy(shared, shared_in, shared_send, shared_recv, k)
        for k in range(seq_bits + head_bits)
    ]

    def small_step(index):
        if index > 0 and index <= seq_bits:
            own_copies[index - 1].wait_recv()
            own[index] = own[index - 1] + own_in[index - 1]
        if index > 0:
            shared_copies[index - 1].wait_recv()
            shared[index] = shared[index - 1] + shared_in[index - 1]
        if index < seq_bits:
            own_copies[index].start()
        if index < seq_bits + head_bits:
            shared_copies[index].start()

    def lap(step, carry):
        for array in range(arrays):
            for direction, sign in ((0, 1), (1, -1)):
                slot = slots[array].at[direction, step - 1]
                copy(array, direction, step - 1, slot).wait_recv()
                local = block(array, direction, place - sign * (step + 1))
                slot[...] = slot[...] + local[...]
                copy(array, direction, step, slot).start()
        return carry

    small_step(0)
    stages.across_chips()
    feeding.start()
    lap(1, 0)
    small_step(1)
    feeding.across_chips()
    lap(2, 0)
    small_step(2)
    stages.hand_back()
    lap(3, 0)
    small_step(3)
    lap(4, 0)
    small_step(4)
    feeding.hand_back()
    lax.fori_loop(5, size - 1, lap, 0)
    for index in range(5, seq_bits + head_bits + 1):
        small_step(index)
    stages.finish()
    feeding.finish()
    base = rows
    packed[base : base + 32, 0:mixed] = own[seq_bits]
    base += 32
    packed[base : base + shared.shape[1], 0:width] = shared[seq_bits + head_bits]
    column = 0
    for array in range(arrays):
        across_columns = slice(column, column + ins[array].shape[1])
        column += -(-ins[array].shape[1] // 128) * 128
        for direction in range(2):
            slot = slots[array].at[direction, size - 2]
            copy(array, direction, size - 2, slot).wait_recv()
            local = block(array, direction, place)
            packed[direction * part : (direction + 1) * part, across_columns] = slot[...] + local[...]

    def finish(step, carry):
        for array in range(arrays):
            for direction in range(2):
                copy(array, direction, step, slots[array].at[direction, step]).wait_send()
        return carry

    lax.fori_loop(0, size - 1, finish, 0)
    for item in own_copies + shared_copies:
        item.wait_send()


def tail(value, feed, own, shared, partials):
    size, heads = lax.axis_size("seq"), lax.axis_size("head")
    arrays = len(partials)
    rows = partials[0].shape[0] // size
    seq_bits, all_bits = size.bit_length() - 1, size.bit_length() + heads.bit_length() - 2
    squeeze = shared[0]
    own_shape = (32, own[0].shape[1])
    shared_shape = (squeeze.shape[0] + 8, squeeze.shape[1])
    wide = sum(-(-x.shape[1] // 128) * 128 for x in partials)
    shapes = [value.shape, feed.shape, (rows + own_shape[0] + shared_shape[0], wide)]
    operands = [value, feed, *own, *shared, *partials]
    return pl.pallas_call(
        functools.partial(tail_kernel, size, heads, arrays),
        out_shape=[jax.ShapeDtypeStruct(x, jnp.float32) for x in shapes],
        in_specs=[pl.BlockSpec(memory_space=pltpu.VMEM)] * len(operands),
        out_specs=[pl.BlockSpec(memory_space=pltpu.VMEM)] * len(shapes),
        scratch_shapes=[
            pltpu.VMEM((seq_bits + 1,) + own_shape, jnp.float32),
            pltpu.VMEM((all_bits + 1,) + shared_shape, jnp.float32),
            pltpu.VMEM((seq_bits,) + own_shape, jnp.float32),
            pltpu.VMEM((all_bits,) + shared_shape, jnp.float32),
        ]
        + [pltpu.VMEM((2, size - 1, rows // 2, x.shape[1]), jnp.float32) for x in partials]
        + [pltpu.SemaphoreType.DMA((seq_bits,))] * 2
        + [pltpu.SemaphoreType.DMA((all_bits,))] * 2
        + [pltpu.SemaphoreType.DMA((arrays, 2, size - 1))] * 2
        + head_scratch(value) * 2,
        compiler_params=pltpu.CompilerParams(
            collective_id=0, has_side_effects=True, vmem_limit_bytes=60 * 1024 * 1024
        ),
    )(*operands)


def finish_kernel(gathering, widths, *refs):
    block_in, gain, grad_one, grad_resid, residual, feed, packed, *refs = refs
    feed_mine, feed_more, *refs = refs if gathering else [None, None] + refs
    block_out, input_grad, first, second, scale, bias, taps, expand, squeeze, *outs = refs

    def step(index, carry):
        rows = pl.ds(pl.multiple_of(index * 64, 64), 64)
        values = block_in[rows].astype(jnp.float32)
        back = rms_back(values, rms_scale(values), gain[...], grad_one[rows])
        input_grad[rows] = grad_resid[rows] + back
        block_out[rows] = (residual[rows] + feed[rows]).astype(jnp.bfloat16)
        return carry

    lax.fori_loop(0, block_in.shape[0] // 64, step, 0)
    rows, width = outs[0].shape[0], block_in.shape[1]
    mixed, lags = taps.shape[2], taps.shape[0]
    rank, keys = expand.shape
    base = rows
    taps[:, 0] = packed[base : base + lags, 0:mixed]
    for index in range(width // mixed):
        second[:, index * mixed : (index + 1) * mixed] = packed[base + 8 + index : base + 9 + index, 0:mixed]
    for index in range(rank // 8):
        expand[index * 8 : (index + 1) * 8] = packed[base + 16 : base + 24, index * keys : (index + 1) * keys]
    bias[...] = packed[base + 24 : base + 25, 0:keys]
    base += 32
    squeeze[...] = packed[base : base + rank, 0:width]
    first[...] = packed[base + rank : base + rank + 1, 0:width]
    scale[...] = packed[base + rank + 1 : base + rank + 2, 0 : scale.shape[1]]
    column = 0
    for index, size in enumerate(widths):
        part = packed[0:rows, column : column + size]
        column += -(-size // 128) * 128
        if index == 0:
            outs[index][:, 0] = part
        else:
            outs[index][...] = jnp.transpose(part) if index == 2 else part
    if gathering:
        for index in range(3):
            outs[len(widths) + index][...] = feed_mine[index] + feed_more[index]


def finishing(block_in, gain, grad_one, grad_resid, residual, feed, packed, feed_pair, lags, expand, scale, widths):
    gathering = len(feed_pair) > 0
    operands = [block_in, gain, grad_one, grad_resid, residual, feed, packed, *feed_pair]
    width = block_in.shape[1]
    rank, keys = expand.shape
    rows = width // lax.axis_size("seq")
    shapes = [grad_one.shape, (1, width), (1, width), (1, scale.shape[0]), (1, keys)]
    shapes += [(lags, 1, widths[0]), expand.shape, (rank, width)]
    shapes += [(rows, 1, widths[0]), (rows, widths[1]), (widths[2], rows)]
    shapes += [(rows, x) for x in widths[3:]]
    if gathering:
        shapes += [feed_pair[0].shape[1:]] * 3
    shapes = [jax.ShapeDtypeStruct(x, jnp.float32) for x in shapes]
    return pl.pallas_call(
        functools.partial(finish_kernel, gathering, widths),
        out_shape=[jax.ShapeDtypeStruct(block_in.shape, jnp.bfloat16)] + shapes,
        in_specs=[pl.BlockSpec(memory_space=pltpu.VMEM)] * len(operands),
        compiler_params=pltpu.CompilerParams(vmem_limit_bytes=40 * 1024 * 1024),
    )(*operands)


def shifted(x, axis, by):
    size = lax.axis_size(axis)
    pairs = [(i, i + by) for i in range(size) if 0 <= i + by < size]
    return lax.ppermute(x, axis, pairs)


def product(left, right):
    return jnp.dot(left, right, preferred_element_type=jnp.float32)


def against(left, right):
    return lax.dot_general(
        left, right, (((1,), (1,)), ((), ())), preferred_element_type=jnp.float32
    )


def across(left, right):
    return lax.dot_general(
        left, right, (((0,), (0,)), ((), ())), preferred_element_type=jnp.float32
    )


def rms_scale(values):
    return lax.rsqrt(jnp.mean(values * values, axis=-1, keepdims=True) + EPS)


def rms_back(values, scale, gain, incoming):
    weighted = gain * incoming
    cube = scale * scale * scale
    return scale * weighted - values * cube * jnp.mean(values * weighted, axis=-1, keepdims=True)


def silu_grad(values):
    logistic = jax.nn.sigmoid(values)
    return logistic * (1.0 + values * (1.0 - logistic))


def causal_mask(size):
    rows = lax.broadcasted_iota(jnp.int32, (size, size), 0)
    columns = lax.broadcasted_iota(jnp.int32, (size, size), 1)
    return (columns <= rows).astype(jnp.float32)


def exact(left, right, contract):
    return lax.dot_general(
        left, right, (contract, ((), ())), precision=HIGH, preferred_element_type=jnp.float32
    )


class LineGather:
    def __init__(self, levels, landed, source, send_sem, recv_sem):
        self.levels, self.landed, self.source = levels, landed, source
        self.send_sem, self.recv_sem = send_sem, recv_sem
        s, h, z, y = place_of()
        self.peers = [(2 * ((z + k) % levels) + y, h) for k in range(1, levels)]

    def start(self, wide, part):
        rows, width = self.source.shape
        columns = pl.ds(pl.multiple_of(part * width, width), width)
        self.source[...] = wide[:, columns].astype(jnp.float32)
        self.sends = [
            pltpu.make_async_remote_copy(
                src_ref=self.source,
                dst_ref=self.landed.at[pl.ds(k * rows, rows)],
                send_sem=self.send_sem.at[k],
                recv_sem=self.recv_sem.at[k],
                device_id=self.peers[k],
                device_id_type=MESH,
            )
            for k in range(self.levels - 1)
        ]
        self.sends[0].start()
        self.sends[-1].start()

    def start_rest(self):
        for item in self.sends[1:-1]:
            item.start()

    def arrive(self, k):
        self.sends[k].wait_recv()

    def finish(self):
        for item in self.sends:
            item.wait_send()


def gather_scratch(levels, rows, width):
    return [pltpu.VMEM((rows, width), jnp.float32)] + [pltpu.SemaphoreType.DMA((levels - 1,))] * 2


FRONT_OUTS = 13


def front_kernel(size, gathering, *refs):
    loads, held, between = load_all(refs, 11 if gathering else 10)
    for item in loads[:1] + loads[10:] + loads[1:10]:
        item.start()
    refs = held + between
    block_in, gain, weight, taps, squeeze, expand, bias, gating, head_scale, project_out, *refs = refs
    wide, *refs = refs if gathering else [None] + refs
    outs, refs = refs[:FRONT_OUTS], refs[FRONT_OUTS:]
    normed, padded, filtered, activated, squeezed, logits, gate_in, running, scores = outs[:9]
    starts, state_end, mixed, branch = outs[9:]
    gated, *refs = refs
    seed_all, *refs = refs if gathering else [None] + refs
    edge, edge_in, edge_send, edge_recv, pay, incoming, value, *refs = refs
    exchange = Exchange(size, False, pay, incoming, *refs[:7])
    stages = HeadSum(value, branch, *refs[7:13])
    refs = refs[13:]
    if gathering:
        landed, far_out, side_mine, side_far, *refs = refs
        line = LineGather(size // 2, landed, *refs[:3])
        share = ColumnShare(landed, far_out, side_mine, side_far, *refs[3:])
    s, h, z, y = place_of()
    following, preceding = ((s + 1) % size, h), ((s + size - 1) % size, h)
    greet([following, preceding, stages.near, stages.far] + exchange.partners)
    tokens = block_in.shape[0]
    keys = expand.shape[1]
    lags = taps.shape[0] - 1
    for item in loads[:2] + loads[10:]:
        item.wait()
    edge[...] = block_in[tokens - 16 : tokens].astype(jnp.float32)
    edge_copy = pltpu.make_async_remote_copy(
        src_ref=edge,
        dst_ref=edge_in,
        send_sem=edge_send,
        recv_sem=edge_recv,
        device_id=following,
        device_id_type=MESH,
    )
    edge_copy.start()
    if gathering:
        line.start(wide, h)

    def norm(values):
        return (values * rms_scale(values) * gain[...]).astype(jnp.bfloat16)

    def norm_rows(index, carry):
        rows = pl.ds(pl.multiple_of(index * GROUP, GROUP), GROUP)
        normed[rows] = norm(block_in[rows].astype(jnp.float32))
        return carry

    lax.fori_loop(0, tokens // GROUP, norm_rows, 0)
    for item in loads[2:10]:
        item.wait()
    padded[16 : 16 + tokens] = product(normed[...], weight[...])
    squeezed[...] = against(normed[...], squeeze[...]).astype(jnp.bfloat16)
    logits[...] = product(squeezed[...], expand[...]) + bias[...]
    edge_copy.wait_recv()
    before = product(norm(edge_in[...]), weight[...])
    padded[0:16] = jnp.where(s > 0, before, 0.0)
    mask = causal_mask(GROUP)
    root = keys ** (-0.5)
    count = tokens // GROUP
    carry = jnp.zeros(incoming.shape, jnp.float32)
    decay_sum = jnp.zeros((1, keys), jnp.float32)
    decays = []
    for group in range(count):
        base = group * GROUP
        rows = slice(base, base + GROUP)
        conv = taps[0:1] * padded[16 + base : 16 + base + GROUP]
        for lag in range(1, lags + 1):
            conv = conv + taps[lag : lag + 1] * padded[16 + base - lag : 16 + base - lag + GROUP]
        filtered[rows] = conv
        act = (conv * jax.nn.sigmoid(conv)).astype(jnp.bfloat16)
        activated[rows] = act
        act = act.astype(jnp.float32)
        query, key, val = act[:, :keys] * root, act[:, keys : 2 * keys], act[:, 2 * keys :]
        logit = logits[rows]
        log_decay = (jnp.minimum(logit, 0.0) - jnp.log1p(jnp.exp(-jnp.abs(logit)))) / NORMALIZER
        run = exact(mask, log_decay, ((1,), (0,)))
        running[rows] = run
        last = run[GROUP - 1 : GROUP]
        query_in, key_in, key_end = query * jnp.exp(run), key * jnp.exp(-run), key * jnp.exp(last - run)
        score = exact(query_in, key_in, ((1,), (1,))) * mask
        scores[rows] = score
        mixed[rows] = exact(score, val, ((1,), (0,)))
        starts[group] = carry
        carry = jnp.exp(last) * carry + exact(val, key_end, ((0,), (0,)))
        decays.append(decay_sum)
        decay_sum = decay_sum + last
    dim = carry.shape[0]
    pay[0:dim] = carry
    pay[dim : dim + 8] = jnp.broadcast_to(jnp.exp(decay_sum), (8, keys))
    exchange.start()
    if gathering:
        for k in (0, SHARES - 1):
            line.arrive(k)
            share.start_piece(k)
    gate_in[...] = product(normed[...], gating[...])
    exchange.along()
    exchange.join()
    if gathering:
        line.start_rest()
    exchange.finish()
    entered = incoming[...]
    state_end[...] = jnp.exp(decay_sum) * entered + pay[0:dim]
    for group in range(count):
        rows = slice(group * GROUP, (group + 1) * GROUP)
        start = starts[group] + jnp.exp(decays[group]) * entered
        starts[group] = start
        query_in = activated[rows, 0:keys].astype(jnp.float32) * root * jnp.exp(running[rows])
        total = mixed[rows] + exact(query_in, start, ((1,), (1,)))
        mixed[rows] = total
        gate = gate_in[rows]
        head = total * rms_scale(total) * head_scale[...]
        gated[rows] = (head * (gate * jax.nn.sigmoid(gate))).astype(jnp.bfloat16)
    value[...] = product(gated[...], project_out[...])
    stages.start()
    stages.across_chips()
    if gathering:
        for k in range(1, SHARES - 1):
            line.arrive(k)
            share.start_piece(k)
        share.copy(SHARES, share.mine, share.side_mine, share.near)
    stages.hand_back()
    stages.finish()
    if gathering:
        share.finish()
        line.finish()
        seed_all[0:tokens] = wide[...]
        collect(seed_all, tokens, h, landed, far_out, side_mine, side_far)
    edge_copy.wait_send()


def collect(target, first, h, mine, far, side_mine, side_far):
    beside = h + 1 - 2 * (h % 2)
    rows, held = mine.shape
    for quarter, source in (
        (h, mine),
        ((h + 2) % 4, far),
        (beside, side_mine),
        ((beside + 2) % 4, side_far),
    ):
        columns = pl.ds(pl.multiple_of(quarter * held, held), held)
        target[first : first + rows, columns] = source[...].astype(jnp.bfloat16)


def load_all(refs, count):
    operands, between = refs[:count], refs[count : -count - 1]
    held, sem = refs[-count - 1 : -1], refs[-1]
    loads = [pltpu.make_async_copy(operands[i], held[i], sem.at[i]) for i in range(count)]
    return loads, list(held), list(between)


def load_scratch(operands):
    return [pltpu.VMEM(x.shape, x.dtype) for x in operands] + [
        pltpu.SemaphoreType.DMA((len(operands),))
    ]


def front(block_in, gain, weight, taps, squeeze, expand, bias, gating, head_scale, project_out, wide):
    size, heads = lax.axis_size("seq"), lax.axis_size("head")
    tokens, width = block_in.shape
    mixed_dim, keys, dim, rank = weight.shape[1], expand.shape[1], gating.shape[1], expand.shape[0]
    gathering = wide is not None
    operands = [block_in, gain, weight, taps, squeeze, expand, bias, gating, head_scale, project_out]
    operands += [wide] if gathering else []
    f32, b16 = jnp.float32, jnp.bfloat16
    shapes = [((tokens, width), b16), ((16 + tokens, mixed_dim), f32), ((tokens, mixed_dim), f32)]
    shapes += [((tokens, mixed_dim), b16), ((tokens, rank), b16), ((tokens, keys), f32)]
    shapes += [((tokens, dim), f32), ((tokens, keys), f32), ((tokens, GROUP), f32)]
    shapes += [((tokens // GROUP, dim, keys), f32), ((dim, keys), f32), ((tokens, dim), f32)]
    shapes += [((tokens, width), f32), ((tokens, dim), b16)]
    levels, share = size // 2, width // heads
    if gathering:
        shapes += [((levels * tokens, width), b16)]
    edge = pltpu.VMEM((16, width), f32)
    value = jax.ShapeDtypeStruct((tokens, width), f32)
    scratch = [edge, edge, pltpu.SemaphoreType.DMA, pltpu.SemaphoreType.DMA]
    scratch += [pltpu.VMEM((dim + 8, keys), f32), pltpu.VMEM((dim, keys), f32)]
    scratch += [pltpu.VMEM(value.shape, f32)]
    scratch += exchange_scratch(size, dim, keys) + head_scratch(value)
    if gathering:
        scratch += [pltpu.VMEM(((levels - 1) * tokens, share), f32)] * 4
        scratch += gather_scratch(levels, tokens, share) + share_scratch()
    scratch += load_scratch(operands)
    return pl.pallas_call(
        functools.partial(front_kernel, size, gathering),
        out_shape=[jax.ShapeDtypeStruct(*x) for x in shapes],
        in_specs=[pl.BlockSpec(memory_space=pl.ANY)] * len(operands),
        out_specs=[pl.BlockSpec(memory_space=pltpu.VMEM)] * len(shapes),
        scratch_shapes=scratch,
        compiler_params=pltpu.CompilerParams(
            collective_id=2, has_side_effects=True, vmem_limit_bytes=60 * 1024 * 1024
        ),
    )(*operands)


def grouped(array, seqs, count):
    return array.reshape((seqs, count, GROUP) + array.shape[2:])


def running_sums(array):
    rows = [array[:, 0]]
    for index in range(1, array.shape[1]):
        rows.append(rows[-1] + array[:, index])
    return jnp.stack(rows, axis=1)


class Ring:
    def __init__(self, size, ins, slots, send_sem, recv_sem):
        self.size, self.ins, self.slots = size, ins, slots
        self.send_sem, self.recv_sem = send_sem, recv_sem
        self.half = size // 2
        me, h = lax.axis_index("seq"), lax.axis_index("head")
        low, high = me % 2, me // 2
        self.place = high + low * (2 * self.half - 1 - 2 * high)
        self.partners = ((self.member(self.place + 1), h), (self.member(self.place - 1), h))
        self.rows = ins[0].shape[0] // size
        self.part = self.rows // 2

    def member(self, position):
        position = (position + 2 * self.size) % self.size
        side = position // self.half
        return 2 * (position + side * (2 * self.half - 1 - 2 * position)) + side

    def block(self, array, direction, position):
        start = self.member(position) * self.rows + direction * self.part
        return self.ins[array].at[pl.ds(pl.multiple_of(start, self.part), self.part)]

    def copy(self, array, direction, step, source):
        return pltpu.make_async_remote_copy(
            src_ref=source,
            dst_ref=self.slots[array].at[direction, step],
            send_sem=self.send_sem.at[array, direction, step],
            recv_sem=self.recv_sem.at[array, direction, step],
            device_id=self.partners[direction],
            device_id_type=MESH,
        )

    def start(self, array):
        for direction, sign in ((0, 1), (1, -1)):
            self.copy(array, direction, 0, self.block(array, direction, self.place - sign)).start()

    def lap(self, array, step):
        for direction, sign in ((0, 1), (1, -1)):
            slot = self.slots[array].at[direction, step - 1]
            self.copy(array, direction, step - 1, slot).wait_recv()
            local = self.block(array, direction, self.place - sign * (step + 1))
            slot[...] = slot[...] + local[...]
            self.copy(array, direction, step, slot).start()

    def last(self, array, packed, columns):
        for direction in range(2):
            slot = self.slots[array].at[direction, self.size - 2]
            self.copy(array, direction, self.size - 2, slot).wait_recv()
            local = self.block(array, direction, self.place)
            rows = slice(direction * self.part, (direction + 1) * self.part)
            packed[rows, columns] = slot[...] + local[...]

    def finish(self):
        for array in range(len(self.ins)):
            for direction in range(2):
                for step in range(self.size - 1):
                    slot = self.slots[array].at[direction, step]
                    self.copy(array, direction, step, slot).wait_send()


OPERANDS = 29


def back_kernel(size, heads, *refs):
    loads, held, between = load_all(refs, OPERANDS)
    early, next_loads = [12, 15, 18], [16, 26, 27, 28]
    others = [i for i in range(OPERANDS) if i not in early + next_loads]
    for i in early + next_loads + others:
        loads[i].start()
    refs = held + between
    normed, padded, filtered, activated, squeezed, logits, gate_in, running, scores, *refs = refs
    starts, state_end, mixed, branch, gated, u_all, *refs = refs
    block_in, seed, first_gain, second_gain, weight, taps, squeeze, expand, gating, *refs = refs
    head_scale, project_out, gate, lift, drop, *refs = refs
    block_out, input_grad, packed, feed_sum, *refs = refs
    residual, normed_two, grad_resid, resid_low, value, feed, grad_two, grad_one, *refs = refs
    feed_out, gatein, mixed_low, act_grad, filtered_grad, edge_in, following, projected_low, *refs = refs
    logits_low, pay, after, n_all, gv_all, lv_all, inner_all, both, *refs = refs
    theirs, theirs_in, landed, far_out, side_mine, side_far, *refs = refs
    own, shared, own_in, shared_in, part_project, part_gating, part_output, *refs = refs
    slots, refs = refs[:3], refs[3:]
    ring_send, ring_recv, own_send, own_recv, shared_send, shared_recv, *refs = refs
    edge_send, edge_recv, pair_send, pair_recv, *refs = refs
    exchange = Exchange(size, True, pay, after, *refs[:7])
    stages = HeadSum(value, grad_two, *refs[7:13])
    feeding = HeadSum(feed, feed_out, *refs[13:19])
    ending = HeadSum(value, grad_one, *refs[19:25])
    line = LineGather(size // 2, landed, *refs[25:28])
    share = ColumnShare(landed, far_out, side_mine, side_far, *refs[28:30])
    ring = Ring(size, (part_project, part_gating, part_output), slots, ring_send, ring_recv)
    levels = size // 2
    s, h, z, y = place_of()
    near, far = stages.near, stages.far
    preceding, later = ((s + size - 1) % size, h), ((s + 1) % size, h)
    seq_bits, head_bits = size.bit_length() - 1, heads.bit_length() - 1
    small_peers = []
    for bit in range(seq_bits):
        step = 1 << bit
        small_peers.append((s + step - 2 * step * ((s // step) % 2), h))
    small_peers += [near, far]
    greet([preceding, later] + exchange.partners + list(ring.partners) + small_peers)

    tokens, width = block_in.shape
    hidden, keys, dim = drop.shape[0], expand.shape[1], gating.shape[1]
    rank, qkv, lags = expand.shape[0], taps.shape[1], taps.shape[0] - 1
    count = tokens // GROUP
    root = keys ** (-0.5)

    def rows_loop(step, carry, block=GROUP):
        def at(index, carry):
            return step(pl.ds(pl.multiple_of(index * block, block), block), carry)

        return lax.fori_loop(0, tokens // block, at, carry)

    def norm_two(rows, carry):
        values = block_in[rows].astype(jnp.float32) + branch[rows]
        residual[rows] = values
        normed_two[rows] = (values * rms_scale(values) * second_gain[...]).astype(jnp.bfloat16)
        return carry

    for i in early:
        loads[i].wait()
    rows_loop(norm_two, 0)
    line.start(normed_two, h)
    line.start_rest()

    def hidden_units(n, u_grad, rows):
        gate_value = against(n, gate[...])
        lift_value = against(n, lift[...])
        logistic = jax.nn.sigmoid(gate_value)
        silu = gate_value * logistic
        slope = logistic * (1.0 + gate_value * (1.0 - logistic))
        gv_all[rows] = (u_grad * lift_value * slope).astype(jnp.bfloat16)
        lv_all[rows] = (u_grad * silu).astype(jnp.bfloat16)
        inner_all[rows] = (silu * lift_value).astype(jnp.bfloat16)

    def feed_rows(rows, carry):
        hidden_units(normed_two[rows], against(seed[rows], drop[...]), rows)
        value[rows] = product(gv_all[rows], gate[...]) + product(lv_all[rows], lift[...])
        return carry

    for i in next_loads:
        loads[i].wait()
    rows_loop(feed_rows, 0, 128)
    stages.start()
    for i in others:
        loads[i].wait()
    stages.across_chips()
    feed[...] = product(inner_all[0:tokens], drop[...])
    n_all[0:tokens] = normed_two[...]
    stages.hand_back()
    stages.finish()

    def resid_rows(rows, total):
        incoming, values = grad_two[rows], residual[rows]
        scale = rms_scale(values)
        grad = seed[rows].astype(jnp.float32) + rms_back(values, scale, second_gain[...], incoming)
        grad_resid[rows] = grad
        resid_low[rows] = grad.astype(jnp.bfloat16)
        return total + jnp.sum(incoming * values * scale, axis=0, keepdims=True)

    grad_second = rows_loop(resid_rows, jnp.zeros((1, width), jnp.float32))

    def head_rows(rows, total):
        grad_gated = against(resid_low[rows], project_out[...])
        values, gates = mixed[rows], gate_in[rows]
        scale = rms_scale(values)
        logistic = jax.nn.sigmoid(gates)
        slope = logistic * (1.0 + gates * (1.0 - logistic))
        gatein[rows] = (grad_gated * (values * scale * head_scale[...]) * slope).astype(jnp.bfloat16)
        grad_norm = grad_gated * (gates * logistic)
        grad = rms_back(values, scale, head_scale[...], grad_norm)
        mixed_low[rows] = grad.astype(jnp.bfloat16).astype(jnp.float32)
        return total + jnp.sum(grad_norm * values * scale, axis=0, keepdims=True)

    grad_scale = rows_loop(head_rows, jnp.zeros((1, dim), jnp.float32))
    mask = causal_mask(GROUP)

    def group_rows(group):
        return slice(group * GROUP, (group + 1) * GROUP)

    def parts(group):
        rows = group_rows(group)
        run = running[rows]
        act = activated[rows].astype(jnp.float32)
        query, key, val = act[:, :keys] * root, act[:, keys : 2 * keys], act[:, 2 * keys :]
        return rows, run, run[GROUP - 1 : GROUP], query, key, val

    carry = jnp.zeros((dim, keys), jnp.float32)
    decay_sum = jnp.zeros((1, keys), jnp.float32)
    decays = [None] * count
    for group in range(count - 1, -1, -1):
        rows, run, last, query, key, val = parts(group)
        following[group] = carry
        decays[group] = decay_sum
        carry = jnp.exp(last) * carry + exact(mixed_low[rows], query * jnp.exp(run), ((0,), (0,)))
        decay_sum = decay_sum + last
    pay[0:dim] = carry
    pay[dim : dim + 8] = jnp.broadcast_to(jnp.exp(decay_sum), (8, keys))
    exchange.start()
    for k in range(levels - 1):
        line.arrive(k)
        share.start_piece(k)
    share.copy(SHARES, share.mine, share.side_mine, share.near)

    def local(group):
        rows, run, last, query, key, val = parts(group)
        outgrad = mixed_low[rows]
        query_in, key_in = query * jnp.exp(run), key * jnp.exp(-run)
        inside = exact(outgrad, val, ((1,), (1,))) * mask
        grad_query = exact(inside, key_in, ((1,), (0,))) + exact(outgrad, starts[group], ((1,), (0,)))
        act_grad[rows, 0:keys] = jnp.exp(run) * grad_query
        act_grad[rows, keys : 2 * keys] = jnp.exp(-run) * exact(inside, query_in, ((0,), (0,)))
        act_grad[rows, 2 * keys : qkv] = exact(scores[rows], outgrad, ((0,), (0,)))

    local(0)
    exchange.along()
    part_gating[...] = across(normed[...], gatein[...])
    part_output[...] = across(resid_low[...], gated[...])
    for group in range(1, count):
        local(group)
    exchange.join()
    ring.start(1)
    ring.start(2)
    exchange.finish()
    entered = after[...]
    tail_sum = jnp.sum(state_end[...] * entered, axis=0, keepdims=True)
    grad_bias = jnp.zeros((1, keys), jnp.float32)
    for group in range(count - 1, -1, -1):
        rows, run, last, query, key, val = parts(group)
        state = following[group] + jnp.exp(decays[group]) * entered
        to_end = jnp.exp(last - run)
        grad_key = act_grad[rows, keys : 2 * keys] + to_end * exact(val, state, ((1,), (0,)))
        grad_val = act_grad[rows, 2 * keys : qkv] + exact(key * to_end, state, ((1,), (1,)))
        grad_query = act_grad[rows, 0:keys]
        grad_run = query * grad_query - key * grad_key
        grad_log = exact(mask, grad_run, ((0,), (0,))) + tail_sum
        tail_sum = tail_sum + jnp.sum(grad_run, axis=0, keepdims=True)
        grad_logits = grad_log * jax.nn.sigmoid(-logits[rows]) / NORMALIZER
        grad_bias = grad_bias + jnp.sum(grad_logits, axis=0, keepdims=True)
        logits_low[rows] = grad_logits.astype(jnp.bfloat16)
        for first, grad in ((0, grad_query * root), (keys, grad_key), (2 * keys, grad_val)):
            columns = slice(first, first + grad.shape[1])
            filtered_grad[rows, columns] = grad * silu_grad(filtered[rows, columns])
    edge_copy = pltpu.make_async_remote_copy(
        src_ref=filtered_grad.at[pl.ds(0, 16)],
        dst_ref=edge_in,
        send_sem=edge_send,
        recv_sem=edge_recv,
        device_id=preceding,
        device_id_type=MESH,
    )
    edge_copy.start()
    ring.lap(1, 1)
    ring.lap(2, 1)
    for lag in range(lags + 1):
        total = jnp.zeros((1, qkv), jnp.float32)
        for group in range(count):
            base = group * GROUP
            before = padded[16 + base - lag : 16 + base - lag + GROUP]
            total = total + jnp.sum(filtered_grad[group_rows(group)] * before, axis=0, keepdims=True)
        own[0, lag : lag + 1] = total
    grad_expand = across(squeezed[...], logits_low[...])
    squeeze_low = against(logits_low[...], expand[...]).astype(jnp.bfloat16)
    shared[0, 0:rank] = across(squeeze_low, normed[...])
    edge_copy.wait_recv()
    filtered_grad[tokens : tokens + 16] = jnp.where(s < size - 1, edge_in[...], 0.0)
    for group in range(count):
        base = group * GROUP
        total = taps[0:1] * filtered_grad[base : base + GROUP]
        for lag in range(1, lags + 1):
            total = total + taps[lag : lag + 1] * filtered_grad[base + lag : base + lag + GROUP]
        projected_low[base : base + GROUP] = total.astype(jnp.bfloat16)
    value[...] = (
        against(projected_low[...], weight[...])
        + against(gatein[...], gating[...])
        + product(squeeze_low, squeeze[...])
    )
    ending.start()
    part_project[...] = across(normed[...], projected_low[...])
    ring.start(0)
    ring.lap(1, 2)
    ring.lap(2, 2)
    ending.across_chips()
    feeding.start()

    def first_rows(rows, total):
        values = block_in[rows].astype(jnp.float32)
        return total + jnp.sum(value[rows] * values * rms_scale(values), axis=0, keepdims=True)

    shared[0, rank : rank + 1] = rows_loop(first_rows, jnp.zeros((1, width), jnp.float32))
    shared[0, rank + 1 : rank + 2, 0:dim] = grad_scale
    for index in range(width // qkv):
        own[0, 8 + index : 9 + index] = grad_second[:, index * qkv : (index + 1) * qkv]
    for index in range(rank // 8):
        own[0, 16:24, index * keys : (index + 1) * keys] = grad_expand[index * 8 : (index + 1) * 8]
    own[0, 24:25, 0:keys] = grad_bias

    def small_copy(buffer, landing, send, recv, index):
        return pltpu.make_async_remote_copy(
            src_ref=buffer.at[index],
            dst_ref=landing.at[index],
            send_sem=send.at[index],
            recv_sem=recv.at[index],
            device_id=small_peers[index],
            device_id_type=MESH,
        )

    own_copies = [small_copy(own, own_in, own_send, own_recv, k) for k in range(seq_bits)]
    shared_copies = [
        small_copy(shared, shared_in, shared_send, shared_recv, k)
        for k in range(seq_bits + head_bits)
    ]

    def small_step(index):
        if index > 0 and index <= seq_bits:
            own_copies[index - 1].wait_recv()
            own[index] = own[index - 1] + own_in[index - 1]
        if index > 0:
            shared_copies[index - 1].wait_recv()
            shared[index] = shared[index - 1] + shared_in[index - 1]
        if index < seq_bits:
            own_copies[index].start()
        if index < seq_bits + head_bits:
            shared_copies[index].start()

    share.finish()
    collect(n_all, tokens, h, landed, far_out, side_mine, side_far)

    def gathered_rows(index, carry):
        rows = pl.ds(pl.multiple_of(tokens + index * 128, 128), 128)
        hidden_units(n_all[rows], against(u_all[rows], drop[...]), rows)
        return carry

    steps = (levels - 1) * tokens // 128
    cuts = [0, steps // 3, 2 * steps // 3, steps]
    small_step(0)
    lax.fori_loop(cuts[0], cuts[1], gathered_rows, 0)
    ring.lap(0, 1)
    ring.lap(1, 3)
    ring.lap(2, 3)
    lax.fori_loop(cuts[1], cuts[2], gathered_rows, 0)
    small_step(1)
    feeding.across_chips()
    ring.lap(0, 2)
    ring.lap(1, 4)
    ring.lap(2, 4)
    lax.fori_loop(cuts[2], cuts[3], gathered_rows, 0)
    per = theirs.shape[2]
    pair = pl.ds(pl.multiple_of(2 * z * per, 2 * per), 2 * per)
    pair_copies = []
    for index, (left, right) in enumerate(((n_all, gv_all), (n_all, lv_all), (u_all, inner_all))):
        both[...] = across(right[...], left[:, pair])
        theirs[index] = both[:, pl.ds(pl.multiple_of((1 - y) * per, per), per)]
        item = pltpu.make_async_remote_copy(
            src_ref=theirs.at[index],
            dst_ref=theirs_in.at[index],
            send_sem=pair_send.at[index],
            recv_sem=pair_recv.at[index],
            device_id=exchange.beside,
            device_id_type=MESH,
        )
        item.start()
        pair_copies.append(item)
        feed_sum[index] = both[:, pl.ds(pl.multiple_of(y * per, per), per)]
        if index == 0:
            small_step(2)
        ring.lap(0, 3 + index)
        if index < 2:
            ring.lap(1, 5 + index)
            ring.lap(2, 5 + index)
    ending.hand_back()
    small_step(3)
    ring.lap(0, 6)
    small_step(4)
    ending.finish()

    def input_rows(rows, carry):
        values = block_in[rows].astype(jnp.float32)
        back = rms_back(values, rms_scale(values), first_gain[...], grad_one[rows])
        input_grad[rows] = grad_resid[rows] + back
        return carry

    rows_loop(input_rows, 0)
    feeding.hand_back()
    small_step(5)
    ring.last(1, packed, slice(qkv, qkv + dim))
    ring.last(2, packed, slice(qkv + dim, qkv + 2 * dim))
    feeding.finish()

    def out_rows(rows, carry):
        block_out[rows] = (residual[rows] + feed_out[rows]).astype(jnp.bfloat16)
        return carry

    rows_loop(out_rows, 0)
    base = ring.rows
    packed[base : base + 32, 0:qkv] = own[seq_bits]
    base += 32
    packed[base : base + shared.shape[1], 0:width] = shared[seq_bits + head_bits]
    ring.last(0, packed, slice(0, qkv))
    for index in range(3):
        pair_copies[index].wait_recv()
        feed_sum[index] = feed_sum[index] + theirs_in[index]
    for item in pair_copies + own_copies + shared_copies + [edge_copy]:
        item.wait_send()
    line.finish()
    ring.finish()


def back(forward, params):
    size, heads = lax.axis_size("seq"), lax.axis_size("head")
    levels = size // 2
    f32, b16 = jnp.float32, jnp.bfloat16
    block_in, weight, taps, squeeze, expand, gating, drop = (params[k] for k in (0, 4, 5, 6, 7, 8, 13))
    tokens, width = block_in.shape
    qkv, keys, dim, rank, hidden = weight.shape[1], expand.shape[1], gating.shape[1], expand.shape[0], drop.shape[0]
    rows, inside, share = width // size, levels * tokens, width // heads
    seq_bits, all_bits = size.bit_length() - 1, size.bit_length() + heads.bit_length() - 2
    own_shape, shared_shape = (32, qkv), (rank + 8, width)
    outs = [((tokens, width), b16), ((tokens, width), f32)]
    outs += [((rows + 32 + shared_shape[0], qkv + 2 * dim), f32), ((3, hidden, rows), f32)]
    held = [((tokens, width), f32), ((tokens, width), b16), ((tokens, width), f32), ((tokens, width), b16)]
    held += [((tokens, width), f32)] * 5
    held += [((tokens, dim), b16), ((tokens, dim), f32), ((tokens, qkv), f32)]
    held += [((tokens + 16, qkv), f32), ((16, qkv), f32), ((tokens // GROUP, dim, keys), f32)]
    held += [((tokens, qkv), b16), ((tokens, keys), b16), ((dim + 8, keys), f32), ((dim, keys), f32)]
    held += [((inside, width), b16)] + [((inside, hidden), b16)] * 3
    held += [((hidden, 2 * rows), f32)]
    held += [((3, hidden, rows), f32)] * 2 + [((inside - tokens, share), f32)] * 4
    held += [((seq_bits + 1,) + own_shape, f32), ((all_bits + 1,) + shared_shape, f32)]
    held += [((seq_bits,) + own_shape, f32), ((all_bits,) + shared_shape, f32)]
    held += [((width, qkv), f32), ((width, dim), f32), ((width, dim), f32)]
    held += [((2, size - 1, rows // 2, x), f32) for x in (qkv, dim, dim)]
    value = jax.ShapeDtypeStruct((tokens, width), f32)
    dma = pltpu.SemaphoreType.DMA
    scratch = [pltpu.VMEM(*x) for x in held]
    scratch += [dma((3, 2, size - 1))] * 2 + [dma((seq_bits,))] * 2 + [dma((all_bits,))] * 2
    scratch += [dma, dma] + [dma((3,))] * 2
    scratch += exchange_scratch(size, dim, keys) + head_scratch(value) * 3
    scratch += gather_scratch(levels, tokens, share) + share_scratch()
    operands = list(forward) + list(params)
    scratch += load_scratch(operands)
    return pl.pallas_call(
        functools.partial(back_kernel, size, heads),
        out_shape=[jax.ShapeDtypeStruct(*x) for x in outs],
        in_specs=[pl.BlockSpec(memory_space=pl.ANY)] * len(operands),
        out_specs=[pl.BlockSpec(memory_space=pltpu.VMEM)] * len(outs),
        scratch_shapes=scratch,
        compiler_params=pltpu.CompilerParams(
            collective_id=5, has_side_effects=True, vmem_limit_bytes=60 * 1024 * 1024
        ),
    )(*operands)


def unpack(packed, taps, rank, keys, dim, width, rows, results):
    lags, qkv = taps.shape[0], taps.shape[1]
    first, second, scale, bias, taps_out, expand, squeeze, *outs = results
    base = rows
    taps_out[:, 0] = packed[base : base + lags, 0:qkv]
    for index in range(width // qkv):
        second[:, index * qkv : (index + 1) * qkv] = packed[base + 8 + index : base + 9 + index, 0:qkv]
    for index in range(rank // 8):
        expand[index * 8 : (index + 1) * 8] = packed[base + 16 : base + 24, index * keys : (index + 1) * keys]
    bias[...] = packed[base + 24 : base + 25, 0:keys]
    base += 32
    squeeze[...] = packed[base : base + rank, 0:width]
    first[...] = packed[base + rank : base + rank + 1, 0:width]
    scale[...] = packed[base + rank + 1 : base + rank + 2, 0:dim]


def spread_kernel(taps_shape, dim, *refs):
    block_out, input_grad, packed, feed, block_result, grad_result, *results = refs
    block_result[...] = block_out[...]
    grad_result[...] = input_grad[...]
    taps = jax.ShapeDtypeStruct(taps_shape, jnp.float32)
    qkv = taps.shape[1]
    rank, keys = results[5].shape
    rows, width = results[7].shape[0], results[0].shape[1]
    unpack(packed, taps, rank, keys, dim, width, rows, results)
    results[7][:, 0] = packed[0:rows, 0:qkv]
    results[8][...] = packed[0:rows, qkv : qkv + dim]
    results[9][...] = jnp.transpose(packed[0:rows, qkv + dim : qkv + 2 * dim])
    for index in range(3):
        results[10 + index][...] = feed[index]


def spread(block_out, input_grad, packed, feed, taps, expand, dim, width):
    rank, keys = expand.shape
    rows, lags, qkv = width // lax.axis_size("seq"), taps.shape[0], taps.shape[1]
    shapes = [(1, width), (1, width), (1, dim), (1, keys), (lags, 1, qkv), expand.shape, (rank, width)]
    shapes += [(rows, 1, qkv), (rows, dim), (dim, rows)] + [feed.shape[1:]] * 3
    return pl.pallas_call(
        functools.partial(spread_kernel, taps.shape, dim),
        out_shape=[jax.ShapeDtypeStruct(x.shape, x.dtype) for x in (block_out, input_grad)]
        + [jax.ShapeDtypeStruct(x, jnp.float32) for x in shapes],
        in_specs=[pl.BlockSpec(memory_space=pltpu.VMEM)] * 4,
        compiler_params=pltpu.CompilerParams(vmem_limit_bytes=60 * 1024 * 1024),
    )(block_out, input_grad, packed, feed)


def local_states(decays, updates, backward):
    count = updates.shape[1]
    carry = jnp.zeros_like(updates[:, 0])
    states = [None] * count
    for index in range(count):
        group = count - 1 - index if backward else index
        states[group] = carry
        carry = jnp.exp(decays[:, group])[:, None] * carry + updates[:, group]
    return (jnp.stack(states, axis=1), carry)


def body(
    block_in,
    upstream,
    first_gain,
    project_in,
    filter_taps,
    squeeze,
    expand,
    decay_bias,
    gating,
    head_scale,
    project_out,
    second_gain,
    hidden_gate,
    hidden_lift,
    hidden_drop,
):
    seqs, tokens, width = block_in.shape
    total_rows = seqs * tokens
    key_dim = expand.shape[1]
    value_dim = gating.shape[1]
    mixed_dim = project_in.shape[2]
    lags = filter_taps.shape[0] - 1
    count = tokens // GROUP
    taps = filter_taps.reshape(lags + 1, mixed_dim)
    weight_in = project_in.reshape(width, mixed_dim)
    size, hidden = lax.axis_size("seq"), hidden_gate.shape[1]
    gathering = size // 2 == SHARES + 1 and total_rows * width <= 512 * 1024
    seed = upstream.reshape(total_rows, width)
    residual_in = block_in.reshape(total_rows, width).astype(jnp.float32)
    scale_one = rms_scale(residual_in)
    (
        normed_one,
        padded,
        filtered,
        activated,
        squeezed,
        logits,
        gate_in,
        running,
        scores,
        starts,
        state_end,
        mixed,
        branch,
        gated,
        *seed_cols,
    ) = front(
        block_in.reshape(total_rows, width),
        first_gain[None],
        weight_in,
        taps,
        jnp.transpose(squeeze),
        expand,
        decay_bias[None],
        gating,
        head_scale[None],
        project_out,
        seed if gathering else None,
    )
    if gathering:
        block_out, input_grad, packed, feed_sum = back(
            (
                normed_one,
                padded,
                filtered,
                activated,
                squeezed,
                logits,
                gate_in,
                running,
                scores,
                starts,
                state_end,
                mixed,
                branch,
                gated,
                *seed_cols,
            ),
            (
                block_in.reshape(total_rows, width),
                seed,
                first_gain[None],
                second_gain[None],
                weight_in,
                taps,
                jnp.transpose(squeeze),
                expand,
                gating,
                head_scale[None],
                project_out,
                jnp.transpose(hidden_gate),
                jnp.transpose(hidden_lift),
                hidden_drop,
            ),
        )
        block_out, input_grad, *done = spread(
            block_out, input_grad, packed, feed_sum, taps, expand, value_dim, width
        )
        return (
            block_out[None],
            input_grad[None],
            done[0][0],
            done[7],
            done[4],
            jnp.transpose(done[6]),
            done[5],
            done[3][0],
            done[8],
            done[2][0],
            done[9],
            done[1][0],
            jnp.transpose(done[10]),
            jnp.transpose(done[11]),
            done[12],
        )
    padded = padded[16 - lags :][None]
    projected = padded[:, lags:]
    filtered, state_end = filtered[None], state_end[None]
    activated = activated.astype(jnp.float32)[None]
    root = key_dim ** (-0.5)
    query = grouped(activated[..., :key_dim] * root, seqs, count)
    keys = grouped(activated[..., key_dim : 2 * key_dim], seqs, count)
    values = grouped(activated[..., 2 * key_dim :], seqs, count)
    mask = causal_mask(GROUP)
    running, starts = grouped(running[None], seqs, count), starts[None]
    last = running[:, :, -1]
    query_in = query * jnp.exp(running)
    key_in = keys * jnp.exp(-running)
    key_end = keys * jnp.exp(last[:, :, None] - running)
    scores = grouped(scores[None], seqs, count)
    decay_sum = jnp.sum(last, axis=1)
    decay_total = jnp.exp(decay_sum)
    scale_head = rms_scale(mixed)
    normed_head = mixed * scale_head * head_scale
    residual = residual_in + branch
    scale_two = rms_scale(residual)
    normed_two = (residual * scale_two * second_gain).astype(jnp.bfloat16)
    gate_value = product(normed_two, hidden_gate)
    lift_value = product(normed_two, hidden_lift)
    inner = (jax.nn.silu(gate_value) * lift_value).astype(jnp.bfloat16)
    partial_feed = product(inner, hidden_drop)
    grad_inner = against(seed, hidden_drop)
    grad_gv = (grad_inner * lift_value * silu_grad(gate_value)).astype(jnp.bfloat16)
    grad_lv = (grad_inner * jax.nn.silu(gate_value)).astype(jnp.bfloat16)
    grad_two = head_sum(against(grad_gv, hidden_gate) + against(grad_lv, hidden_lift))
    grad_second = jnp.sum(grad_two * residual * scale_two, axis=0)
    grad_resid = seed.astype(jnp.float32) + rms_back(residual, scale_two, second_gain, grad_two)
    resid_low = grad_resid.astype(jnp.bfloat16)
    grad_output = across(resid_low, gated)
    grad_gated = against(resid_low, project_out)
    grad_gatein = (grad_gated * normed_head * silu_grad(gate_in)).astype(jnp.bfloat16)
    grad_normhead = grad_gated * jax.nn.silu(gate_in)
    grad_scale = jnp.sum(grad_normhead * mixed * scale_head, axis=0)
    grad_mixed_low = rms_back(mixed, scale_head, head_scale, grad_normhead).astype(jnp.bfloat16)
    grad_mixed = lax.optimization_barrier(grad_mixed_low).astype(jnp.float32)
    outgrad = grouped(grad_mixed.reshape(seqs, tokens, value_dim), seqs, count)
    query_end = jnp.einsum("snic,snid->sndc", query_in, outgrad, precision=HIGH)
    following_zero, back_total = local_states(last, query_end, True)
    after = entering(decay_total[0], back_total[0])[None]
    after_group = decay_sum[:, None] - running_sums(last)
    following = following_zero + jnp.exp(after_group)[:, :, None] * after[:, None]
    inner_group = jnp.einsum("snid,snjd->snij", outgrad, values, precision=HIGH) * mask
    grad_query = jnp.exp(running) * (
        jnp.einsum("snij,snjc->snic", inner_group, key_in, precision=HIGH)
        + jnp.einsum("snid,sndc->snic", outgrad, starts, precision=HIGH)
    )
    grad_keys = jnp.exp(-running) * jnp.einsum(
        "snij,snic->snjc", inner_group, query_in, precision=HIGH
    )
    grad_keys = grad_keys + jnp.exp(last[:, :, None] - running) * jnp.einsum(
        "snjd,sndc->snjc", values, following, precision=HIGH
    )
    grad_values = jnp.einsum("snij,snid->snjd", scores, outgrad, precision=HIGH)
    grad_values = grad_values + jnp.einsum("snjc,sndc->snjd", key_end, following, precision=HIGH)
    grad_running = (query * grad_query - keys * grad_keys).reshape(seqs, tokens, key_dim)
    beyond = jnp.sum(state_end * after, axis=1)
    upper = jnp.transpose(causal_mask(tokens))
    suffix = jnp.einsum("ij,sjc->sic", upper, grad_running, precision=HIGH)
    grad_log = suffix + beyond[:, None]
    grad_act = jnp.concatenate(
        [
            grad_query.reshape(seqs, tokens, key_dim) * root,
            grad_keys.reshape(seqs, tokens, key_dim),
            grad_values.reshape(seqs, tokens, value_dim),
        ],
        axis=-1,
    )
    grad_filtered = grad_act * silu_grad(filtered)
    later = shifted(grad_filtered[:, :lags], "seq", -1)
    padded_back = jnp.concatenate([grad_filtered, later], axis=1)
    grad_projected = taps[0] * grad_filtered
    tap_rows = [jnp.sum(grad_filtered * projected, axis=(0, 1))]
    for lag in range(1, lags + 1):
        grad_projected = grad_projected + taps[lag] * padded_back[:, lag : lag + tokens]
        tap_rows.append(
            jnp.sum(grad_filtered * padded[:, lags - lag : lags - lag + tokens], axis=(0, 1))
        )
    grad_taps = jnp.stack(tap_rows).reshape(lags + 1, 1, mixed_dim)
    grad_projected = grad_projected.reshape(total_rows, mixed_dim).astype(jnp.bfloat16)
    grad_logits = grad_log.reshape(total_rows, key_dim) * jax.nn.sigmoid(-logits) / NORMALIZER
    grad_bias = jnp.sum(grad_logits, axis=0)
    logits_low = grad_logits.astype(jnp.bfloat16)
    grad_expand = across(squeezed, logits_low)
    squeeze_low = against(logits_low, expand).astype(jnp.bfloat16)
    grad_squeeze = across(squeeze_low, normed_one)
    partials = [across(normed_one, grad_projected), across(normed_one, grad_gatein), grad_output]
    partials += [across(normed_two, grad_gv), across(normed_two, grad_lv), across(seed, inner)]
    partial_value = (
        against(grad_projected, weight_in)
        + against(grad_gatein, gating)
        + against(squeeze_low, squeeze)
    )
    partial_first = jnp.sum(partial_value * residual_in * scale_one, axis=0)
    grad_one, feed, packed = tail(
        partial_value,
        partial_feed,
        (grad_taps[:, 0], grad_expand, grad_bias[None], grad_second[None]),
        (grad_squeeze, partial_first[None], grad_scale[None]),
        partials,
    )
    done = finishing(
        block_in[0],
        first_gain[None],
        grad_one,
        grad_resid,
        residual,
        feed,
        packed,
        (),
        lags + 1,
        expand,
        head_scale,
        tuple(x.shape[1] for x in partials),
    )
    block_out, input_grad, sum_first, sum_second, sum_scale, sum_bias = done[:6]
    sum_taps, sum_expand, sum_squeeze = done[6:9]
    own_project, own_gating, own_output, own_gate, own_lift, own_drop = done[9:]
    own_drop = jnp.transpose(own_drop)
    return (
        block_out[None],
        input_grad[None],
        sum_first[0],
        own_project,
        sum_taps,
        jnp.transpose(sum_squeeze),
        sum_expand,
        sum_bias[0],
        own_gating,
        sum_scale[0],
        own_output,
        sum_second[0],
        own_gate,
        own_lift,
        own_drop,
    )


def solution(mesh):
    in_specs = (
        P(None, "seq", None),
        P(None, "seq", None),
        P(),
        P(None, "head", None),
        P(None, "head", None),
        P(),
        P(None, "head"),
        P("head"),
        P(None, "head"),
        P(),
        P("head", None),
        P(),
        P(None, "head"),
        P(None, "head"),
        P("head", None),
    )
    out_specs = (
        P(None, "seq", None),
        P(None, "seq", None),
        P(),
        P("seq", "head", None),
        P(None, "head", None),
        P(),
        P(None, "head"),
        P("head"),
        P("seq", "head"),
        P(),
        P("head", "seq"),
        P(),
        P("seq", "head"),
        P("seq", "head"),
        P("head", "seq"),
    )
    return jax.shard_map(body, mesh=mesh, in_specs=in_specs, out_specs=out_specs, check_vma=False)
```
